32 devices in a mesh: parts: 2 (over y), seq: 16 (over z, x, core).
Axes of the slice: x: 2, y: 2, z: 4, core: 2. Of those that a mesh axis runs over, the one named last changes fastest.
Arguments:
- queries: bfloat16 [32, 8192], P(('parts', 'seq')), parts along dimension 0, may hold values from -140 to 140
- new_keys: bfloat16 [32, 1024], P(('parts', 'seq')), parts along dimension 0, may hold values from -7 to 7
- new_values: bfloat16 [32, 1024], P(('parts', 'seq')), parts along dimension 0, may hold values from -6 to 6
- doc_keys: bfloat16 [32768, 1024], P(('parts', 'seq')), parts along dimension 0, may hold values from -6 to 6
- doc_values: bfloat16 [32768, 1024], P(('parts', 'seq')), parts along dimension 0, may hold values from -6 to 6
- suffix_keys: bfloat16 [32768, 1024], P(('parts', 'seq')), parts along dimension 0, may hold values from -6 to 6
- suffix_values: bfloat16 [32768, 1024], P(('parts', 'seq')), parts along dimension 0, may hold values from -6 to 6
- keep_lists: int32 [32, 32], P(('parts', 'seq')), parts along dimension 0, may hold values from 0 to 127, as said below
- suffix_lengths: int32 [16], P('parts'), parts along dimension 0, may hold values from 1 to 2048
Outputs:
- attended: bfloat16 [32, 8192], P(('parts', 'seq')), parts along dimension 0
The draws below stay inside these ranges and needn't reach their ends.
There are 2 independent parts, one for each index of `parts`. The reference program is written for one: setup_inputs(seed, part) draws one part's arguments, and reference() takes and returns one part's arrays. A program takes and returns all parts, laid end to end along the dimension named above; each array names one. Nothing has to cross between parts.
Inputs may be any that keep to these rules, and one draw needn't show every extreme that they name: Row r's list (rows 2r and 2r+1 of keep_lists) names 64 different blocks of 0 to 127.
All inputs are finite; a program needn't handle non-finite values.
Results may differ from the reference program's by a relative error of at most 0.007.
Values may be sent and summed in bfloat16 or wider, within the bound.
No kernel may reach another device: no remote copies, remote signals or barrier semaphores. Data moves between devices by JAX's collectives and lax.ppermute only.
A program may use at most 128 MiB of HBM per device.

```python
import jax
import jax.numpy as jnp
from jax import lax

HEADS = 64
KVH = 8
HD = 128
BLOCK = 128
DOC_DEV = 1024
SUF_DEV = 1024
ROWS = 8
QTOK = 16
SUFFIX = 2048
L_DOC = 16384
CORPUS_TILES = 128
KEEP = 64
N_SEQ = 16


def common_new(key):
    fresh = jnp.clip(jax.random.normal(jax.random.fold_in(key, 11), (QTOK, KVH * HD), jnp.float32), -6.0, 6.0)
    return fresh


def draw_new_keys(key, part):
    return common_new(key).astype(jnp.bfloat16)


def draw_queries(key, part):
    fresh = common_new(key)
    drawn_sample = 3.0 * jnp.clip(jax.random.normal(jax.random.fold_in(key, 13), (QTOK, HEADS * HD), jnp.float32), -4.0, 4.0)
    own_part = jnp.repeat(fresh.reshape(QTOK, KVH, 1, HD), HEADS // KVH, axis=2).reshape(QTOK, HEADS * HD)
    result = drawn_sample + 1.3 * own_part
    return result.astype(jnp.bfloat16)


def draw_doc_values(key, part):
    fluctuation = jnp.clip(jax.random.normal(jax.random.fold_in(key, 31), (L_DOC, KVH * HD), jnp.float32), -4.0, 4.0)
    column_offset = jnp.clip(jax.random.normal(jax.random.fold_in(key, 32), (KVH * HD,), jnp.float32), -2.0, 2.0)
    return (fluctuation + column_offset[None, :]).astype(jnp.bfloat16)


def draw_keep_lists(key, part):
    shard_mass = jax.random.randint(jax.random.fold_in(key, 21), (N_SEQ,), 0, 3) * 32768
    holding_shard = jnp.arange(CORPUS_TILES, dtype=jnp.int32) // (CORPUS_TILES // N_SEQ)
    extra_credit = shard_mass[holding_shard]
    stochastic_jitter = jax.random.randint(jax.random.fold_in(key, 22), (ROWS, CORPUS_TILES), 0, 65536)
    sorted_position = (stochastic_jitter + extra_credit[None, :]) * CORPUS_TILES + jnp.arange(CORPUS_TILES, dtype=jnp.int32)[None, :]
    _, selected_entries = lax.top_k(sorted_position, KEEP)
    return selected_entries.astype(jnp.int32).reshape(QTOK, KEEP // 2)


def set_ends(drawn, own_key, smallest, high):
    index_at = [jax.random.randint(jax.random.fold_in(own_key, axis), (), 0, length) for axis, length in enumerate(drawn.shape)]
    longest = drawn.shape.index(max(drawn.shape))
    beside = index_at[:longest] + [(index_at[longest] + 1) % drawn.shape[longest]] + index_at[longest + 1:]
    return drawn.at[tuple(index_at)].set(smallest).at[tuple(beside)].set(high)


def level_of(own_key, shape, shards, low, largest):
    level = 1.0
    for dim, shards_of in shards:
        steps = jax.random.uniform(jax.random.fold_in(jax.random.fold_in(own_key, 6), dim), (shards_of,), jnp.float32, low / len(shards), largest / len(shards))
        level = level * jnp.repeat(jnp.exp(steps), shape[dim] // shards_of).reshape((-1,) + (1,) * (len(shape) - 1 - dim))
    return level


def normal_values(stream_key, shape, spread, reach, cuts=(), held_as=jnp.bfloat16):
    loudness = level_of(stream_key, shape, cuts, -0.22, 0.18) if cuts else 1.0
    values = jax.random.normal(stream_key, shape, jnp.float32) * spread * loudness
    return jnp.minimum(jnp.maximum(values, -reach), reach).astype(held_as)


def setup_inputs(seed: int = 0, part: int = 0) -> dict:
    key_of = jax.random.split(jax.random.key(seed), 10)
    part_splits = jax.random.split(jax.random.fold_in(key_of[9], part), 10)
    queries = draw_queries(jax.random.fold_in(jax.random.fold_in(key_of[9], part), 71), part)
    new_keys = draw_new_keys(jax.random.fold_in(jax.random.fold_in(key_of[9], part), 71), part)
    new_values = normal_values(part_splits[2], (QTOK, KVH * HD), 1.0, 6.0, ((0, 16),))
    doc_keys = normal_values(part_splits[3], (L_DOC, KVH * HD), 1.0, 6.0, ((0, 16),))
    doc_values = draw_doc_values(jax.random.fold_in(jax.random.fold_in(key_of[9], part), 71), part)
    suffix_keys = normal_values(part_splits[5], (ROWS * SUFFIX, KVH * HD), 1.0, 6.0, ((0, 16),))
    suffix_values = normal_values(part_splits[6], (ROWS * SUFFIX, KVH * HD), 1.0, 6.0, ((0, 16),))
    keep_lists = draw_keep_lists(jax.random.fold_in(jax.random.fold_in(key_of[9], part), 71), part)
    suffix_lengths = set_ends(jax.random.randint(part_splits[8], (ROWS,), 1, SUFFIX + 1), jax.random.fold_in(part_splits[8], 1), 1, SUFFIX).astype(jnp.int32)
    return {"queries": queries, "new_keys": new_keys, "new_values": new_values, "doc_keys": doc_keys, "doc_values": doc_values, "suffix_keys": suffix_keys, "suffix_values": suffix_values, "keep_lists": keep_lists, "suffix_lengths": suffix_lengths}


NEG_BIG = -1e30


def merge_terms(first, second):
    ceiling = jnp.maximum(first[0], second[0])
    left_scale = jnp.exp(first[0] - ceiling)
    right_scale = jnp.exp(second[0] - ceiling)
    return (ceiling, left_scale * first[1] + right_scale * second[1],
            left_scale[..., None] * first[2] + right_scale[..., None] * second[2])


def block_parts(scores, live_keys, value_rows):
    masked = jnp.where(live_keys, scores, NEG_BIG)
    block_max = jnp.max(masked, axis=-1)
    weights = jnp.where(live_keys, jnp.exp(scores - block_max[..., None]), 0.0)
    block_sum = jnp.sum(weights, axis=-1)
    rounded = lax.optimization_barrier(weights.astype(jnp.bfloat16)).astype(jnp.float32)
    block_out = jnp.einsum("tkgbj,bjkd->tkgbd", rounded, value_rows)
    return block_max, block_sum, block_out


def collapse(parts):
    block_max, block_sum, block_out = parts
    global_maximum = jnp.max(block_max, axis=-1)
    factor = jnp.exp(block_max - global_maximum[..., None])
    return (global_maximum, jnp.sum(factor * block_sum, axis=-1), jnp.sum(factor[..., None] * block_out, axis=-2))


def reference(queries, new_keys, new_values, doc_keys, doc_values, suffix_keys, suffix_values, keep_lists, suffix_lengths):
    groups = HEADS // KVH
    factor_scale = HD ** -0.5
    keep_rows = keep_lists.reshape(ROWS, KEEP)
    group_len = 8 if KEEP % 8 == 0 else 1
    doc_kblocks = doc_keys.reshape(CORPUS_TILES, BLOCK, KVH, HD)
    doc_vblocks = doc_values.reshape(CORPUS_TILES, BLOCK, KVH, HD)
    half_blocks = SUF_DEV // BLOCK
    span_blocks = DOC_DEV // BLOCK

    def one_row(row_id):
        q_rows = lax.dynamic_slice_in_dim(queries, (2 * row_id).astype(jnp.int32), 2, 0)
        q_rows = q_rows.astype(jnp.float32).reshape(2, KVH, groups, HD)

        def visit_group(block_ids):
            keys_now = doc_kblocks[block_ids].astype(jnp.float32)
            values_now = doc_vblocks[block_ids].astype(jnp.float32)
            scores = jnp.einsum("tkgd,bjkd->tkgbj", q_rows, keys_now) * factor_scale
            return block_parts(scores, True, values_now)

        ids = keep_rows[row_id]
        b_max, b_sum, b_out = lax.map(visit_group, ids.reshape(KEEP // group_len, group_len))
        b_max = jnp.moveaxis(b_max, 0, 3).reshape(2, KVH, groups, KEEP)
        b_sum = jnp.moveaxis(b_sum, 0, 3).reshape(2, KVH, groups, KEEP)
        b_out = jnp.moveaxis(b_out, 0, 3).reshape(2, KVH, groups, KEEP, HD)
        span_of = ids // span_blocks
        member = span_of[:, None] == jnp.arange(N_SEQ, dtype=jnp.int32)[None, :]
        span_max = jnp.max(jnp.where(member, b_max[..., None], NEG_BIG), axis=-2)
        back_max = jnp.max(jnp.where(member, span_max[..., None, :], NEG_BIG), axis=-1)
        factor = jnp.exp(b_max - back_max)
        onehot = member.astype(jnp.float32)
        span_sum = jnp.einsum("tkgb,bs->tkgs", factor * b_sum, onehot, precision=lax.Precision.HIGHEST)
        span_out = jnp.einsum("tkgbd,bs->tkgsd", factor[..., None] * b_out, onehot, precision=lax.Precision.HIGHEST)

        offset = (row_id * SUFFIX).astype(jnp.int32)
        keys_new = lax.dynamic_slice_in_dim(new_keys, (2 * row_id).astype(jnp.int32), 2, 0)
        keys_new = keys_new.astype(jnp.float32).reshape(2, KVH, HD)
        values_new = lax.dynamic_slice_in_dim(new_values, (2 * row_id).astype(jnp.int32), 2, 0)
        values_new = values_new.astype(jnp.float32).reshape(2, KVH, HD)
        own_scores = jnp.einsum("tkgd,ukd->tkgu", q_rows, keys_new) * factor_scale
        visible = (jnp.arange(2)[None, :] <= jnp.arange(2)[:, None])[:, None, None, :]
        for half in range(2):
            start = offset + half * SUF_DEV
            keys_suf = lax.dynamic_slice_in_dim(suffix_keys, start, SUF_DEV, 0).astype(jnp.float32)
            keys_suf = keys_suf.reshape(half_blocks, BLOCK, KVH, HD)
            values_suf = lax.dynamic_slice_in_dim(suffix_values, start, SUF_DEV, 0).astype(jnp.float32)
            values_suf = values_suf.reshape(half_blocks, BLOCK, KVH, HD)
            scores = jnp.einsum("tkgd,bjkd->tkgbj", q_rows, keys_suf) * factor_scale
            position = half * SUF_DEV + jnp.arange(SUF_DEV, dtype=jnp.int32).reshape(half_blocks, BLOCK)
            live_keys = position < suffix_lengths[row_id]
            suffix_part = collapse(block_parts(scores, live_keys, values_suf))
            seen = visible[..., half]
            own_part = (jnp.where(seen, own_scores[..., half], NEG_BIG),
                        jnp.where(seen, 1.0, 0.0) * jnp.ones_like(own_scores[..., half]),
                        jnp.where(seen[..., None], values_new[None, half][:, :, None, :], 0.0) * jnp.ones_like(q_rows))
            span_id = (2 * row_id + half).astype(jnp.int32)
            doc_part = (lax.dynamic_index_in_dim(span_max, span_id, 3, False),
                        lax.dynamic_index_in_dim(span_sum, span_id, 3, False),
                        lax.dynamic_index_in_dim(span_out, span_id, 3, False))
            joined = merge_terms(merge_terms(doc_part, suffix_part), own_part)
            span_max = lax.dynamic_update_index_in_dim(span_max, joined[0], span_id, 3)
            span_sum = lax.dynamic_update_index_in_dim(span_sum, joined[1], span_id, 3)
            span_out = lax.dynamic_update_index_in_dim(span_out, joined[2], span_id, 3)
        units = span_out / jnp.maximum(span_sum, 1.0)[..., None]
        units = lax.optimization_barrier(units.astype(jnp.bfloat16)).astype(jnp.float32)
        ceiling = jnp.max(span_max, axis=-1)
        weight = jnp.exp(span_max - ceiling[..., None]) * span_sum
        total_out = jnp.sum(weight[..., None] * units, axis=-2)
        total_sum = jnp.sum(weight, axis=-1)
        return (total_out / total_sum[..., None]).reshape(2, HEADS * HD)

    result = lax.map(one_row, jnp.arange(ROWS, dtype=jnp.int32))
    return result.reshape(QTOK, HEADS * HD).astype(jnp.bfloat16)
```

```python
import functools
import math

import jax
import jax.numpy as jnp
from jax import lax
from jax.experimental import pallas as pl
from jax.experimental.pallas import tpu as pltpu
from jax.sharding import PartitionSpec as P

HEADS = 64
KVH = 8
HD = 128
BLOCK = 128
GROUPS = HEADS // KVH
LANES = 128
SLOTS = 8

NEG_BIG = -1e30
NEG_SAFE = -5e29
EXP2_SCALE = HD**-0.5 * math.log2(math.e)

VMEM = pltpu.VMEM
SMEM = pltpu.SMEM


def pack_kernel(flag_rows, list_ref, q_ref, out_ref):
    q = q_ref[...].astype(jnp.float32)
    rows = [q[:, h * HD : (h + 1) * HD] for h in range(HEADS)]
    out_ref[0:HEADS, :] = jnp.concatenate(rows, axis=0).astype(jnp.bfloat16)
    ids = (
        lax.broadcasted_iota(jnp.int32, (flag_rows, LANES), 0) * LANES
        + lax.broadcasted_iota(jnp.int32, (flag_rows, LANES), 1)
    )

    def mark(k, found):
        return jnp.where(ids == list_ref[0, k], 1.0, found)

    found = lax.fori_loop(
        0, list_ref.shape[1], mark, jnp.zeros((flag_rows, LANES), jnp.float32), unroll=8
    )
    out_ref[HEADS : HEADS + flag_rows, :] = found.astype(jnp.bfloat16)


def lane_dot(a, b):
    return lax.dot_general(a, b, (((1,), (1,)), ((), ())), preferred_element_type=jnp.float32)


def partial_softmax(scores):
    top = jnp.max(scores, axis=-1, keepdims=True)
    weights = jnp.exp2((scores - jnp.maximum(top, NEG_SAFE)) * EXP2_SCALE)
    return top, jnp.sum(weights, axis=-1, keepdims=True), weights.astype(jnp.bfloat16)


def attend_kernel(
    flag_rows,
    me_ref,
    len_ref,
    near_ref,
    far_ref,
    dk_ref,
    dv_ref,
    sk_ref,
    sv_ref,
    nk_ref,
    nv_ref,
    out_ref,
    bias_ref,
):
    half_tokens = near_ref.shape[0]
    span = dk_ref.shape[0]
    suffix = sk_ref.shape[0]
    blocks_here = span // BLOCK
    me = me_ref[0]
    parity = lax.rem(me, 2)
    live_left = len_ref[lax.div(me, 2)] - parity * suffix
    first_block = me * blocks_here
    flag_row = lax.div(first_block, LANES)
    flag_lane = lax.rem(first_block, LANES)
    row_ids = lax.broadcasted_iota(jnp.int32, (1, flag_rows, LANES), 1)
    pick = (
        lax.broadcasted_iota(jnp.int32, (LANES, span), 0)
        == flag_lane + lax.broadcasted_iota(jnp.int32, (LANES, span), 1) // BLOCK
    ).astype(jnp.float32).astype(jnp.bfloat16)
    lane_ids = lax.broadcasted_iota(jnp.int32, (2 * SLOTS * GROUPS, LANES), 1)

    def do_chunk(chunk, local):
        start = chunk * SLOTS
        flags = near_ref[pl.ds(start, SLOTS), HEADS:, :].astype(jnp.float32) + far_ref[
            pl.ds(start, SLOTS), HEADS:, :
        ].astype(jnp.float32)
        flags = jnp.sum(jnp.where(row_ids == flag_row, flags, 0.0), axis=1)
        count = jnp.dot(flags.astype(jnp.bfloat16), pick, preferred_element_type=jnp.float32)
        bias = jnp.where(count > 0.5, 0.0, NEG_BIG)
        for s in range(SLOTS):
            bias_ref[s * GROUPS : (s + 1) * GROUPS, :] = jnp.broadcast_to(
                bias[s : s + 1, :], (GROUPS, span)
            )
        chunk_mask = chunk * (2 * SLOTS)
        folded = chunk
        for shift in (8, 4, 2, 1):
            folded = folded ^ (folded >> shift)
        chunk_mask = chunk_mask ^ (folded & 1)
        stats = jnp.zeros((2 * SLOTS * GROUPS, LANES), jnp.float32)
        for head in range(KVH):
            rows = slice(head * GROUPS, (head + 1) * GROUPS)
            cols = slice(head * HD, (head + 1) * HD)
            q = jnp.concatenate(
                [
                    ref[pl.ds(start, SLOTS), rows, :].astype(jnp.float32).reshape(SLOTS * GROUPS, HD)
                    for ref in (near_ref, far_ref)
                ],
                axis=0,
            ).astype(jnp.bfloat16)
            scores = lane_dot(q, dk_ref[:, cols])
            bias = bias_ref[...]
            scores = scores + jnp.concatenate([bias, bias], axis=0)
            top, total, weights = partial_softmax(scores)
            out = jnp.dot(weights, dv_ref[:, cols], preferred_element_type=jnp.float32)
            if local:
                pick_rows = lambda x: jnp.concatenate(
                    [x[0:GROUPS], x[SLOTS * GROUPS : (SLOTS + 1) * GROUPS]], axis=0
                )
                q_own = pick_rows(q.astype(jnp.float32))
                s_scores = lane_dot(q_own.astype(jnp.bfloat16), sk_ref[:, cols])
                position = lax.broadcasted_iota(jnp.int32, s_scores.shape, 1)
                s_scores = jnp.where(position < live_left, s_scores, NEG_BIG)
                s_top, s_total, s_weights = partial_softmax(s_scores)
                s_out = jnp.dot(s_weights, sv_ref[:, cols], preferred_element_type=jnp.float32)
                n_top = jnp.sum(
                    q_own * nk_ref[:, cols].astype(jnp.float32), axis=-1, keepdims=True
                )
                hidden = (lax.broadcasted_iota(jnp.int32, n_top.shape, 0) >= GROUPS) & (parity == 1)
                n_top = jnp.where(hidden, NEG_BIG, n_top)
                d_top, d_total, d_out = pick_rows(top), pick_rows(total), pick_rows(out)
                new_top = jnp.maximum(jnp.maximum(d_top, s_top), n_top)
                base = jnp.maximum(new_top, NEG_SAFE)
                d_scale = jnp.exp2((d_top - base) * EXP2_SCALE)
                s_scale = jnp.exp2((s_top - base) * EXP2_SCALE)
                n_scale = jnp.exp2((n_top - base) * EXP2_SCALE)
                new_total = d_scale * d_total + s_scale * s_total + n_scale
                new_out = (
                    d_scale * d_out
                    + s_scale * s_out
                    + n_scale * nv_ref[:, cols].astype(jnp.float32)
                )
                put_rows = lambda x, y: jnp.concatenate(
                    [
                        y[0:GROUPS],
                        x[GROUPS : SLOTS * GROUPS],
                        y[GROUPS:],
                        x[(SLOTS + 1) * GROUPS :],
                    ],
                    axis=0,
                )
                top, total, out = put_rows(top, new_top), put_rows(total, new_total), put_rows(
                    out, new_out
                )
            units = (out / jnp.maximum(total, 1.0)).astype(jnp.bfloat16)
            stats = jnp.where(lane_ids == head, top * EXP2_SCALE, stats)
            stats = jnp.where(lane_ids == KVH + head, total, stats)
            for s in range(2 * SLOTS):
                own = s % SLOTS
                mask = (own << 1) | (bin(own).count("1") & 1) ^ (s // SLOTS)
                out_ref[me ^ mask ^ chunk_mask, rows, :] = units[s * GROUPS : (s + 1) * GROUPS]
        high = stats.astype(jnp.bfloat16).astype(jnp.float32)
        rest = stats - high
        middle = rest.astype(jnp.bfloat16).astype(jnp.float32)
        low = rest - middle
        packed = high + pltpu.roll(middle, 2 * KVH, 1) + pltpu.roll(low, 4 * KVH, 1)
        packed = packed.astype(jnp.bfloat16)
        for s in range(2 * SLOTS):
            own = s % SLOTS
            mask = (own << 1) | (bin(own).count("1") & 1) ^ (s // SLOTS)
            out_ref[me ^ mask ^ chunk_mask, HEADS : HEADS + GROUPS, :] = packed[
                s * GROUPS : (s + 1) * GROUPS
            ]

    do_chunk(0, True)
    chunks = half_tokens // SLOTS
    if chunks > 1:
        lax.fori_loop(1, chunks, lambda c, _: do_chunk(c, False), None)


def combine_kernel(parts_ref, out_ref):
    packed = parts_ref[:, HEADS : HEADS + GROUPS, :].astype(jnp.float32)
    stats = (
        packed
        + pltpu.roll(packed, LANES - 2 * KVH, 2)
        + pltpu.roll(packed, LANES - 4 * KVH, 2)
    )
    live = lax.broadcasted_iota(jnp.int32, stats.shape, 2) < KVH
    top = jnp.where(live, stats, 0.0)
    total = jnp.where(live, pltpu.roll(stats, LANES - KVH, 2), 1.0)
    weight = jnp.exp2(top - jnp.max(top, axis=0, keepdims=True)) * total
    weight = weight / jnp.sum(weight, axis=0, keepdims=True)
    for head in range(KVH):
        rows = slice(head * GROUPS, (head + 1) * GROUPS)
        units = parts_ref[:, rows, :].astype(jnp.float32)
        mixed = jnp.sum(units * weight[:, :, head : head + 1], axis=0)
        for g in range(GROUPS):
            h = head * GROUPS + g
            out_ref[:, h * HD : (h + 1) * HD] = mixed[g : g + 1, :].astype(jnp.bfloat16)


def whole(space=VMEM):
    return pl.BlockSpec(memory_space=space)


def per_device(
    queries,
    new_keys,
    new_values,
    doc_keys,
    doc_values,
    suffix_keys,
    suffix_values,
    keep_lists,
    suffix_lengths,
):
    devices = lax.axis_size("seq")
    me = lax.axis_index("seq")
    blocks = devices * doc_keys.shape[0] // BLOCK
    flag_rows = 8 * pl.cdiv(blocks, 8 * LANES)
    packed = pl.pallas_call(
        functools.partial(pack_kernel, flag_rows),
        out_shape=jax.ShapeDtypeStruct((HEADS + flag_rows, HD), jnp.bfloat16),
        in_specs=[whole(SMEM), whole()],
        out_specs=whole(),
        name="pack",
    )(keep_lists, queries)
    near = packed[None]
    step = 2
    while step < devices:
        pairs = [(i, i ^ (step | 1)) for i in range(devices)]
        near = jnp.concatenate([near, lax.ppermute(near, "seq", pairs)], axis=0)
        step *= 2
    far = lax.ppermute(near, "seq", [(i, i ^ 1) for i in range(devices)])
    spread = pl.pallas_call(
        functools.partial(attend_kernel, flag_rows),
        out_shape=jax.ShapeDtypeStruct((devices, HEADS + GROUPS, HD), jnp.bfloat16),
        in_specs=[whole(SMEM), whole(SMEM)] + [whole()] * 8,
        out_specs=whole(),
        scratch_shapes=[VMEM((SLOTS * GROUPS, doc_keys.shape[0]), jnp.float32)],
        name="attend",
    )(
        me.astype(jnp.int32).reshape(1),
        suffix_lengths,
        near,
        far,
        doc_keys,
        doc_values,
        suffix_keys,
        suffix_values,
        new_keys,
        new_values,
    )
    parts = lax.all_to_all(spread, "seq", split_axis=0, concat_axis=0, tiled=True)
    return pl.pallas_call(
        combine_kernel,
        out_shape=jax.ShapeDtypeStruct((1, HEADS * HD), jnp.bfloat16),
        in_specs=[whole()],
        out_specs=whole(),
        name="combine",
    )(parts)


def solution(mesh):
    split = P(("parts", "seq"), None)
    return jax.shard_map(
        per_device,
        mesh=mesh,
        in_specs=(split,) * 8 + (P("parts"),),
        out_specs=split,
        check_vma=False,
    )
```

```python
import functools
import math

import jax
import jax.numpy as jnp
from jax import lax
from jax.experimental import pallas as pl
from jax.experimental.pallas import tpu as pltpu
from jax.sharding import PartitionSpec as P


HEADS = 64
KVH = 8
HD = 128
BLOCK = 128
GROUPS = HEADS // KVH
LANES = 128
SLOTS = 8

NEG_BIG = -1e30
NEG_SAFE = -5e29
EXP2_SCALE = HD**-0.5 * math.log2(math.e)

VMEM = pltpu.VMEM
SMEM = pltpu.SMEM


def pack_kernel(flag_rows, list_ref, q_ref, out_ref):
    q = q_ref[...].astype(jnp.float32)
    rows = [q[:, h * HD : (h + 1) * HD] for h in range(HEADS)]
    out_ref[0:HEADS, :] = jnp.concatenate(rows, axis=0).astype(jnp.bfloat16)
    ids = (
        lax.broadcasted_iota(jnp.int32, (flag_rows, LANES), 0) * LANES
        + lax.broadcasted_iota(jnp.int32, (flag_rows, LANES), 1)
    )

    def mark(k, found):
        return jnp.where(ids == list_ref[0, k], 1.0, found)

    found = lax.fori_loop(
        0, list_ref.shape[1], mark, jnp.zeros((flag_rows, LANES), jnp.float32), unroll=8
    )
    out_ref[HEADS : HEADS + flag_rows, :] = found.astype(jnp.bfloat16)


def lane_dot(a, b):
    return lax.dot_general(a, b, (((1,), (1,)), ((), ())), preferred_element_type=jnp.float32)


def partial_softmax(scores):
    top = jnp.max(scores, axis=-1, keepdims=True)
    weights = jnp.exp2((scores - jnp.maximum(top, NEG_SAFE)) * EXP2_SCALE)
    return top, jnp.sum(weights, axis=-1, keepdims=True), weights.astype(jnp.bfloat16)


def fetch_kernel(count, *refs):
    sources, targets, sem = refs[:count], refs[count : 2 * count], refs[-1]
    copies = [
        pltpu.make_async_copy(source, target, sem.at[i])
        for i, (source, target) in enumerate(zip(sources, targets))
    ]
    for copy in copies:
        copy.start()
    for copy in copies:
        copy.wait()


def suffix_kernel(
    me_ref, len_ref, own_ref, pair_ref, sk_ref, sv_ref, nk_ref, nv_ref, top_ref, total_ref, out_ref
):
    me = me_ref[0]
    parity = lax.rem(me, 2)
    live_left = len_ref[lax.div(me, 2)] - parity * sk_ref.shape[0]
    for head in range(KVH):
        rows = slice(head * GROUPS, (head + 1) * GROUPS)
        cols = slice(head * HD, (head + 1) * HD)
        q = jnp.concatenate(
            [ref[0, rows, :].astype(jnp.float32) for ref in (own_ref, pair_ref)], axis=0
        )
        scores = lane_dot(q.astype(jnp.bfloat16), sk_ref[:, cols])
        position = lax.broadcasted_iota(jnp.int32, scores.shape, 1)
        scores = jnp.where(position < live_left, scores, NEG_BIG)
        s_top, s_total, weights = partial_softmax(scores)
        s_out = jnp.dot(weights, sv_ref[:, cols], preferred_element_type=jnp.float32)
        n_top = jnp.sum(q * nk_ref[:, cols].astype(jnp.float32), axis=-1, keepdims=True)
        hidden = (lax.broadcasted_iota(jnp.int32, n_top.shape, 0) >= GROUPS) & (parity == 1)
        n_top = jnp.where(hidden, NEG_BIG, n_top)
        top = jnp.maximum(s_top, n_top)
        base = jnp.maximum(top, NEG_SAFE)
        s_scale = jnp.exp2((s_top - base) * EXP2_SCALE)
        n_scale = jnp.exp2((n_top - base) * EXP2_SCALE)
        top_ref[head] = jnp.broadcast_to(top, (2 * GROUPS, LANES))
        total_ref[head] = jnp.broadcast_to(s_scale * s_total + n_scale, (2 * GROUPS, LANES))
        out_ref[head] = s_scale * s_out + n_scale * nv_ref[:, cols].astype(jnp.float32)


def split_stats(stats, axis):
    high = stats.astype(jnp.bfloat16).astype(jnp.float32)
    rest = stats - high
    middle = rest.astype(jnp.bfloat16).astype(jnp.float32)
    low = rest - middle
    packed = high + pltpu.roll(middle, 2 * KVH, axis) + pltpu.roll(low, 4 * KVH, axis)
    return packed.astype(jnp.bfloat16)


def join_stats(packed, axis):
    packed = packed.astype(jnp.float32)
    stats = (
        packed
        + pltpu.roll(packed, LANES - 2 * KVH, axis)
        + pltpu.roll(packed, LANES - 4 * KVH, axis)
    )
    live = lax.broadcasted_iota(jnp.int32, stats.shape, axis) < KVH
    top = jnp.where(live, stats, 0.0)
    total = jnp.where(live, pltpu.roll(stats, LANES - KVH, axis), 0.0)
    return top, total


def attend_kernel(
    flag_rows,
    me_ref,
    near_ref,
    far_ref,
    dk_ref,
    dv_ref,
    top_ref,
    total_ref,
    extra_ref,
    near_out_ref,
    far_out_ref,
    bias_ref,
):
    half_tokens = near_ref.shape[0]
    span = dk_ref.shape[0]
    half = SLOTS * GROUPS
    first_block = me_ref[0] * (span // BLOCK)
    flag_row = lax.div(first_block, LANES)
    flag_lane = lax.rem(first_block, LANES)
    row_ids = lax.broadcasted_iota(jnp.int32, (1, flag_rows, LANES), 1)
    pick = (
        lax.broadcasted_iota(jnp.int32, (LANES, span), 0)
        == flag_lane + lax.broadcasted_iota(jnp.int32, (LANES, span), 1) // BLOCK
    ).astype(jnp.float32).astype(jnp.bfloat16)
    lane_ids = lax.broadcasted_iota(jnp.int32, (2 * half, LANES), 1)

    def do_chunk(chunk, local):
        start = chunk * SLOTS
        slots = pl.ds(start, SLOTS)
        flags = near_ref[slots, HEADS:, :].astype(jnp.float32) + far_ref[slots, HEADS:, :].astype(
            jnp.float32
        )
        flags = jnp.sum(jnp.where(row_ids == flag_row, flags, 0.0), axis=1)
        count = jnp.dot(flags.astype(jnp.bfloat16), pick, preferred_element_type=jnp.float32)
        bias = jnp.where(count > 0.5, 0.0, NEG_BIG)
        for s in range(SLOTS):
            bias_ref[s * GROUPS : (s + 1) * GROUPS, :] = jnp.broadcast_to(
                bias[s : s + 1, :], (GROUPS, span)
            )

        def scores_of(head):
            rows = slice(head * GROUPS, (head + 1) * GROUPS)
            q = jnp.concatenate(
                [
                    ref[slots, rows, :].astype(jnp.float32).reshape(half, HD)
                    for ref in (near_ref, far_ref)
                ],
                axis=0,
            ).astype(jnp.bfloat16)
            scores = lane_dot(q, dk_ref[:, head * HD : (head + 1) * HD])
            bias = bias_ref[...]
            return scores + jnp.concatenate([bias, bias], axis=0)

        stats = jnp.zeros((2 * half, LANES), jnp.float32)
        upcoming = scores_of(0)
        for head in range(KVH):
            rows = slice(head * GROUPS, (head + 1) * GROUPS)
            cols = slice(head * HD, (head + 1) * HD)
            scores = upcoming
            if head + 1 < KVH:
                upcoming = scores_of(head + 1)
            top, total, weights = partial_softmax(scores)
            out = jnp.dot(weights, dv_ref[:, cols], preferred_element_type=jnp.float32)
            if local:

                def joined(at, x_top, x_total, x_out):
                    own = slice(at * GROUPS, (at + 1) * GROUPS)
                    y_top = top_ref[head, own, 0:1]
                    new_top = jnp.maximum(x_top, y_top)
                    base = jnp.maximum(new_top, NEG_SAFE)
                    x_scale = jnp.exp2((x_top - base) * EXP2_SCALE)
                    y_scale = jnp.exp2((y_top - base) * EXP2_SCALE)
                    return (
                        new_top,
                        x_scale * x_total + y_scale * total_ref[head, own, 0:1],
                        x_scale * x_out + y_scale * extra_ref[head, own, :],
                    )

                pieces = []
                for at in range(2):
                    lo = at * half
                    first = slice(lo, lo + GROUPS)
                    others = slice(lo + GROUPS, lo + half)
                    new = joined(at, top[first], total[first], out[first])
                    pieces.append(new)
                    pieces.append((top[others], total[others], out[others]))
                top, total, out = [jnp.concatenate(p, axis=0) for p in zip(*pieces)]
            units = (out / jnp.maximum(total, 1.0)).astype(jnp.bfloat16)
            stats = jnp.where(lane_ids == head, top * EXP2_SCALE, stats)
            stats = jnp.where(lane_ids == KVH + head, total, stats)
            near_out_ref[slots, rows, :] = units[:half].reshape(SLOTS, GROUPS, HD)
            far_out_ref[slots, rows, :] = units[half:].reshape(SLOTS, GROUPS, HD)
        packed = split_stats(stats, 1)
        rows = slice(HEADS, HEADS + GROUPS)
        near_out_ref[slots, rows, :] = packed[:half].reshape(SLOTS, GROUPS, LANES)
        far_out_ref[slots, rows, :] = packed[half:].reshape(SLOTS, GROUPS, LANES)

    do_chunk(0, True)
    chunks = half_tokens // SLOTS
    if chunks > 1:
        lax.fori_loop(1, chunks, lambda c, _: do_chunk(c, False), None)


def mix_weights(mine_ref, theirs_ref):
    rows = slice(HEADS, HEADS + GROUPS)
    a_top, a_total = join_stats(mine_ref[:, rows, :], 2)
    b_top, b_total = join_stats(theirs_ref[:, rows, :], 2)
    top = jnp.maximum(a_top, b_top)
    a_weight = jnp.exp2(a_top - top) * a_total
    b_weight = jnp.exp2(b_top - top) * b_total
    total = a_weight + b_weight
    scale = 1.0 / jnp.maximum(total, 1.0)
    return top, total, a_weight * scale, b_weight * scale


def mixed_units(head, mine_ref, theirs_ref, a_weight, b_weight):
    rows = slice(head * GROUPS, (head + 1) * GROUPS)
    one = slice(head, head + 1)
    return mine_ref[:, rows, :].astype(jnp.float32) * a_weight[:, :, one] + theirs_ref[
        :, rows, :
    ].astype(jnp.float32) * b_weight[:, :, one]


def merge_kernel(mine_ref, theirs_ref, keep_ref, send_ref):
    half = keep_ref.shape[0]
    top, total, a_weight, b_weight = mix_weights(mine_ref, theirs_ref)
    for head in range(KVH):
        rows = slice(head * GROUPS, (head + 1) * GROUPS)
        units = mixed_units(head, mine_ref, theirs_ref, a_weight, b_weight).astype(jnp.bfloat16)
        keep_ref[:, rows, :] = units[:half]
        send_ref[:, rows, :] = units[half:]
    packed = split_stats(top + pltpu.roll(total, KVH, 2), 2)
    keep_ref[:, HEADS : HEADS + GROUPS, :] = packed[:half]
    send_ref[:, HEADS : HEADS + GROUPS, :] = packed[half:]


def finish_kernel(mine_ref, theirs_ref, out_ref):
    _, _, a_weight, b_weight = mix_weights(mine_ref, theirs_ref)
    for head in range(KVH):
        units = mixed_units(head, mine_ref, theirs_ref, a_weight, b_weight)[0]
        for g in range(GROUPS):
            h = head * GROUPS + g
            out_ref[:, h * HD : (h + 1) * HD] = units[g : g + 1, :].astype(jnp.bfloat16)


def whole(space=VMEM):
    return pl.BlockSpec(memory_space=space)


def near_core(x):
    return pltpu.with_memory_space_constraint(x, VMEM)


def on_core(kernel, out_shape, operands, scalars=0, cost=None, **kwargs):
    in_specs = [whole(SMEM)] * scalars + [whole()] * (len(operands) - scalars)
    return pl.pallas_call(
        kernel,
        out_shape=out_shape,
        in_specs=kwargs.pop("in_specs", in_specs),
        out_specs=jax.tree.map(lambda _: whole(), out_shape),
        compiler_params=pltpu.CompilerParams(vmem_limit_bytes=16 << 20),
        cost_estimate=cost,
        **kwargs,
    )(*operands)


def swap(x, bits):
    devices = lax.axis_size("seq")
    return lax.ppermute(x, "seq", [(i, i ^ bits) for i in range(devices)])


def per_device(
    queries,
    new_keys,
    new_values,
    doc_keys,
    doc_values,
    suffix_keys,
    suffix_values,
    keep_lists,
    suffix_lengths,
):
    devices = lax.axis_size("seq")
    me = lax.axis_index("seq").astype(jnp.int32).reshape(1)
    blocks = devices * doc_keys.shape[0] // BLOCK
    flag_rows = 8 * pl.cdiv(blocks, 8 * LANES)
    strides = []
    while 2 ** (len(strides) + 1) < devices:
        strides.insert(0, 2 ** (len(strides) + 1) | 1)
    packed = on_core(
        functools.partial(pack_kernel, flag_rows),
        VMEM((HEADS + flag_rows, HD), jnp.bfloat16),
        (keep_lists, queries),
        scalars=1,
    )
    near = packed[None]
    own = near
    caches = (doc_keys, doc_values, suffix_keys, suffix_values)
    size = sum(c.size * 2 for c in caches)
    dk, dv, sk, sv = on_core(
        functools.partial(fetch_kernel, len(caches)),
        [VMEM(c.shape, c.dtype) for c in caches],
        [pltpu.with_memory_space_constraint(c, pltpu.HBM) for c in caches],
        in_specs=[whole(pltpu.HBM)] * len(caches),
        scratch_shapes=[pltpu.SemaphoreType.DMA((len(caches),))],
        cost=pl.CostEstimate(flops=0, bytes_accessed=size, transcendentals=0),
    )
    pair = swap(own, 1)
    stat = VMEM((KVH, 2 * GROUPS, LANES), jnp.float32)
    local = on_core(
        suffix_kernel,
        [stat, stat, VMEM((KVH, 2 * GROUPS, HD), jnp.float32)],
        (me, suffix_lengths, own, near_core(pair), sk, sv, new_keys, new_values),
        scalars=2,
        cost=pl.CostEstimate(flops=10**9, bytes_accessed=size // 2, transcendentals=10**6),
    )
    for bits in strides:
        arrived = swap(near, bits)
        near = jnp.concatenate([near, arrived], axis=0)
    far = swap(near, 1)
    tokens = lambda count: VMEM((count, HEADS + GROUPS, HD), jnp.bfloat16)
    keep, send = on_core(
        functools.partial(attend_kernel, flag_rows),
        [tokens(devices // 2)] * 2,
        (me, near_core(near), near_core(far), dk, dv, *local),
        scalars=1,
        scratch_shapes=[VMEM((SLOTS * GROUPS, doc_keys.shape[0]), jnp.float32)],
    )
    bits = 1
    while strides:
        count = keep.shape[0] // 2
        keep, send = on_core(merge_kernel, [tokens(count)] * 2, (keep, near_core(swap(send, bits))))
        bits = strides.pop()
    return on_core(
        finish_kernel,
        jax.ShapeDtypeStruct((1, HEADS * HD), jnp.bfloat16),
        (keep, near_core(swap(send, bits))),
    )


def solution(mesh):
    split = P(("parts", "seq"), None)
    return jax.shard_map(
        per_device,
        mesh=mesh,
        in_specs=(split,) * 8 + (P("parts"),),
        out_specs=split,
        check_vma=False,
    )
```

```python
import functools
import math

import jax
import jax.numpy as jnp
from jax import lax
from jax.experimental import pallas as pl
from jax.experimental.pallas import tpu as pltpu
from jax.sharding import PartitionSpec as P


HEADS = 64
KVH = 8
HD = 128
BLOCK = 128
GROUPS = HEADS // KVH
LANES = 128
SLOTS = 8

NEG_BIG = -1e30
NEG_SAFE = -5e29
AHEAD = 2
EXP2_SCALE = HD**-0.5 * math.log2(math.e)

VMEM = pltpu.VMEM


def pack_kernel(list_ref, q_ref, out_ref):
    q = q_ref[...].astype(jnp.float32)
    rows = [q[:, h * HD : (h + 1) * HD] for h in range(HEADS)]
    out_ref[0:HEADS, :] = jnp.concatenate(rows, axis=0).astype(jnp.bfloat16)
    entries = list_ref.shape[1]
    ids = list_ref[...].astype(jnp.float32)
    diagonal = lax.broadcasted_iota(jnp.int32, (entries, entries), 0) == lax.broadcasted_iota(
        jnp.int32, (entries, entries), 1
    )
    column = jnp.sum(jnp.where(diagonal, ids, 0.0), axis=1, keepdims=True)
    lanes = lax.broadcasted_iota(jnp.int32, (entries, LANES), 1).astype(jnp.float32)
    found = [
        jnp.max(jnp.where(column == lanes + float(i * LANES), 1.0, 0.0), axis=0, keepdims=True)
        for i in range(out_ref.shape[0] - HEADS)
    ]
    out_ref[HEADS:, :] = jnp.concatenate(found, axis=0).astype(jnp.bfloat16)


def lane_dot(a, b):
    return lax.dot_general(a, b, (((1,), (1,)), ((), ())), preferred_element_type=jnp.float32)


def partial_softmax(scores):
    top = jnp.max(scores, axis=-1, keepdims=True)
    weights = jnp.exp2((scores - jnp.maximum(top, NEG_SAFE)) * EXP2_SCALE)
    return top, jnp.sum(weights, axis=-1, keepdims=True), weights.astype(jnp.bfloat16)


def head_copies(source, target, sem):
    return [
        pltpu.make_async_copy(source.at[:, pl.ds(head * HD, HD)], target.at[head], sem.at[head])
        for head in range(KVH)
    ]


def fetch_kernel(sk_hbm, sv_hbm, sk_ref, sv_ref, sk_sem, sv_sem):
    copies = head_copies(sk_hbm, sk_ref, sk_sem) + head_copies(sv_hbm, sv_ref, sv_sem)
    for copy in copies:
        copy.start()
    for copy in copies:
        copy.wait()


def suffix_kernel(
    len_ref,
    own_ref,
    pair_ref,
    sk_ref,
    sv_ref,
    nk_ref,
    nv_ref,
    dk_hbm,
    dv_hbm,
    top_ref,
    total_ref,
    out_ref,
    dk_ref,
    dv_ref,
    dk_sem,
    dv_sem,
):
    copies = head_copies(dk_hbm, dk_ref, dk_sem) + head_copies(dv_hbm, dv_ref, dv_sem)
    for copy in copies:
        copy.start()
    me = lax.axis_index("seq")
    parity = lax.rem(me, 2)
    mine = lax.broadcasted_iota(jnp.int32, len_ref.shape, 1) == lax.div(me, 2)
    length = jnp.sum(
        jnp.where(mine, len_ref[...].astype(jnp.float32), 0.0), axis=1, keepdims=True
    )
    live_left = length.astype(jnp.int32) - parity * sk_ref.shape[1]

    def scores_of(head):
        rows = slice(head * GROUPS, (head + 1) * GROUPS)
        cols = slice(head * HD, (head + 1) * HD)
        q = jnp.concatenate(
            [ref[0, rows, :].astype(jnp.float32) for ref in (own_ref, pair_ref)], axis=0
        )
        scores = lane_dot(q.astype(jnp.bfloat16), sk_ref[head])
        position = lax.broadcasted_iota(jnp.int32, scores.shape, 1)
        scores = jnp.where(position < live_left, scores, NEG_BIG)
        n_top = jnp.sum(q * nk_ref[:, cols].astype(jnp.float32), axis=-1, keepdims=True)
        hidden = (lax.broadcasted_iota(jnp.int32, n_top.shape, 0) >= GROUPS) & (parity == 1)
        return scores, jnp.where(hidden, NEG_BIG, n_top)

    ready = [scores_of(head) for head in range(AHEAD)]
    for head in range(KVH):
        cols = slice(head * HD, (head + 1) * HD)
        scores, n_top = ready.pop(0)
        if head + AHEAD < KVH:
            ready.append(scores_of(head + AHEAD))
        top = jnp.maximum(jnp.max(scores, axis=-1, keepdims=True), n_top)
        base = jnp.maximum(top, NEG_SAFE)
        weights = jnp.exp2((scores - base) * EXP2_SCALE)
        n_scale = jnp.exp2((n_top - base) * EXP2_SCALE)
        total = jnp.sum(weights, axis=-1, keepdims=True) + n_scale
        out = jnp.dot(
            weights.astype(jnp.bfloat16), sv_ref[head], preferred_element_type=jnp.float32
        )
        top_ref[head] = jnp.broadcast_to(top, (2 * GROUPS, LANES))
        total_ref[head] = jnp.broadcast_to(total, (2 * GROUPS, LANES))
        out_ref[head] = out + n_scale * nv_ref[:, cols].astype(jnp.float32)
    for copy in copies:
        copy.wait()


def split_stats(stats, axis):
    high = stats.astype(jnp.bfloat16).astype(jnp.float32)
    rest = stats - high
    middle = rest.astype(jnp.bfloat16).astype(jnp.float32)
    low = rest - middle
    packed = high + pltpu.roll(middle, 2 * KVH, axis) + pltpu.roll(low, 4 * KVH, axis)
    return packed.astype(jnp.bfloat16)


def join_stats(packed, axis):
    packed = packed.astype(jnp.float32)
    shifted = lambda by: pltpu.roll(packed, LANES - by * KVH, axis)
    live = lax.broadcasted_iota(jnp.int32, packed.shape, axis) < KVH
    top = jnp.where(live, packed + shifted(2) + shifted(4), 0.0)
    total = jnp.where(live, shifted(1) + shifted(3) + shifted(5), 0.0)
    return top, total


def attend_kernel(
    flag_rows,
    near_ref,
    far_ref,
    dk_ref,
    dv_ref,
    top_ref,
    total_ref,
    extra_ref,
    near_out_ref,
    far_out_ref,
    bias_ref,
):
    half_tokens = near_ref.shape[0]
    span = dk_ref.shape[1]
    half = SLOTS * GROUPS
    first_block = lax.axis_index("seq") * (span // BLOCK)
    flag_row = lax.div(first_block, LANES)
    flag_lane = lax.rem(first_block, LANES)
    row_ids = lax.broadcasted_iota(jnp.int32, (1, flag_rows, LANES), 1)
    pick = (
        lax.broadcasted_iota(jnp.int32, (LANES, span), 0)
        == flag_lane + lax.broadcasted_iota(jnp.int32, (LANES, span), 1) // BLOCK
    ).astype(jnp.float32).astype(jnp.bfloat16)
    lane_ids = lax.broadcasted_iota(jnp.int32, (2 * half, LANES), 1)

    def do_chunk(chunk, local):
        start = chunk * SLOTS
        slots = pl.ds(start, SLOTS)
        flags = near_ref[slots, HEADS:, :].astype(jnp.float32) + far_ref[slots, HEADS:, :].astype(
            jnp.float32
        )
        flags = jnp.sum(jnp.where(row_ids == flag_row, flags, 0.0), axis=1)
        count = jnp.dot(flags.astype(jnp.bfloat16), pick, preferred_element_type=jnp.float32)
        bias = jnp.where(count > 0.5, 0.0, NEG_BIG)
        for s in range(SLOTS):
            bias_ref[s * GROUPS : (s + 1) * GROUPS, :] = jnp.broadcast_to(
                bias[s : s + 1, :], (GROUPS, span)
            )

        def scores_of(head):
            rows = slice(head * GROUPS, (head + 1) * GROUPS)
            q = jnp.concatenate(
                [
                    ref[slots, rows, :].astype(jnp.float32).reshape(half, HD)
                    for ref in (near_ref, far_ref)
                ],
                axis=0,
            ).astype(jnp.bfloat16)
            scores = lane_dot(q, dk_ref[head])
            bias = bias_ref[...]
            return scores + jnp.concatenate([bias, bias], axis=0)

        stats = jnp.zeros((2 * half, LANES), jnp.float32)
        upcoming = scores_of(0)
        for head in range(KVH):
            rows = slice(head * GROUPS, (head + 1) * GROUPS)
            scores = upcoming
            if head + 1 < KVH:
                upcoming = scores_of(head + 1)
            top, total, weights = partial_softmax(scores)
            out = jnp.dot(weights, dv_ref[head], preferred_element_type=jnp.float32)
            if local:

                def joined(at, x_top, x_total, x_out):
                    own = slice(at * GROUPS, (at + 1) * GROUPS)
                    y_top = top_ref[head, own, 0:1]
                    new_top = jnp.maximum(x_top, y_top)
                    base = jnp.maximum(new_top, NEG_SAFE)
                    x_scale = jnp.exp2((x_top - base) * EXP2_SCALE)
                    y_scale = jnp.exp2((y_top - base) * EXP2_SCALE)
                    return (
                        new_top,
                        x_scale * x_total + y_scale * total_ref[head, own, 0:1],
                        x_scale * x_out + y_scale * extra_ref[head, own, :],
                    )

                pieces = []
                for at in range(2):
                    lo = at * half
                    first = slice(lo, lo + GROUPS)
                    others = slice(lo + GROUPS, lo + half)
                    new = joined(at, top[first], total[first], out[first])
                    pieces.append(new)
                    pieces.append((top[others], total[others], out[others]))
                top, total, out = [jnp.concatenate(p, axis=0) for p in zip(*pieces)]
            units = (out / jnp.maximum(total, 1.0)).astype(jnp.bfloat16)
            stats = jnp.where(lane_ids == head, top * EXP2_SCALE, stats)
            stats = jnp.where(lane_ids == KVH + head, total, stats)
            near_out_ref[slots, rows, :] = units[:half].reshape(SLOTS, GROUPS, HD)
            far_out_ref[slots, rows, :] = units[half:].reshape(SLOTS, GROUPS, HD)
        packed = split_stats(stats, 1)
        rows = slice(HEADS, HEADS + GROUPS)
        near_out_ref[slots, rows, :] = packed[:half].reshape(SLOTS, GROUPS, LANES)
        far_out_ref[slots, rows, :] = packed[half:].reshape(SLOTS, GROUPS, LANES)

    do_chunk(0, True)
    chunks = half_tokens // SLOTS
    if chunks > 1:
        lax.fori_loop(1, chunks, lambda c, _: do_chunk(c, False), None)


def mix_weights(refs):
    rows = slice(HEADS, HEADS + GROUPS)
    stats = [join_stats(ref[:, rows, :], 2) for ref in refs]
    top = functools.reduce(jnp.maximum, [t for t, _ in stats])
    weights = [jnp.exp2(t - top) * total for t, total in stats]
    total = functools.reduce(jnp.add, weights)
    scale = 1.0 / jnp.maximum(total, 1.0)
    return top, total, [w * scale for w in weights]


def mixed_units(head, refs, weights):
    rows = slice(head * GROUPS, (head + 1) * GROUPS)
    return functools.reduce(
        jnp.add,
        [
            ref[:, rows, :].astype(jnp.float32) * w[:, :, head : head + 1]
            for ref, w in zip(refs, weights)
        ],
    )


def merge_kernel(count, *refs):
    sources, targets = refs[:count], refs[count:]
    top, total, weights = mix_weights(sources)
    size = targets[0].shape[0]
    for head in range(KVH):
        rows = slice(head * GROUPS, (head + 1) * GROUPS)
        units = mixed_units(head, sources, weights).astype(jnp.bfloat16)
        for i, target in enumerate(targets):
            target[:, rows, :] = units[i * size : (i + 1) * size]
    packed = split_stats(top + pltpu.roll(total, KVH, 2), 2)
    for i, target in enumerate(targets):
        target[:, HEADS : HEADS + GROUPS, :] = packed[i * size : (i + 1) * size]


def finish_kernel(count, *refs):
    sources, out_ref = refs[:count], refs[count]
    _, _, weights = mix_weights(sources)
    for head in range(KVH):
        units = mixed_units(head, sources, weights)[0]
        for g in range(GROUPS):
            h = head * GROUPS + g
            out_ref[:, h * HD : (h + 1) * HD] = units[g : g + 1, :].astype(jnp.bfloat16)


def whole(space=VMEM):
    return pl.BlockSpec(memory_space=space)


def near_core(x):
    return pltpu.with_memory_space_constraint(x, VMEM)


def on_core(kernel, out_shape, operands, cost=None, **kwargs):
    return pl.pallas_call(
        kernel,
        out_shape=out_shape,
        in_specs=kwargs.pop("in_specs", [whole()] * len(operands)),
        out_specs=jax.tree.map(lambda _: whole(), out_shape),
        compiler_params=pltpu.CompilerParams(vmem_limit_bytes=16 << 20),
        cost_estimate=cost,
        **kwargs,
    )(*operands)


def in_hbm(x):
    return pltpu.with_memory_space_constraint(x, pltpu.HBM)


def swap(x, bits):
    devices = lax.axis_size("seq")
    return lax.ppermute(x, "seq", [(i, i ^ bits) for i in range(devices)])


def stages_of(devices):
    far_bits = []
    while 2 ** (len(far_bits) + 3) < devices:
        far_bits.insert(0, (2 ** (len(far_bits) + 3) | 1,))
    return far_bits + [(3, 5, 7)[: devices // 2 - 1]]


def per_device(
    queries,
    new_keys,
    new_values,
    doc_keys,
    doc_values,
    suffix_keys,
    suffix_values,
    keep_lists,
    suffix_lengths,
):
    devices = lax.axis_size("seq")
    blocks = devices * doc_keys.shape[0] // BLOCK
    flag_rows = 8 * pl.cdiv(blocks, 8 * LANES)
    stages = stages_of(devices)
    packed = on_core(
        pack_kernel,
        VMEM((HEADS + flag_rows, HD), jnp.bfloat16),
        (in_hbm(keep_lists), in_hbm(queries)),
    )
    near = packed[None]
    own = near
    by_head = lambda x: VMEM((KVH, x.shape[0], HD), x.dtype)
    sems = pltpu.SemaphoreType.DMA((KVH,))
    hbm = whole(pltpu.HBM)
    size = 2 * (suffix_keys.size + suffix_values.size)
    sk, sv = on_core(
        fetch_kernel,
        [by_head(suffix_keys), by_head(suffix_values)],
        (in_hbm(suffix_keys), in_hbm(suffix_values)),
        in_specs=[hbm] * 2,
        scratch_shapes=[sems, sems],
        cost=pl.CostEstimate(flops=0, bytes_accessed=size, transcendentals=0),
    )
    pair = swap(own, 1)
    stat = VMEM((KVH, 2 * GROUPS, LANES), jnp.float32)
    *local, dk, dv = on_core(
        suffix_kernel,
        [stat, stat, VMEM((KVH, 2 * GROUPS, HD), jnp.float32)] + [by_head(doc_keys), by_head(doc_values)],
        (
            near_core(suffix_lengths[None]),
            own,
            near_core(pair),
            sk,
            sv,
            new_keys,
            new_values,
            in_hbm(doc_keys),
            in_hbm(doc_values),
        ),
        in_specs=[whole()] * 7 + [hbm] * 2,
        scratch_shapes=[sems, sems],
        cost=pl.CostEstimate(flops=10**9, bytes_accessed=size, transcendentals=10**6),
    )
    for step, stage in enumerate(stages):
        arrived = []
        for bits in stage:
            arrived.append(swap(near, bits))
        near = jnp.concatenate([near] + arrived, axis=0)
    far = swap(near, 1)
    tokens = lambda count: VMEM((count, HEADS + GROUPS, HD), jnp.bfloat16)
    parts = on_core(
        functools.partial(attend_kernel, flag_rows),
        [tokens(devices // 2)] * 2,
        (near_core(near), near_core(far), dk, dv, *local),
        scratch_shapes=[VMEM((SLOTS * GROUPS, doc_keys.shape[0]), jnp.float32)],
    )
    step = len(stages)
    stages.append((1,))
    while stages:
        stage = stages.pop()
        sources = [parts[0]]
        for bits, part in zip(stage, parts[1:]):
            sources.append(near_core(swap(part, bits)))
        step -= 1
        if stages:
            pieces = len(stages[-1]) + 1
            parts = on_core(
                functools.partial(merge_kernel, len(sources)),
                [tokens(sources[0].shape[0] // pieces)] * pieces,
                sources,
            )
    return on_core(
        functools.partial(finish_kernel, len(sources)),
        jax.ShapeDtypeStruct((1, HEADS * HD), jnp.bfloat16),
        sources,
    )


def solution(mesh):
    split = P(("parts", "seq"), None)
    return jax.shard_map(
        per_device,
        mesh=mesh,
        in_specs=(split,) * 8 + (P("parts"),),
        out_specs=split,
        check_vma=False,
    )
```

```python
import functools
import math

import jax
import jax.numpy as jnp
from jax import lax
from jax.experimental import pallas as pl
from jax.experimental.pallas import tpu as pltpu
from jax.sharding import PartitionSpec as P


HEADS = 64
KVH = 8
HD = 128
BLOCK = 128
GROUPS = HEADS // KVH
LANES = 128
SLOTS = 8

NEG_BIG = -1e30
NEG_SAFE = -5e29
AHEAD = 2
DOC_AHEAD = 2
EXP2_SCALE = HD**-0.5 * math.log2(math.e)

VMEM = pltpu.VMEM


def pack_kernel(list_ref, q_ref, out_ref):
    q = q_ref[...].astype(jnp.float32)
    rows = [q[:, h * HD : (h + 1) * HD] for h in range(HEADS)]
    out_ref[0:HEADS, :] = jnp.concatenate(rows, axis=0).astype(jnp.bfloat16)
    entries = list_ref.shape[1]
    ids = list_ref[...].astype(jnp.float32)
    diagonal = lax.broadcasted_iota(jnp.int32, (entries, entries), 0) == lax.broadcasted_iota(
        jnp.int32, (entries, entries), 1
    )
    column = jnp.sum(jnp.where(diagonal, ids, 0.0), axis=1, keepdims=True)
    lanes = lax.broadcasted_iota(jnp.int32, (entries, LANES), 1).astype(jnp.float32)
    found = [
        jnp.max(jnp.where(column == lanes + float(i * LANES), 1.0, 0.0), axis=0, keepdims=True)
        for i in range(out_ref.shape[0] - HEADS)
    ]
    out_ref[HEADS:, :] = jnp.concatenate(found, axis=0).astype(jnp.bfloat16)


def lane_dot(a, b):
    return lax.dot_general(a, b, (((1,), (1,)), ((), ())), preferred_element_type=jnp.float32)


def partial_softmax(scores):
    top = jnp.max(scores, axis=-1, keepdims=True)
    weights = jnp.exp2((scores - jnp.maximum(top, NEG_SAFE)) * EXP2_SCALE)
    return top, jnp.sum(weights, axis=-1, keepdims=True), weights.astype(jnp.bfloat16)


def head_copies(source, target, sem):
    return [
        pltpu.make_async_copy(source.at[:, pl.ds(head * HD, HD)], target.at[head], sem.at[head])
        for head in range(KVH)
    ]


def fetch_kernel(source, target, sem):
    copies = head_copies(source, target, sem)
    for copy in copies:
        copy.start()
    for copy in copies:
        copy.wait()


def suffix_kernel(
    len_ref,
    own_ref,
    pair_ref,
    sk_ref,
    nk_ref,
    nv_ref,
    sv_hbm,
    dk_hbm,
    dv_hbm,
    top_ref,
    total_ref,
    out_ref,
    dk_ref,
    dv_ref,
    sv_ref,
    sv_sem,
    dk_sem,
    dv_sem,
):
    arriving = head_copies(sv_hbm, sv_ref, sv_sem)
    copies = head_copies(dk_hbm, dk_ref, dk_sem) + head_copies(dv_hbm, dv_ref, dv_sem)
    for copy in arriving + copies:
        copy.start()
    me = lax.axis_index("seq")
    parity = lax.rem(me, 2)
    mine = lax.broadcasted_iota(jnp.int32, len_ref.shape, 1) == lax.div(me, 2)
    length = jnp.sum(
        jnp.where(mine, len_ref[...].astype(jnp.float32), 0.0), axis=1, keepdims=True
    )
    live_left = length.astype(jnp.int32) - parity * sk_ref.shape[1]

    def scores_of(head):
        rows = slice(head * GROUPS, (head + 1) * GROUPS)
        cols = slice(head * HD, (head + 1) * HD)
        q = jnp.concatenate(
            [ref[0, rows, :].astype(jnp.float32) for ref in (own_ref, pair_ref)], axis=0
        )
        scores = lane_dot(q.astype(jnp.bfloat16), sk_ref[head])
        position = lax.broadcasted_iota(jnp.int32, scores.shape, 1)
        scores = jnp.where(position < live_left, scores, NEG_BIG)
        n_top = jnp.sum(q * nk_ref[:, cols].astype(jnp.float32), axis=-1, keepdims=True)
        hidden = (lax.broadcasted_iota(jnp.int32, n_top.shape, 0) >= GROUPS) & (parity == 1)
        return scores, jnp.where(hidden, NEG_BIG, n_top)

    ready = [scores_of(head) for head in range(AHEAD)]
    for head in range(KVH):
        cols = slice(head * HD, (head + 1) * HD)
        scores, n_top = ready.pop(0)
        if head + AHEAD < KVH:
            ready.append(scores_of(head + AHEAD))
        top = jnp.maximum(jnp.max(scores, axis=-1, keepdims=True), n_top)
        base = jnp.maximum(top, NEG_SAFE)
        weights = jnp.exp2((scores - base) * EXP2_SCALE)
        n_scale = jnp.exp2((n_top - base) * EXP2_SCALE)
        total = jnp.sum(weights, axis=-1, keepdims=True) + n_scale
        arriving[head].wait()
        out = jnp.dot(
            weights.astype(jnp.bfloat16), sv_ref[head], preferred_element_type=jnp.float32
        )
        top_ref[head] = jnp.broadcast_to(top, (2 * GROUPS, LANES))
        total_ref[head] = jnp.broadcast_to(total, (2 * GROUPS, LANES))
        out_ref[head] = out + n_scale * nv_ref[:, cols].astype(jnp.float32)
    for copy in copies:
        copy.wait()


def split_stats(stats, axis):
    high = stats.astype(jnp.bfloat16).astype(jnp.float32)
    rest = stats - high
    middle = rest.astype(jnp.bfloat16).astype(jnp.float32)
    low = rest - middle
    packed = high + pltpu.roll(middle, 2 * KVH, axis) + pltpu.roll(low, 4 * KVH, axis)
    return packed.astype(jnp.bfloat16)


def join_stats(packed, axis):
    packed = packed.astype(jnp.float32)
    shifted = lambda by: pltpu.roll(packed, LANES - by * KVH, axis)
    live = lax.broadcasted_iota(jnp.int32, packed.shape, axis) < KVH
    top = jnp.where(live, packed + shifted(2) + shifted(4), 0.0)
    total = jnp.where(live, shifted(1) + shifted(3) + shifted(5), 0.0)
    return top, total


def attend_kernel(
    flag_rows,
    which,
    token_ref,
    other_ref,
    dk_ref,
    dv_ref,
    top_ref,
    total_ref,
    extra_ref,
    out_ref,
    bias_ref,
):
    tokens = token_ref.shape[0]
    span = dk_ref.shape[1]
    rows_here = SLOTS * GROUPS
    first_block = lax.axis_index("seq") * (span // BLOCK)
    flag_row = lax.div(first_block, LANES)
    flag_lane = lax.rem(first_block, LANES)
    row_ids = lax.broadcasted_iota(jnp.int32, (1, flag_rows, LANES), 1)
    pick = (
        lax.broadcasted_iota(jnp.int32, (LANES, span), 0)
        == flag_lane + lax.broadcasted_iota(jnp.int32, (LANES, span), 1) // BLOCK
    ).astype(jnp.float32).astype(jnp.bfloat16)
    lane_ids = lax.broadcasted_iota(jnp.int32, (rows_here, LANES), 1)
    own = slice(which * GROUPS, (which + 1) * GROUPS)

    def do_chunk(chunk, local):
        slots = pl.ds(chunk * SLOTS, SLOTS)
        flags = token_ref[slots, HEADS:, :].astype(jnp.float32) + other_ref[
            slots, HEADS:, :
        ].astype(jnp.float32)
        flags = jnp.sum(jnp.where(row_ids == flag_row, flags, 0.0), axis=1)
        count = jnp.dot(flags.astype(jnp.bfloat16), pick, preferred_element_type=jnp.float32)
        bias = jnp.where(count > 0.5, 0.0, NEG_BIG)
        for s in range(SLOTS):
            bias_ref[s * GROUPS : (s + 1) * GROUPS, :] = jnp.broadcast_to(
                bias[s : s + 1, :], (GROUPS, span)
            )

        def scores_of(head):
            rows = slice(head * GROUPS, (head + 1) * GROUPS)
            q = token_ref[slots, rows, :].astype(jnp.float32).reshape(rows_here, HD)
            return lane_dot(q.astype(jnp.bfloat16), dk_ref[head]) + bias_ref[...]

        stats = jnp.zeros((rows_here, LANES), jnp.float32)
        ready = [scores_of(head) for head in range(DOC_AHEAD)]
        for head in range(KVH):
            rows = slice(head * GROUPS, (head + 1) * GROUPS)
            scores = ready.pop(0)
            if head + DOC_AHEAD < KVH:
                ready.append(scores_of(head + DOC_AHEAD))
            top, total, weights = partial_softmax(scores)
            out = jnp.dot(weights, dv_ref[head], preferred_element_type=jnp.float32)
            if local:
                x_top, y_top = top[:GROUPS], top_ref[head, own, 0:1]
                new_top = jnp.maximum(x_top, y_top)
                base = jnp.maximum(new_top, NEG_SAFE)
                x_scale = jnp.exp2((x_top - base) * EXP2_SCALE)
                y_scale = jnp.exp2((y_top - base) * EXP2_SCALE)
                new_total = x_scale * total[:GROUPS] + y_scale * total_ref[head, own, 0:1]
                new_out = x_scale * out[:GROUPS] + y_scale * extra_ref[head, own, :]
                top = jnp.concatenate([new_top, top[GROUPS:]], axis=0)
                total = jnp.concatenate([new_total, total[GROUPS:]], axis=0)
                out = jnp.concatenate([new_out, out[GROUPS:]], axis=0)
            units = (out / jnp.maximum(total, 1.0)).astype(jnp.bfloat16)
            stats = jnp.where(lane_ids == head, top * EXP2_SCALE, stats)
            stats = jnp.where(lane_ids == KVH + head, total, stats)
            out_ref[slots, rows, :] = units.reshape(SLOTS, GROUPS, HD)
        rows = slice(HEADS, HEADS + GROUPS)
        out_ref[slots, rows, :] = split_stats(stats, 1).reshape(SLOTS, GROUPS, LANES)

    do_chunk(0, True)
    chunks = tokens // SLOTS
    if chunks > 1:
        lax.fori_loop(1, chunks, lambda c, _: do_chunk(c, False), None)


def mix_weights(refs):
    rows = slice(HEADS, HEADS + GROUPS)
    stats = [join_stats(ref[:, rows, :], 2) for ref in refs]
    top = functools.reduce(jnp.maximum, [t for t, _ in stats])
    weights = [jnp.exp2(t - top) * total for t, total in stats]
    total = functools.reduce(jnp.add, weights)
    scale = 1.0 / jnp.maximum(total, 1.0)
    return top, total, [w * scale for w in weights]


def mixed_units(head, refs, weights):
    rows = slice(head * GROUPS, (head + 1) * GROUPS)
    return functools.reduce(
        jnp.add,
        [
            ref[:, rows, :].astype(jnp.float32) * w[:, :, head : head + 1]
            for ref, w in zip(refs, weights)
        ],
    )


def merge_kernel(count, *refs):
    sources, targets = refs[:count], refs[count:]
    top, total, weights = mix_weights(sources)
    size = targets[0].shape[0]
    for head in range(KVH):
        rows = slice(head * GROUPS, (head + 1) * GROUPS)
        units = mixed_units(head, sources, weights).astype(jnp.bfloat16)
        for i, target in enumerate(targets):
            target[:, rows, :] = units[i * size : (i + 1) * size]
    packed = split_stats(top + pltpu.roll(total, KVH, 2), 2)
    for i, target in enumerate(targets):
        target[:, HEADS : HEADS + GROUPS, :] = packed[i * size : (i + 1) * size]


def finish_kernel(count, *refs):
    sources, out_ref = refs[:count], refs[count]
    _, _, weights = mix_weights(sources)
    for head in range(KVH):
        units = mixed_units(head, sources, weights)[0]
        for g in range(GROUPS):
            h = head * GROUPS + g
            out_ref[:, h * HD : (h + 1) * HD] = units[g : g + 1, :].astype(jnp.bfloat16)


def whole(space=VMEM):
    return pl.BlockSpec(memory_space=space)


def near_core(x):
    return pltpu.with_memory_space_constraint(x, VMEM)


def on_core(kernel, out_shape, operands, cost=None, **kwargs):
    return pl.pallas_call(
        kernel,
        out_shape=out_shape,
        in_specs=kwargs.pop("in_specs", [whole()] * len(operands)),
        out_specs=jax.tree.map(lambda _: whole(), out_shape),
        compiler_params=pltpu.CompilerParams(vmem_limit_bytes=16 << 20),
        cost_estimate=cost,
        **kwargs,
    )(*operands)


def in_hbm(x):
    return pltpu.with_memory_space_constraint(x, pltpu.HBM)


def swap(x, bits):
    devices = lax.axis_size("seq")
    return lax.ppermute(x, "seq", [(i, i ^ bits) for i in range(devices)])


def stages_of(devices):
    far_bits = []
    while 2 ** (len(far_bits) + 3) < devices:
        far_bits.insert(0, (2 ** (len(far_bits) + 3) | 1,))
    return far_bits + [(3, 5, 7)[: devices // 2 - 1]]


def per_device(
    queries,
    new_keys,
    new_values,
    doc_keys,
    doc_values,
    suffix_keys,
    suffix_values,
    keep_lists,
    suffix_lengths,
):
    devices = lax.axis_size("seq")
    blocks = devices * doc_keys.shape[0] // BLOCK
    flag_rows = 8 * pl.cdiv(blocks, 8 * LANES)
    stages = stages_of(devices)
    packed = on_core(
        pack_kernel,
        VMEM((HEADS + flag_rows, HD), jnp.bfloat16),
        (in_hbm(keep_lists), in_hbm(queries)),
    )
    near = packed[None]
    own = near
    by_head = lambda x: VMEM((KVH, x.shape[0], HD), x.dtype)
    sems = pltpu.SemaphoreType.DMA((KVH,))
    hbm = whole(pltpu.HBM)
    size = 2 * suffix_keys.size
    sk = on_core(
        fetch_kernel,
        by_head(suffix_keys),
        (in_hbm(suffix_keys),),
        in_specs=[hbm],
        scratch_shapes=[sems],
        cost=pl.CostEstimate(flops=0, bytes_accessed=size, transcendentals=0),
    )
    pair = swap(own, 1)
    stat = VMEM((KVH, 2 * GROUPS, LANES), jnp.float32)
    *local, dk, dv = on_core(
        suffix_kernel,
        [stat, stat, VMEM((KVH, 2 * GROUPS, HD), jnp.float32)] + [by_head(doc_keys), by_head(doc_values)],
        (
            near_core(suffix_lengths[None]),
            own,
            near_core(pair),
            sk,
            new_keys,
            new_values,
            in_hbm(suffix_values),
            in_hbm(doc_keys),
            in_hbm(doc_values),
        ),
        in_specs=[whole()] * 6 + [hbm] * 3,
        scratch_shapes=[by_head(suffix_values), sems, sems, sems],
        cost=pl.CostEstimate(flops=10**9, bytes_accessed=3 * size, transcendentals=10**6),
    )
    for step, stage in enumerate(stages):
        arrived = []
        for bits in stage:
            arrived.append(swap(near, bits))
        near = jnp.concatenate([near] + arrived, axis=0)
    far = swap(near, 1)
    tokens = lambda count: VMEM((count, HEADS + GROUPS, HD), jnp.bfloat16)
    near, far = near_core(near), near_core(far)
    parts = [
        on_core(
            functools.partial(attend_kernel, flag_rows, which),
            tokens(devices // 2),
            (mine, other, dk, dv, *local),
            scratch_shapes=[VMEM((SLOTS * GROUPS, doc_keys.shape[0]), jnp.float32)],
            cost=pl.CostEstimate(flops=10**9, bytes_accessed=2 * size, transcendentals=10**6),
        )
        for which, mine, other in ((0, near, far), (1, far, near))
    ]
    step = len(stages)
    stages.append((1,))
    while stages:
        stage = stages.pop()
        sources = [parts[0]]
        for bits, part in zip(stage, parts[1:]):
            sources.append(near_core(swap(part, bits)))
        step -= 1
        if stages:
            pieces = len(stages[-1]) + 1
            parts = on_core(
                functools.partial(merge_kernel, len(sources)),
                [tokens(sources[0].shape[0] // pieces)] * pieces,
                sources,
            )
    return on_core(
        functools.partial(finish_kernel, len(sources)),
        jax.ShapeDtypeStruct((1, HEADS * HD), jnp.bfloat16),
        sources,
    )


def solution(mesh):
    split = P(("parts", "seq"), None)
    return jax.shard_map(
        per_device,
        mesh=mesh,
        in_specs=(split,) * 8 + (P("parts"),),
        out_specs=split,
        check_vma=False,
    )
```

```python
import functools
import math

import jax
import jax.numpy as jnp
from jax import lax
from jax.experimental import pallas as pl
from jax.experimental.pallas import tpu as pltpu
from jax.sharding import PartitionSpec as P


HEADS = 64
KVH = 8
HD = 128
BLOCK = 128
GROUPS = HEADS // KVH
LANES = 128
SLOTS = 8

NEG_BIG = -1e30
NEG_SAFE = -5e29
AHEAD = 4
DOC_AHEAD = 2
EXP2_SCALE = HD**-0.5 * math.log2(math.e)

VMEM = pltpu.VMEM


def pack_kernel(list_ref, q_ref, out_ref):
    q = q_ref[...].astype(jnp.float32)
    rows = [q[:, h * HD : (h + 1) * HD] for h in range(HEADS)]
    out_ref[0:HEADS, :] = jnp.concatenate(rows, axis=0).astype(jnp.bfloat16)
    entries = list_ref.shape[1]
    ids = list_ref[...].astype(jnp.float32)
    diagonal = lax.broadcasted_iota(jnp.int32, (entries, entries), 0) == lax.broadcasted_iota(
        jnp.int32, (entries, entries), 1
    )
    column = jnp.sum(jnp.where(diagonal, ids, 0.0), axis=1, keepdims=True)
    lanes = lax.broadcasted_iota(jnp.int32, (entries, LANES), 1).astype(jnp.float32)
    found = [
        jnp.max(jnp.where(column == lanes + float(i * LANES), 1.0, 0.0), axis=0, keepdims=True)
        for i in range(out_ref.shape[0] - HEADS)
    ]
    out_ref[HEADS:, :] = jnp.concatenate(found, axis=0).astype(jnp.bfloat16)


def lane_dot(a, b):
    return lax.dot_general(a, b, (((1,), (1,)), ((), ())), preferred_element_type=jnp.float32)


def partial_softmax(scores):
    top = jnp.max(scores, axis=-1, keepdims=True)
    weights = jnp.exp2((scores - jnp.maximum(top, NEG_SAFE)) * EXP2_SCALE)
    return top, jnp.sum(weights, axis=-1, keepdims=True), weights.astype(jnp.bfloat16)


def suffix_kernel(
    len_ref,
    own_ref,
    pair_ref,
    sk_ref,
    sv_ref,
    nk_ref,
    nv_ref,
    dk_ref,
    dv_ref,
    top_ref,
    total_ref,
    out_ref,
    dk_out_ref,
    dv_out_ref,
):
    me = lax.axis_index("seq")
    parity = lax.rem(me, 2)
    mine = lax.broadcasted_iota(jnp.int32, len_ref.shape, 1) == lax.div(me, 2)
    length = jnp.sum(
        jnp.where(mine, len_ref[...].astype(jnp.float32), 0.0), axis=1, keepdims=True
    )
    live_left = length.astype(jnp.int32) - parity * sv_ref.shape[0]

    def scores_of(head):
        rows = slice(head * GROUPS, (head + 1) * GROUPS)
        cols = slice(head * HD, (head + 1) * HD)
        q = jnp.concatenate(
            [ref[0, rows, :].astype(jnp.float32) for ref in (own_ref, pair_ref)], axis=0
        )
        scores = lane_dot(q.astype(jnp.bfloat16), sk_ref[:, cols])
        position = lax.broadcasted_iota(jnp.int32, scores.shape, 1)
        scores = jnp.where(position < live_left, scores, NEG_BIG)
        n_top = jnp.sum(q * nk_ref[:, cols].astype(jnp.float32), axis=-1, keepdims=True)
        hidden = (lax.broadcasted_iota(jnp.int32, n_top.shape, 0) >= GROUPS) & (parity == 1)
        return scores, jnp.where(hidden, NEG_BIG, n_top)

    ready = [scores_of(head) for head in range(AHEAD)]
    for head in range(KVH):
        cols = slice(head * HD, (head + 1) * HD)
        scores, n_top = ready.pop(0)
        if head + AHEAD < KVH:
            ready.append(scores_of(head + AHEAD))
        top = jnp.maximum(jnp.max(scores, axis=-1, keepdims=True), n_top)
        base = jnp.maximum(top, NEG_SAFE)
        weights = jnp.exp2((scores - base) * EXP2_SCALE)
        n_scale = jnp.exp2((n_top - base) * EXP2_SCALE)
        total = jnp.sum(weights, axis=-1, keepdims=True) + n_scale
        out = jnp.dot(
            weights.astype(jnp.bfloat16), sv_ref[:, cols], preferred_element_type=jnp.float32
        )
        top_ref[head] = jnp.broadcast_to(top, (2 * GROUPS, LANES))
        total_ref[head] = jnp.broadcast_to(total, (2 * GROUPS, LANES))
        out_ref[head] = out + n_scale * nv_ref[:, cols].astype(jnp.float32)
        dk_out_ref[head] = dk_ref[:, cols]
        dv_out_ref[head] = dv_ref[:, cols]


def split_stats(stats, axis):
    high = stats.astype(jnp.bfloat16).astype(jnp.float32)
    rest = stats - high
    middle = rest.astype(jnp.bfloat16).astype(jnp.float32)
    low = rest - middle
    packed = high + pltpu.roll(middle, 2 * KVH, axis) + pltpu.roll(low, 4 * KVH, axis)
    return packed.astype(jnp.bfloat16)


def join_stats(packed, axis):
    packed = packed.astype(jnp.float32)
    shifted = lambda by: pltpu.roll(packed, LANES - by * KVH, axis)
    live = lax.broadcasted_iota(jnp.int32, packed.shape, axis) < KVH
    top = jnp.where(live, packed + shifted(2) + shifted(4), 0.0)
    total = jnp.where(live, shifted(1) + shifted(3) + shifted(5), 0.0)
    return top, total


def attend_kernel(which, flag_rows, *refs):
    if flag_rows:
        token_ref, other_ref, *refs = refs
    else:
        token_ref, bias_ref, *refs = refs
    dk_ref, dv_ref, top_ref, total_ref, extra_ref, out_ref, *refs = refs
    if flag_rows:
        (bias_ref,) = refs
    tokens = token_ref.shape[0]
    span = dk_ref.shape[1]
    blocks_here = span // BLOCK
    rows_here = SLOTS * GROUPS
    first_block = lax.axis_index("seq") * blocks_here
    flag_row = lax.div(first_block, LANES)
    flag_lane = lax.rem(first_block, LANES)
    lane_ids = lax.broadcasted_iota(jnp.int32, (rows_here, LANES), 1)
    own = slice(which * GROUPS, (which + 1) * GROUPS)

    def do_chunk(chunk, local):
        slots = pl.ds(chunk * SLOTS, SLOTS)
        here = pl.ds(chunk * rows_here, rows_here)
        if flag_rows:
            flags = token_ref[slots, HEADS:, :].astype(jnp.float32) + other_ref[
                slots, HEADS:, :
            ].astype(jnp.float32)
            row_ids = lax.broadcasted_iota(jnp.int32, (1, flag_rows, LANES), 1)
            flags = jnp.sum(jnp.where(row_ids == flag_row, flags, 0.0), axis=1)
            flags = pltpu.roll(flags, LANES - flag_lane, 1)
            bias = jnp.where(flags > 0.5, 0.0, NEG_BIG)
            for b in range(blocks_here):
                wide = jnp.broadcast_to(bias[:, b : b + 1], (SLOTS, BLOCK))
                bias_ref[here, b * BLOCK : (b + 1) * BLOCK] = jnp.broadcast_to(
                    wide[:, None, :], (SLOTS, GROUPS, BLOCK)
                ).reshape(rows_here, BLOCK)

        def scores_of(head):
            rows = slice(head * GROUPS, (head + 1) * GROUPS)
            q = token_ref[slots, rows, :].astype(jnp.float32).reshape(rows_here, HD)
            return lane_dot(q.astype(jnp.bfloat16), dk_ref[head]) + bias_ref[here, :]

        stats = jnp.zeros((rows_here, LANES), jnp.float32)
        ready = [scores_of(head) for head in range(DOC_AHEAD)]
        for head in range(KVH):
            rows = slice(head * GROUPS, (head + 1) * GROUPS)
            scores = ready.pop(0)
            if head + DOC_AHEAD < KVH:
                ready.append(scores_of(head + DOC_AHEAD))
            top, total, weights = partial_softmax(scores)
            out = jnp.dot(
                weights, dv_ref[head], preferred_element_type=jnp.float32
            )
            if local:
                x_top, y_top = top[:GROUPS], top_ref[head, own, 0:1]
                new_top = jnp.maximum(x_top, y_top)
                base = jnp.maximum(new_top, NEG_SAFE)
                x_scale = jnp.exp2((x_top - base) * EXP2_SCALE)
                y_scale = jnp.exp2((y_top - base) * EXP2_SCALE)
                new_total = x_scale * total[:GROUPS] + y_scale * total_ref[head, own, 0:1]
                new_out = x_scale * out[:GROUPS] + y_scale * extra_ref[head, own, :]
                top = jnp.concatenate([new_top, top[GROUPS:]], axis=0)
                total = jnp.concatenate([new_total, total[GROUPS:]], axis=0)
                out = jnp.concatenate([new_out, out[GROUPS:]], axis=0)
            units = (out / jnp.maximum(total, 1.0)).astype(jnp.bfloat16)
            stats = jnp.where(lane_ids == head, top * EXP2_SCALE, stats)
            stats = jnp.where(lane_ids == KVH + head, total, stats)
            out_ref[slots, rows, :] = units.reshape(SLOTS, GROUPS, HD)
        rows = slice(HEADS, HEADS + GROUPS)
        out_ref[slots, rows, :] = split_stats(stats, 1).reshape(SLOTS, GROUPS, LANES)

    do_chunk(0, True)
    chunks = tokens // SLOTS
    if chunks > 1:
        lax.fori_loop(1, chunks, lambda c, _: do_chunk(c, False), None)


def mix_weights(refs):
    rows = slice(HEADS, HEADS + GROUPS)
    stats = [join_stats(ref[:, rows, :], 2) for ref in refs]
    top = functools.reduce(jnp.maximum, [t for t, _ in stats])
    weights = [jnp.exp2(t - top) * total for t, total in stats]
    total = functools.reduce(jnp.add, weights)
    scale = 1.0 / jnp.maximum(total, 1.0)
    return top, total, [w * scale for w in weights[1:]]


def mixed_units(head, refs, weights):
    rows = slice(head * GROUPS, (head + 1) * GROUPS)
    first, *others = [ref[:, rows, :].astype(jnp.float32) for ref in refs]
    steps = [(u - first) * w[:, :, head : head + 1] for u, w in zip(others, weights)]
    return functools.reduce(jnp.add, steps, first)


def merge_kernel(count, *refs):
    sources, targets = refs[:count], refs[count:]
    top, total, weights = mix_weights(sources)
    size = targets[0].shape[0]
    for head in range(KVH):
        rows = slice(head * GROUPS, (head + 1) * GROUPS)
        units = mixed_units(head, sources, weights).astype(jnp.bfloat16)
        for i, target in enumerate(targets):
            target[:, rows, :] = units[i * size : (i + 1) * size]
    packed = split_stats(top + pltpu.roll(total, KVH, 2), 2)
    for i, target in enumerate(targets):
        target[:, HEADS : HEADS + GROUPS, :] = packed[i * size : (i + 1) * size]


def finish_kernel(count, *refs):
    sources, out_ref = refs[:count], refs[count]
    _, _, weights = mix_weights(sources)
    for head in range(KVH):
        units = mixed_units(head, sources, weights)[0]
        for g in range(GROUPS):
            h = head * GROUPS + g
            out_ref[:, h * HD : (h + 1) * HD] = units[g : g + 1, :].astype(jnp.bfloat16)


def whole(space=VMEM):
    return pl.BlockSpec(memory_space=space)


def near_core(x):
    return pltpu.with_memory_space_constraint(x, VMEM)


def on_core(kernel, out_shape, operands, cost=None, **kwargs):
    return pl.pallas_call(
        kernel,
        out_shape=out_shape,
        in_specs=kwargs.pop("in_specs", [whole()] * len(operands)),
        out_specs=jax.tree.map(lambda _: whole(), out_shape),
        compiler_params=pltpu.CompilerParams(vmem_limit_bytes=16 << 20),
        cost_estimate=cost,
        **kwargs,
    )(*operands)


def in_hbm(x):
    return pltpu.with_memory_space_constraint(x, pltpu.HBM)


def swap(x, bits):
    devices = lax.axis_size("seq")
    return lax.ppermute(x, "seq", [(i, i ^ bits) for i in range(devices)])


def stages_of(devices):
    far_bits = []
    while 2 ** (len(far_bits) + 3) < devices:
        far_bits.insert(0, (2 ** (len(far_bits) + 3) | 1,))
    return far_bits + [(3, 5, 7)[: devices // 2 - 1]]


def per_device(
    queries,
    new_keys,
    new_values,
    doc_keys,
    doc_values,
    suffix_keys,
    suffix_values,
    keep_lists,
    suffix_lengths,
):
    devices = lax.axis_size("seq")
    blocks = devices * doc_keys.shape[0] // BLOCK
    flag_rows = 8 * pl.cdiv(blocks, 8 * LANES)
    stages = stages_of(devices)
    packed = on_core(
        pack_kernel,
        VMEM((HEADS + flag_rows, HD), jnp.bfloat16),
        (in_hbm(keep_lists), in_hbm(queries)),
        cost=pl.CostEstimate(flops=10**10, bytes_accessed=10**5, transcendentals=0),
    )
    near = packed[None]
    own = near
    heads_of = lambda x: VMEM((KVH, x.shape[0], HD), x.dtype)
    size = 2 * suffix_keys.size
    pair = swap(own, 1)
    stat = VMEM((KVH, 2 * GROUPS, LANES), jnp.float32)
    *local, dk, dv = on_core(
        suffix_kernel,
        [stat, stat, VMEM((KVH, 2 * GROUPS, HD), jnp.float32)]
        + [heads_of(doc_keys), heads_of(doc_values)],
        (
            near_core(suffix_lengths[None]),
            own,
            near_core(pair),
            suffix_keys,
            suffix_values,
            new_keys,
            new_values,
            doc_keys,
            doc_values,
        ),
        cost=pl.CostEstimate(flops=10**9, bytes_accessed=3 * size, transcendentals=10**6),
    )
    for step, stage in enumerate(stages):
        arrived = []
        for bits in stage:
            arrived.append(swap(near, bits))
        near = jnp.concatenate([near] + arrived, axis=0)
    far = swap(near, 1)
    tokens = lambda count: VMEM((count, HEADS + GROUPS, HD), jnp.bfloat16)
    near, far = near_core(near), near_core(far)
    half = tokens(devices // 2)
    cost = pl.CostEstimate(flops=10**9, bytes_accessed=2 * size, transcendentals=10**6)
    span = doc_keys.shape[0]
    caches = (dk, dv, *local)
    sent, bias = on_core(
        functools.partial(attend_kernel, 1, flag_rows),
        [half, VMEM((devices // 2 * GROUPS, span), jnp.float32)],
        (far, near, *caches),
        cost=cost,
    )
    kept = on_core(functools.partial(attend_kernel, 0, 0), half, (near, bias, *caches), cost=cost)
    parts = [kept, sent]
    step = len(stages)
    stages.append((1,))
    while stages:
        stage = stages.pop()
        sources = [parts[0]]
        for bits, part in zip(stage, parts[1:]):
            sources.append(near_core(swap(part, bits)))
        step -= 1
        if stages:
            pieces = len(stages[-1]) + 1
            parts = on_core(
                functools.partial(merge_kernel, len(sources)),
                [tokens(sources[0].shape[0] // pieces)] * pieces,
                sources,
            )
    return on_core(
        functools.partial(finish_kernel, len(sources)),
        jax.ShapeDtypeStruct((1, HEADS * HD), jnp.bfloat16),
        sources,
    )


def solution(mesh):
    split = P(("parts", "seq"), None)
    return jax.shard_map(
        per_device,
        mesh=mesh,
        in_specs=(split,) * 8 + (P("parts"),),
        out_specs=split,
        check_vma=False,
    )
```

```python
import functools
import math

import jax
import jax.numpy as jnp
from jax import lax
from jax.experimental import pallas as pl
from jax.experimental.pallas import tpu as pltpu
from jax.sharding import PartitionSpec as P


HEADS = 64
KVH = 8
HD = 128
BLOCK = 128
GROUPS = HEADS // KVH
LANES = 128
SLOTS = 8

NEG_BIG = -1e30
NEG_SAFE = -5e29
AHEAD = 4
DOC_AHEAD = 2
EXP2_SCALE = HD**-0.5 * math.log2(math.e)

VMEM = pltpu.VMEM


def pack_kernel(list_ref, q_ref, out_ref):
    q = q_ref[...].astype(jnp.float32)
    rows = [q[:, h * HD : (h + 1) * HD] for h in range(HEADS)]
    out_ref[0:HEADS, :] = jnp.concatenate(rows, axis=0).astype(jnp.bfloat16)
    entries = list_ref.shape[1]
    ids = list_ref[...].astype(jnp.float32)
    diagonal = lax.broadcasted_iota(jnp.int32, (entries, entries), 0) == lax.broadcasted_iota(
        jnp.int32, (entries, entries), 1
    )
    column = jnp.sum(jnp.where(diagonal, ids, 0.0), axis=1, keepdims=True)
    lanes = lax.broadcasted_iota(jnp.int32, (entries, LANES), 1).astype(jnp.float32)
    found = [
        jnp.max(jnp.where(column == lanes + float(i * LANES), 1.0, 0.0), axis=0, keepdims=True)
        for i in range(out_ref.shape[0] - HEADS)
    ]
    out_ref[HEADS:, :] = jnp.concatenate(found, axis=0).astype(jnp.bfloat16)


def lane_dot(a, b):
    return lax.dot_general(a, b, (((1,), (1,)), ((), ())), preferred_element_type=jnp.float32)


def partial_softmax(scores):
    top = jnp.max(scores, axis=-1, keepdims=True)
    weights = jnp.exp2((scores - jnp.maximum(top, NEG_SAFE)) * EXP2_SCALE)
    return top, jnp.sum(weights, axis=-1, keepdims=True), weights.astype(jnp.bfloat16)


def suffix_kernel(
    len_ref,
    own_ref,
    pair_ref,
    sk_ref,
    sv_ref,
    nk_ref,
    nv_ref,
    dk_ref,
    dv_ref,
    top_ref,
    total_ref,
    out_ref,
    dk_out_ref,
    dv_out_ref,
):
    me = lax.axis_index("seq")
    parity = lax.rem(me, 2)
    mine = lax.broadcasted_iota(jnp.int32, len_ref.shape, 1) == lax.div(me, 2)
    length = jnp.sum(
        jnp.where(mine, len_ref[...].astype(jnp.float32), 0.0), axis=1, keepdims=True
    )
    live_left = length.astype(jnp.int32) - parity * sv_ref.shape[0]

    def scores_of(head):
        rows = slice(head * GROUPS, (head + 1) * GROUPS)
        cols = slice(head * HD, (head + 1) * HD)
        q = jnp.concatenate(
            [ref[0, rows, :].astype(jnp.float32) for ref in (own_ref, pair_ref)], axis=0
        )
        scores = lane_dot(q.astype(jnp.bfloat16), sk_ref[:, cols])
        position = lax.broadcasted_iota(jnp.int32, scores.shape, 1)
        scores = jnp.where(position < live_left, scores, NEG_BIG)
        n_top = jnp.sum(q * nk_ref[:, cols].astype(jnp.float32), axis=-1, keepdims=True)
        hidden = (lax.broadcasted_iota(jnp.int32, n_top.shape, 0) >= GROUPS) & (parity == 1)
        return scores, jnp.where(hidden, NEG_BIG, n_top)

    ready = [scores_of(head) for head in range(AHEAD)]
    for head in range(KVH):
        cols = slice(head * HD, (head + 1) * HD)
        scores, n_top = ready.pop(0)
        if head + AHEAD < KVH:
            ready.append(scores_of(head + AHEAD))
        top = jnp.maximum(jnp.max(scores, axis=-1, keepdims=True), n_top)
        base = jnp.maximum(top, NEG_SAFE)
        weights = jnp.exp2((scores - base) * EXP2_SCALE)
        n_scale = jnp.exp2((n_top - base) * EXP2_SCALE)
        total = jnp.sum(weights, axis=-1, keepdims=True) + n_scale
        out = jnp.dot(
            weights.astype(jnp.bfloat16), sv_ref[:, cols], preferred_element_type=jnp.float32
        )
        top_ref[head] = jnp.broadcast_to(top, (2 * GROUPS, LANES))
        total_ref[head] = jnp.broadcast_to(total, (2 * GROUPS, LANES))
        out_ref[head] = out + n_scale * nv_ref[:, cols].astype(jnp.float32)
        dk_out_ref[head] = dk_ref[:, cols]
        dv_out_ref[head] = dv_ref[:, cols]


def split_stats(stats, axis):
    high = stats.astype(jnp.bfloat16).astype(jnp.float32)
    rest = stats - high
    middle = rest.astype(jnp.bfloat16).astype(jnp.float32)
    low = rest - middle
    packed = high + pltpu.roll(middle, 2 * KVH, axis) + pltpu.roll(low, 4 * KVH, axis)
    return packed.astype(jnp.bfloat16)


def join_stats(packed, axis):
    packed = packed.astype(jnp.float32)
    shifted = lambda by: pltpu.roll(packed, LANES - by * KVH, axis)
    live = lax.broadcasted_iota(jnp.int32, packed.shape, axis) < KVH
    top = jnp.where(live, packed + shifted(2) + shifted(4), 0.0)
    total = jnp.where(live, shifted(1) + shifted(3) + shifted(5), 0.0)
    return top, total


def head_queries(ref, slots, head):
    q = ref[slots, head * GROUPS : (head + 1) * GROUPS, :].astype(jnp.float32)
    return q.reshape(SLOTS * GROUPS, HD).astype(jnp.bfloat16)


def score_kernel(token_ref, dk_ref, score_ref, peak_ref):
    rows_here = SLOTS * GROUPS
    lane_ids = lax.broadcasted_iota(jnp.int32, (rows_here, LANES), 1)
    for head in range(KVH):
        scores = lane_dot(head_queries(token_ref, pl.ds(0, SLOTS), head), dk_ref[head])
        score_ref[head] = scores
        peaks = jnp.full((rows_here, LANES), NEG_BIG, jnp.float32)
        for b in range(scores.shape[1] // BLOCK):
            block = scores[:, b * BLOCK : (b + 1) * BLOCK]
            peaks = jnp.where(lane_ids == b, jnp.max(block, axis=-1, keepdims=True), peaks)
        peak_ref[head] = peaks


def attend_kernel(which, flag_rows, scored, *refs):
    if flag_rows:
        token_ref, other_ref, *refs = refs
    elif scored:
        token_ref, score_ref, peak_ref, bias_ref, mark_ref, *refs = refs
    else:
        token_ref, bias_ref, mark_ref, *refs = refs
    dk_ref, dv_ref, top_ref, total_ref, extra_ref, out_ref, *refs = refs
    if flag_rows:
        bias_ref, mark_ref = refs
    tokens = token_ref.shape[0]
    span = dk_ref.shape[1]
    blocks_here = span // BLOCK
    rows_here = SLOTS * GROUPS
    first_block = lax.axis_index("seq") * blocks_here
    flag_row = lax.div(first_block, LANES)
    flag_lane = lax.rem(first_block, LANES)
    lane_ids = lax.broadcasted_iota(jnp.int32, (rows_here, LANES), 1)
    own = slice(which * GROUPS, (which + 1) * GROUPS)

    def do_chunk(chunk, local):
        slots = pl.ds(chunk * SLOTS, SLOTS)
        here = pl.ds(chunk * rows_here, rows_here)
        if flag_rows:
            flags = token_ref[slots, HEADS:, :].astype(jnp.float32) + other_ref[
                slots, HEADS:, :
            ].astype(jnp.float32)
            row_ids = lax.broadcasted_iota(jnp.int32, (1, flag_rows, LANES), 1)
            flags = jnp.sum(jnp.where(row_ids == flag_row, flags, 0.0), axis=1)
            flags = pltpu.roll(flags, LANES - flag_lane, 1)
            bias = jnp.where(flags > 0.5, 0.0, NEG_BIG)
            mark_ref[here, :] = jnp.broadcast_to(
                bias[:, None, :], (SLOTS, GROUPS, LANES)
            ).reshape(rows_here, LANES)
            for b in range(blocks_here):
                wide = jnp.broadcast_to(bias[:, b : b + 1], (SLOTS, BLOCK))
                bias_ref[here, b * BLOCK : (b + 1) * BLOCK] = jnp.broadcast_to(
                    wide[:, None, :], (SLOTS, GROUPS, BLOCK)
                ).reshape(rows_here, BLOCK)

        def scores_of(head):
            if scored:
                return None
            q = head_queries(token_ref, slots, head)
            return lane_dot(q, dk_ref[head]) + bias_ref[here, :]

        def softmax_of(head, scores):
            if not scored:
                return partial_softmax(scores)
            top = jnp.max(peak_ref[head] + mark_ref[here, :], axis=-1, keepdims=True)
            shifted = score_ref[head] + bias_ref[here, :] - jnp.maximum(top, NEG_SAFE)
            weights = jnp.exp2(shifted * EXP2_SCALE)
            return top, jnp.sum(weights, axis=-1, keepdims=True), weights.astype(jnp.bfloat16)

        stats = jnp.zeros((rows_here, LANES), jnp.float32)
        ready = [scores_of(head) for head in range(DOC_AHEAD)]
        for head in range(KVH):
            rows = slice(head * GROUPS, (head + 1) * GROUPS)
            scores = ready.pop(0)
            if head + DOC_AHEAD < KVH:
                ready.append(scores_of(head + DOC_AHEAD))
            top, total, weights = softmax_of(head, scores)
            out = jnp.dot(weights, dv_ref[head], preferred_element_type=jnp.float32)
            if local:
                x_top, y_top = top[:GROUPS], top_ref[head, own, 0:1]
                new_top = jnp.maximum(x_top, y_top)
                base = jnp.maximum(new_top, NEG_SAFE)
                x_scale = jnp.exp2((x_top - base) * EXP2_SCALE)
                y_scale = jnp.exp2((y_top - base) * EXP2_SCALE)
                new_total = x_scale * total[:GROUPS] + y_scale * total_ref[head, own, 0:1]
                new_out = x_scale * out[:GROUPS] + y_scale * extra_ref[head, own, :]
                top = jnp.concatenate([new_top, top[GROUPS:]], axis=0)
                total = jnp.concatenate([new_total, total[GROUPS:]], axis=0)
                out = jnp.concatenate([new_out, out[GROUPS:]], axis=0)
            units = (out / jnp.maximum(total, 1.0)).astype(jnp.bfloat16)
            stats = jnp.where(lane_ids == head, top * EXP2_SCALE, stats)
            stats = jnp.where(lane_ids == KVH + head, total, stats)
            out_ref[slots, rows, :] = units.reshape(SLOTS, GROUPS, HD)
        rows = slice(HEADS, HEADS + GROUPS)
        out_ref[slots, rows, :] = split_stats(stats, 1).reshape(SLOTS, GROUPS, LANES)

    do_chunk(0, True)
    chunks = tokens // SLOTS
    if chunks > 1:
        lax.fori_loop(1, chunks, lambda c, _: do_chunk(c, False), None)


def mix_weights(refs):
    rows = slice(HEADS, HEADS + GROUPS)
    stats = [join_stats(ref[:, rows, :], 2) for ref in refs]
    top = functools.reduce(jnp.maximum, [t for t, _ in stats])
    weights = [jnp.exp2(t - top) * total for t, total in stats]
    total = functools.reduce(jnp.add, weights)
    scale = 1.0 / jnp.maximum(total, 1.0)
    return top, total, [w * scale for w in weights[1:]]


def mixed_units(head, refs, weights):
    rows = slice(head * GROUPS, (head + 1) * GROUPS)
    first, *others = [ref[:, rows, :].astype(jnp.float32) for ref in refs]
    steps = [(u - first) * w[:, :, head : head + 1] for u, w in zip(others, weights)]
    return functools.reduce(jnp.add, steps, first)


def merge_kernel(count, *refs):
    sources, targets = refs[:count], refs[count:]
    top, total, weights = mix_weights(sources)
    size = targets[0].shape[0]
    for head in range(KVH):
        rows = slice(head * GROUPS, (head + 1) * GROUPS)
        units = mixed_units(head, sources, weights).astype(jnp.bfloat16)
        for i, target in enumerate(targets):
            target[:, rows, :] = units[i * size : (i + 1) * size]
    packed = split_stats(top + pltpu.roll(total, KVH, 2), 2)
    for i, target in enumerate(targets):
        target[:, HEADS : HEADS + GROUPS, :] = packed[i * size : (i + 1) * size]


def finish_kernel(count, *refs):
    sources, out_ref = refs[:count], refs[count]
    _, _, weights = mix_weights(sources)
    for head in range(KVH):
        units = mixed_units(head, sources, weights)[0]
        for g in range(GROUPS):
            h = head * GROUPS + g
            out_ref[:, h * HD : (h + 1) * HD] = units[g : g + 1, :].astype(jnp.bfloat16)


def whole(space=VMEM):
    return pl.BlockSpec(memory_space=space)


def near_core(x):
    return pltpu.with_memory_space_constraint(x, VMEM)


def on_core(kernel, out_shape, operands, cost=None, **kwargs):
    return pl.pallas_call(
        kernel,
        out_shape=out_shape,
        in_specs=kwargs.pop("in_specs", [whole()] * len(operands)),
        out_specs=jax.tree.map(lambda _: whole(), out_shape),
        compiler_params=pltpu.CompilerParams(vmem_limit_bytes=16 << 20),
        cost_estimate=cost,
        **kwargs,
    )(*operands)


def in_hbm(x):
    return pltpu.with_memory_space_constraint(x, pltpu.HBM)


def swap(x, bits):
    devices = lax.axis_size("seq")
    return lax.ppermute(x, "seq", [(i, i ^ bits) for i in range(devices)])


def stages_of(devices):
    far_bits = []
    while 2 ** (len(far_bits) + 3) < devices:
        far_bits.insert(0, (2 ** (len(far_bits) + 3) | 1,))
    return far_bits + [(3, 5, 7)[: devices // 2 - 1]]


def per_device(
    queries,
    new_keys,
    new_values,
    doc_keys,
    doc_values,
    suffix_keys,
    suffix_values,
    keep_lists,
    suffix_lengths,
):
    devices = lax.axis_size("seq")
    blocks = devices * doc_keys.shape[0] // BLOCK
    flag_rows = 8 * pl.cdiv(blocks, 8 * LANES)
    stages = stages_of(devices)
    packed = on_core(
        pack_kernel,
        VMEM((HEADS + flag_rows, HD), jnp.bfloat16),
        (in_hbm(keep_lists), in_hbm(queries)),
        cost=pl.CostEstimate(flops=10**10, bytes_accessed=10**5, transcendentals=0),
    )
    near = packed[None]
    own = near
    heads_of = lambda x: VMEM((KVH, x.shape[0], HD), x.dtype)
    size = 2 * suffix_keys.size
    pair = swap(own, 1)
    stat = VMEM((KVH, 2 * GROUPS, LANES), jnp.float32)
    *local, dk, dv = on_core(
        suffix_kernel,
        [stat, stat, VMEM((KVH, 2 * GROUPS, HD), jnp.float32)]
        + [heads_of(doc_keys), heads_of(doc_values)],
        (
            near_core(suffix_lengths[None]),
            own,
            near_core(pair),
            suffix_keys,
            suffix_values,
            new_keys,
            new_values,
            doc_keys,
            doc_values,
        ),
        cost=pl.CostEstimate(flops=10**9, bytes_accessed=3 * size, transcendentals=10**6),
    )
    for step, stage in enumerate(stages):
        arrived = []
        for bits in stage:
            arrived.append(swap(near, bits))
        near = jnp.concatenate([near] + arrived, axis=0)
    far = swap(near, 1)
    tokens = lambda count: VMEM((count, HEADS + GROUPS, HD), jnp.bfloat16)
    near, far = near_core(near), near_core(far)
    half = tokens(devices // 2)
    cost = pl.CostEstimate(flops=10**9, bytes_accessed=2 * size, transcendentals=10**6)
    span = doc_keys.shape[0]
    caches = (dk, dv, *local)
    rows = devices // 2 * GROUPS
    near_operands = (near,)
    scored = devices // 2 == SLOTS
    if scored:
        near_operands += on_core(
            score_kernel,
            (
                VMEM((KVH, rows, span), jnp.float32),
                VMEM((KVH, rows, LANES), jnp.float32),
            ),
            (near, dk),
            cost=cost,
        )
    sent, bias, mark = on_core(
        functools.partial(attend_kernel, 1, flag_rows, False),
        [half, VMEM((rows, span), jnp.float32), VMEM((rows, LANES), jnp.float32)],
        (far, near, *caches),
        cost=cost,
    )
    kept = on_core(
        functools.partial(attend_kernel, 0, 0, scored),
        half,
        (*near_operands, bias, mark, *caches),
        cost=cost,
    )
    parts = [kept, sent]
    step = len(stages)
    stages.append((1,))
    while stages:
        stage = stages.pop()
        sources = [parts[0]]
        for bits, part in zip(stage, parts[1:]):
            sources.append(near_core(swap(part, bits)))
        step -= 1
        if stages:
            pieces = len(stages[-1]) + 1
            parts = on_core(
                functools.partial(merge_kernel, len(sources)),
                [tokens(sources[0].shape[0] // pieces)] * pieces,
                sources,
            )
    return on_core(
        functools.partial(finish_kernel, len(sources)),
        jax.ShapeDtypeStruct((1, HEADS * HD), jnp.bfloat16),
        sources,
    )


def solution(mesh):
    split = P(("parts", "seq"), None)
    return jax.shard_map(
        per_device,
        mesh=mesh,
        in_specs=(split,) * 8 + (P("parts"),),
        out_specs=split,
        check_vma=False,
    )
```

```python
import functools
import math

import jax
import jax.numpy as jnp
from jax import lax
from jax.experimental import pallas as pl
from jax.experimental.pallas import tpu as pltpu
from jax.sharding import PartitionSpec as P


HEADS = 64
KVH = 8
HD = 128
BLOCK = 128
GROUPS = HEADS // KVH
LANES = 128
SLOTS = 8

NEG_BIG = -1e30
NEG_SAFE = -5e29
AHEAD = 4
DOC_AHEAD = 3
EXP2_SCALE = HD**-0.5 * math.log2(math.e)

VMEM = pltpu.VMEM


def pack_kernel(list_ref, q_ref, out_ref):
    q = q_ref[...].astype(jnp.float32)
    rows = [q[:, h * HD : (h + 1) * HD] for h in range(HEADS)]
    out_ref[0:HEADS, :] = jnp.concatenate(rows, axis=0).astype(jnp.bfloat16)
    entries = list_ref.shape[1]
    ids = list_ref[...].astype(jnp.float32)
    diagonal = lax.broadcasted_iota(jnp.int32, (entries, entries), 0) == lax.broadcasted_iota(
        jnp.int32, (entries, entries), 1
    )
    column = jnp.sum(jnp.where(diagonal, ids, 0.0), axis=1, keepdims=True)
    lanes = lax.broadcasted_iota(jnp.int32, (entries, LANES), 1).astype(jnp.float32)
    found = [
        jnp.max(jnp.where(column == lanes + float(i * LANES), 1.0, 0.0), axis=0, keepdims=True)
        for i in range(out_ref.shape[0] - HEADS)
    ]
    out_ref[HEADS:, :] = jnp.concatenate(found, axis=0).astype(jnp.bfloat16)


def lane_dot(a, b):
    return lax.dot_general(a, b, (((1,), (1,)), ((), ())), preferred_element_type=jnp.float32)


def suffix_kernel(
    len_ref,
    own_ref,
    pair_ref,
    sk_ref,
    sv_ref,
    nk_ref,
    nv_ref,
    dk_ref,
    dv_ref,
    top_ref,
    total_ref,
    out_ref,
    dk_out_ref,
    dv_out_ref,
):
    me = lax.axis_index("seq")
    parity = lax.rem(me, 2)
    mine = lax.broadcasted_iota(jnp.int32, len_ref.shape, 1) == lax.div(me, 2)
    length = jnp.sum(
        jnp.where(mine, len_ref[...].astype(jnp.float32), 0.0), axis=1, keepdims=True
    )
    live_left = length.astype(jnp.int32) - parity * sv_ref.shape[0]

    def scores_of(head):
        rows = slice(head * GROUPS, (head + 1) * GROUPS)
        cols = slice(head * HD, (head + 1) * HD)
        q = jnp.concatenate(
            [ref[0, rows, :].astype(jnp.float32) for ref in (own_ref, pair_ref)], axis=0
        )
        scores = lane_dot(q.astype(jnp.bfloat16), sk_ref[:, cols])
        position = lax.broadcasted_iota(jnp.int32, scores.shape, 1)
        scores = jnp.where(position < live_left, scores, NEG_BIG)
        n_top = jnp.sum(q * nk_ref[:, cols].astype(jnp.float32), axis=-1, keepdims=True)
        hidden = (lax.broadcasted_iota(jnp.int32, n_top.shape, 0) >= GROUPS) & (parity == 1)
        return scores, jnp.where(hidden, NEG_BIG, n_top)

    ready = [scores_of(head) for head in range(AHEAD)]
    for head in range(KVH):
        cols = slice(head * HD, (head + 1) * HD)
        scores, n_top = ready.pop(0)
        if head + AHEAD < KVH:
            ready.append(scores_of(head + AHEAD))
        top = jnp.maximum(jnp.max(scores, axis=-1, keepdims=True), n_top)
        base = jnp.maximum(top, NEG_SAFE)
        weights = jnp.exp2((scores - base) * EXP2_SCALE)
        n_scale = jnp.exp2((n_top - base) * EXP2_SCALE)
        total = jnp.sum(weights, axis=-1, keepdims=True) + n_scale
        out = jnp.dot(
            weights.astype(jnp.bfloat16), sv_ref[:, cols], preferred_element_type=jnp.float32
        )
        top_ref[head] = jnp.broadcast_to(top, (2 * GROUPS, LANES))
        total_ref[head] = jnp.broadcast_to(total, (2 * GROUPS, LANES))
        out_ref[head] = out + n_scale * nv_ref[:, cols].astype(jnp.float32)
        dk_out_ref[head] = dk_ref[:, cols]
        dv_out_ref[head] = dv_ref[:, cols]


def split_stats(stats, axis):
    high = stats.astype(jnp.bfloat16).astype(jnp.float32)
    rest = stats - high
    middle = rest.astype(jnp.bfloat16).astype(jnp.float32)
    low = rest - middle
    packed = high + pltpu.roll(middle, 2 * KVH, axis) + pltpu.roll(low, 4 * KVH, axis)
    return packed.astype(jnp.bfloat16)


def join_stats(packed, axis):
    packed = packed.astype(jnp.float32)
    shifted = lambda by: pltpu.roll(packed, LANES - by * KVH, axis)
    live = lax.broadcasted_iota(jnp.int32, packed.shape, axis) < KVH
    top = jnp.where(live, packed + shifted(2) + shifted(4), 0.0)
    total = jnp.where(live, shifted(1) + shifted(3) + shifted(5), 0.0)
    return top, total


def head_queries(ref, slots, head):
    q = ref[slots, head * GROUPS : (head + 1) * GROUPS, :].astype(jnp.float32)
    return q.reshape(SLOTS * GROUPS, HD).astype(jnp.bfloat16)


def score_kernel(token_ref, dk_ref, score_ref, peak_ref):
    rows_here = SLOTS * GROUPS
    lane_ids = lax.broadcasted_iota(jnp.int32, (rows_here, LANES), 1)
    for head in range(KVH):
        scores = lane_dot(head_queries(token_ref, pl.ds(0, SLOTS), head), dk_ref[head])
        score_ref[head] = scores
        peaks = jnp.full((rows_here, LANES), NEG_BIG, jnp.float32)
        for b in range(scores.shape[1] // BLOCK):
            block = scores[:, b * BLOCK : (b + 1) * BLOCK]
            peaks = jnp.where(lane_ids == b, jnp.max(block, axis=-1, keepdims=True), peaks)
        peak_ref[head] = peaks


def attend_kernel(which, flag_rows, scored, *refs):
    if flag_rows:
        token_ref, other_ref, *refs = refs
    elif scored:
        token_ref, score_ref, peak_ref, bias_ref, mark_ref, *refs = refs
    else:
        token_ref, bias_ref, mark_ref, *refs = refs
    dk_ref, dv_ref, top_ref, total_ref, extra_ref, out_ref, *refs = refs
    if flag_rows:
        bias_ref, mark_ref = refs
    tokens = token_ref.shape[0]
    span = dk_ref.shape[1]
    blocks_here = span // BLOCK
    rows_here = SLOTS * GROUPS
    first_block = lax.axis_index("seq") * blocks_here
    flag_row = lax.div(first_block, LANES)
    flag_lane = lax.rem(first_block, LANES)
    lane_ids = lax.broadcasted_iota(jnp.int32, (rows_here, LANES), 1)
    own = slice(which * GROUPS, (which + 1) * GROUPS)

    def do_chunk(chunk, local):
        slots = pl.ds(chunk * SLOTS, SLOTS)
        here = pl.ds(chunk * rows_here, rows_here)
        if flag_rows:
            flags = token_ref[slots, HEADS:, :].astype(jnp.float32) + other_ref[
                slots, HEADS:, :
            ].astype(jnp.float32)
            row_ids = lax.broadcasted_iota(jnp.int32, (1, flag_rows, LANES), 1)
            flags = jnp.sum(jnp.where(row_ids == flag_row, flags, 0.0), axis=1)
            flags = pltpu.roll(flags, LANES - flag_lane, 1)
            bias = jnp.where(flags > 0.5, 0.0, NEG_BIG)
            mark_ref[here, :] = jnp.broadcast_to(
                bias[:, None, :], (SLOTS, GROUPS, LANES)
            ).reshape(rows_here, LANES)
            for b in range(blocks_here):
                wide = jnp.broadcast_to(bias[:, b : b + 1], (SLOTS, BLOCK))
                bias_ref[here, b * BLOCK : (b + 1) * BLOCK] = jnp.broadcast_to(
                    wide[:, None, :], (SLOTS, GROUPS, BLOCK)
                ).reshape(rows_here, BLOCK)

        def scores_of(head):
            if scored:
                return None
            q = head_queries(token_ref, slots, head)
            return lane_dot(q, dk_ref[head]) + bias_ref[here, :]

        def softmax_of(head, scores):
            if scored:
                peaks = peak_ref[head] + mark_ref[here, :]
                scores = score_ref[head] + bias_ref[here, :]
                blocks = [scores[:, b * LANES : (b + 1) * LANES] for b in range(span // LANES)]
            else:
                blocks = [scores[:, b * LANES : (b + 1) * LANES] for b in range(span // LANES)]
                peaks = functools.reduce(jnp.maximum, blocks)
            top = jnp.broadcast_to(jnp.max(peaks, axis=-1, keepdims=True), (rows_here, LANES))
            base = jnp.maximum(top, NEG_SAFE)
            weights = [jnp.exp2((block - base) * EXP2_SCALE) for block in blocks]
            total = jnp.sum(functools.reduce(jnp.add, weights), axis=-1, keepdims=True)
            total = jnp.broadcast_to(total, (rows_here, LANES))
            weights = jnp.concatenate([w.astype(jnp.bfloat16) for w in weights], axis=1)
            return top, total, weights

        stats = jnp.zeros((rows_here, LANES), jnp.float32)
        ready = [scores_of(head) for head in range(DOC_AHEAD)]
        for head in range(KVH):
            rows = slice(head * GROUPS, (head + 1) * GROUPS)
            scores = ready.pop(0)
            if head + DOC_AHEAD < KVH:
                ready.append(scores_of(head + DOC_AHEAD))
            top, total, weights = softmax_of(head, scores)
            out = jnp.dot(weights, dv_ref[head], preferred_element_type=jnp.float32)
            if local:
                x_top, y_top = top[:GROUPS], top_ref[head, own, :]
                new_top = jnp.maximum(x_top, y_top)
                base = jnp.maximum(new_top, NEG_SAFE)
                x_scale = jnp.exp2((x_top - base) * EXP2_SCALE)
                y_scale = jnp.exp2((y_top - base) * EXP2_SCALE)
                new_total = x_scale * total[:GROUPS] + y_scale * total_ref[head, own, :]
                new_out = x_scale * out[:GROUPS] + y_scale * extra_ref[head, own, :]
                top = jnp.concatenate([new_top, top[GROUPS:]], axis=0)
                total = jnp.concatenate([new_total, total[GROUPS:]], axis=0)
                out = jnp.concatenate([new_out, out[GROUPS:]], axis=0)
            units = (out / jnp.maximum(total, 1.0)).astype(jnp.bfloat16)
            stats = jnp.where(lane_ids == head, top * EXP2_SCALE, stats)
            stats = jnp.where(lane_ids == KVH + head, total, stats)
            out_ref[slots, rows, :] = units.reshape(SLOTS, GROUPS, HD)
        rows = slice(HEADS, HEADS + GROUPS)
        out_ref[slots, rows, :] = split_stats(stats, 1).reshape(SLOTS, GROUPS, LANES)

    do_chunk(0, True)
    chunks = tokens // SLOTS
    if chunks > 1:
        lax.fori_loop(1, chunks, lambda c, _: do_chunk(c, False), None)


def mix_weights(refs):
    rows = slice(HEADS, HEADS + GROUPS)
    stats = [join_stats(ref[:, rows, :], 2) for ref in refs]
    top = functools.reduce(jnp.maximum, [t for t, _ in stats])
    weights = [jnp.exp2(t - top) * total for t, total in stats]
    total = functools.reduce(jnp.add, weights)
    scale = 1.0 / jnp.maximum(total, 1.0)
    return top, total, [w * scale for w in weights[1:]]


def mixed_units(head, refs, weights):
    rows = slice(head * GROUPS, (head + 1) * GROUPS)
    first, *others = [ref[:, rows, :].astype(jnp.float32) for ref in refs]
    steps = [(u - first) * w[:, :, head : head + 1] for u, w in zip(others, weights)]
    return functools.reduce(jnp.add, steps, first)


def merge_kernel(count, *refs):
    sources, targets = refs[:count], refs[count:]
    top, total, weights = mix_weights(sources)
    size = targets[0].shape[0]
    for head in range(KVH):
        rows = slice(head * GROUPS, (head + 1) * GROUPS)
        units = mixed_units(head, sources, weights).astype(jnp.bfloat16)
        for i, target in enumerate(targets):
            target[:, rows, :] = units[i * size : (i + 1) * size]
    packed = split_stats(top + pltpu.roll(total, KVH, 2), 2)
    for i, target in enumerate(targets):
        target[:, HEADS : HEADS + GROUPS, :] = packed[i * size : (i + 1) * size]


def finish_kernel(count, *refs):
    sources, out_ref = refs[:count], refs[count]
    _, _, weights = mix_weights(sources)
    for head in range(KVH):
        units = mixed_units(head, sources, weights)[0]
        for g in range(GROUPS):
            h = head * GROUPS + g
            out_ref[:, h * HD : (h + 1) * HD] = units[g : g + 1, :].astype(jnp.bfloat16)


def whole(space=VMEM):
    return pl.BlockSpec(memory_space=space)


def near_core(x):
    return pltpu.with_memory_space_constraint(x, VMEM)


def on_core(kernel, out_shape, operands, cost=None, **kwargs):
    return pl.pallas_call(
        kernel,
        out_shape=out_shape,
        in_specs=kwargs.pop("in_specs", [whole()] * len(operands)),
        out_specs=jax.tree.map(lambda _: whole(), out_shape),
        compiler_params=pltpu.CompilerParams(vmem_limit_bytes=16 << 20),
        cost_estimate=cost,
        **kwargs,
    )(*operands)


def in_hbm(x):
    return pltpu.with_memory_space_constraint(x, pltpu.HBM)


def swap(x, bits):
    devices = lax.axis_size("seq")
    return lax.ppermute(x, "seq", [(i, i ^ bits) for i in range(devices)])


def stages_of(devices):
    far_bits = []
    while 2 ** (len(far_bits) + 3) < devices:
        far_bits.insert(0, (2 ** (len(far_bits) + 3) | 1,))
    return far_bits + [(3, 5, 7)[: devices // 2 - 1]]


def per_device(
    queries,
    new_keys,
    new_values,
    doc_keys,
    doc_values,
    suffix_keys,
    suffix_values,
    keep_lists,
    suffix_lengths,
):
    devices = lax.axis_size("seq")
    blocks = devices * doc_keys.shape[0] // BLOCK
    flag_rows = 8 * pl.cdiv(blocks, 8 * LANES)
    stages = stages_of(devices)
    packed = on_core(
        pack_kernel,
        VMEM((HEADS + flag_rows, HD), jnp.bfloat16),
        (in_hbm(keep_lists), in_hbm(queries)),
        cost=pl.CostEstimate(flops=10**10, bytes_accessed=10**5, transcendentals=0),
    )
    near = packed[None]
    own = near
    heads_of = lambda x: VMEM((KVH, x.shape[0], HD), x.dtype)
    size = 2 * suffix_keys.size
    pair = swap(own, 1)
    stat = VMEM((KVH, 2 * GROUPS, LANES), jnp.float32)
    *local, dk, dv = on_core(
        suffix_kernel,
        [stat, stat, VMEM((KVH, 2 * GROUPS, HD), jnp.float32)]
        + [heads_of(doc_keys), heads_of(doc_values)],
        (
            near_core(suffix_lengths[None]),
            own,
            near_core(pair),
            suffix_keys,
            suffix_values,
            new_keys,
            new_values,
            doc_keys,
            doc_values,
        ),
        cost=pl.CostEstimate(flops=10**9, bytes_accessed=3 * size, transcendentals=10**6),
    )
    for step, stage in enumerate(stages):
        arrived = []
        for bits in stage:
            arrived.append(swap(near, bits))
        near = jnp.concatenate([near] + arrived, axis=0)
    far = swap(near, 1)
    tokens = lambda count: VMEM((count, HEADS + GROUPS, HD), jnp.bfloat16)
    near, far = near_core(near), near_core(far)
    half = tokens(devices // 2)
    cost = pl.CostEstimate(flops=10**9, bytes_accessed=2 * size, transcendentals=10**6)
    span = doc_keys.shape[0]
    caches = (dk, dv, *local)
    rows = devices // 2 * GROUPS
    near_operands = (near,)
    scored = devices // 2 == SLOTS
    if scored:
        near_operands += on_core(
            score_kernel,
            (
                VMEM((KVH, rows, span), jnp.float32),
                VMEM((KVH, rows, LANES), jnp.float32),
            ),
            (near, dk),
            cost=cost,
        )
    sent, bias, mark = on_core(
        functools.partial(attend_kernel, 1, flag_rows, False),
        [half, VMEM((rows, span), jnp.float32), VMEM((rows, LANES), jnp.float32)],
        (far, near, *caches),
        cost=cost,
    )
    kept = on_core(
        functools.partial(attend_kernel, 0, 0, scored),
        half,
        (*near_operands, bias, mark, *caches),
        cost=cost,
    )
    parts = [kept, sent]
    step = len(stages)
    stages.append((1,))
    while stages:
        stage = stages.pop()
        sources = [parts[0]]
        for bits, part in zip(stage, parts[1:]):
            sources.append(near_core(swap(part, bits)))
        step -= 1
        if stages:
            pieces = len(stages[-1]) + 1
            parts = on_core(
                functools.partial(merge_kernel, len(sources)),
                [tokens(sources[0].shape[0] // pieces)] * pieces,
                sources,
            )
    return on_core(
        functools.partial(finish_kernel, len(sources)),
        jax.ShapeDtypeStruct((1, HEADS * HD), jnp.bfloat16),
        sources,
    )


def solution(mesh):
    split = P(("parts", "seq"), None)
    return jax.shard_map(
        per_device,
        mesh=mesh,
        in_specs=(split,) * 8 + (P("parts"),),
        out_specs=split,
        check_vma=False,
    )
```

```python
import functools
import math

import jax
import jax.numpy as jnp
from jax import lax
from jax.experimental import pallas as pl
from jax.experimental.pallas import tpu as pltpu
from jax.sharding import PartitionSpec as P


HEADS = 64
KVH = 8
HD = 128
BLOCK = 128
GROUPS = HEADS // KVH
LANES = 128
SLOTS = 8

NEG_BIG = -1e30
NEG_SAFE = -5e29
AHEAD = 4
DOC_AHEAD = 3
EXP2_SCALE = HD**-0.5 * math.log2(math.e)

VMEM = pltpu.VMEM


def pack_kernel(list_ref, q_ref, out_ref):
    q = q_ref[...].astype(jnp.float32)
    rows = [q[:, h * HD : (h + 1) * HD] for h in range(HEADS)]
    out_ref[0:HEADS, :] = jnp.concatenate(rows, axis=0).astype(jnp.bfloat16)
    entries = list_ref.shape[1]
    ids = list_ref[...].astype(jnp.float32)
    diagonal = lax.broadcasted_iota(jnp.int32, (entries, entries), 0) == lax.broadcasted_iota(
        jnp.int32, (entries, entries), 1
    )
    column = jnp.sum(jnp.where(diagonal, ids, 0.0), axis=1, keepdims=True)
    lanes = lax.broadcasted_iota(jnp.int32, (entries, LANES), 1).astype(jnp.float32)
    found = [
        jnp.max(jnp.where(column == lanes + float(i * LANES), 1.0, 0.0), axis=0, keepdims=True)
        for i in range(out_ref.shape[0] - HEADS)
    ]
    out_ref[HEADS:, :] = jnp.concatenate(found, axis=0).astype(jnp.bfloat16)


def lane_dot(a, b):
    return lax.dot_general(a, b, (((1,), (1,)), ((), ())), preferred_element_type=jnp.float32)


def suffix_kernel(
    len_ref,
    own_ref,
    pair_ref,
    sk_ref,
    sv_ref,
    nk_ref,
    nv_ref,
    dk_ref,
    dv_ref,
    own_out_ref,
    pair_out_ref,
    dk_out_ref,
    dv_out_ref,
):
    me = lax.axis_index("seq")
    parity = lax.rem(me, 2)
    mine = lax.broadcasted_iota(jnp.int32, len_ref.shape, 1) == lax.div(me, 2)
    length = jnp.sum(
        jnp.where(mine, len_ref[...].astype(jnp.float32), 0.0), axis=1, keepdims=True
    )
    live_left = length.astype(jnp.int32) - parity * sv_ref.shape[0]

    def scores_of(head):
        rows = slice(head * GROUPS, (head + 1) * GROUPS)
        cols = slice(head * HD, (head + 1) * HD)
        q = jnp.concatenate(
            [ref[0, rows, :].astype(jnp.float32) for ref in (own_ref, pair_ref)], axis=0
        )
        scores = lane_dot(q.astype(jnp.bfloat16), sk_ref[:, cols])
        position = lax.broadcasted_iota(jnp.int32, scores.shape, 1)
        scores = jnp.where(position < live_left, scores, NEG_BIG)
        n_top = jnp.sum(q * nk_ref[:, cols].astype(jnp.float32), axis=-1, keepdims=True)
        hidden = (lax.broadcasted_iota(jnp.int32, n_top.shape, 0) >= GROUPS) & (parity == 1)
        return scores, jnp.where(hidden, NEG_BIG, n_top)

    ready = [scores_of(head) for head in range(AHEAD)]
    for head in range(KVH):
        cols = slice(head * HD, (head + 1) * HD)
        scores, n_top = ready.pop(0)
        if head + AHEAD < KVH:
            ready.append(scores_of(head + AHEAD))
        top = jnp.maximum(jnp.max(scores, axis=-1, keepdims=True), n_top)
        base = jnp.maximum(top, NEG_SAFE)
        weights = jnp.exp2((scores - base) * EXP2_SCALE)
        n_scale = jnp.exp2((n_top - base) * EXP2_SCALE)
        total = jnp.sum(weights, axis=-1, keepdims=True) + n_scale
        out = jnp.dot(
            weights.astype(jnp.bfloat16), sv_ref[:, cols], preferred_element_type=jnp.float32
        )
        out = out + n_scale * nv_ref[:, cols].astype(jnp.float32)
        for i, target in enumerate((own_out_ref, pair_out_ref)):
            mine = slice(i * GROUPS, (i + 1) * GROUPS)
            target[head, 0:GROUPS] = jnp.broadcast_to(top[mine], (GROUPS, LANES))
            target[head, GROUPS : 2 * GROUPS] = jnp.broadcast_to(total[mine], (GROUPS, LANES))
            target[head, 2 * GROUPS :] = out[mine]
        dk_out_ref[head] = dk_ref[:, cols]
        dv_out_ref[head] = dv_ref[:, cols]


def split_stats(stats, axis):
    high = stats.astype(jnp.bfloat16).astype(jnp.float32)
    rest = stats - high
    middle = rest.astype(jnp.bfloat16).astype(jnp.float32)
    low = rest - middle
    packed = high + pltpu.roll(middle, 2 * KVH, axis) + pltpu.roll(low, 4 * KVH, axis)
    return packed.astype(jnp.bfloat16)


def join_stats(packed, axis):
    packed = packed.astype(jnp.float32)
    shifted = lambda by: pltpu.roll(packed, LANES - by * KVH, axis)
    live = lax.broadcasted_iota(jnp.int32, packed.shape, axis) < KVH
    top = jnp.where(live, packed + shifted(2) + shifted(4), 0.0)
    total = jnp.where(live, shifted(1) + shifted(3) + shifted(5), 0.0)
    return top, total


def head_queries(ref, slots, head):
    q = ref[slots, head * GROUPS : (head + 1) * GROUPS, :].astype(jnp.float32)
    return q.reshape(SLOTS * GROUPS, HD).astype(jnp.bfloat16)


def score_kernel(token_ref, dk_ref, score_ref, peak_ref):
    rows_here = SLOTS * GROUPS
    lane_ids = lax.broadcasted_iota(jnp.int32, (rows_here, LANES), 1)
    for head in range(KVH):
        scores = lane_dot(head_queries(token_ref, pl.ds(0, SLOTS), head), dk_ref[head])
        score_ref[head] = scores
        peaks = jnp.full((rows_here, LANES), NEG_BIG, jnp.float32)
        for b in range(scores.shape[1] // BLOCK):
            block = scores[:, b * BLOCK : (b + 1) * BLOCK]
            peaks = jnp.where(lane_ids == b, jnp.max(block, axis=-1, keepdims=True), peaks)
        peak_ref[head] = peaks


def attend_kernel(flag_rows, scored, pieces, *refs):
    near_ref, other_ref, *refs = refs
    if scored:
        score_ref, peak_ref, *refs = refs
    dk_ref, dv_ref, far_dk_ref, far_dv_ref, own_ref, theirs_ref, *refs = refs
    out_refs, (bias_ref,) = refs[:pieces], refs[pieces:]
    span = far_dk_ref.shape[0]
    blocks_here = span // BLOCK
    rows_here = SLOTS * GROUPS
    me = lax.axis_index("seq")
    flag_row = lax.div(me * blocks_here, LANES)
    row_ids = lax.broadcasted_iota(jnp.int32, (1, flag_rows, LANES), 1)
    lane_ids = lax.broadcasted_iota(jnp.int32, (rows_here, LANES), 1)

    def tall(x):
        wide = jnp.broadcast_to(x[:, None, :], (SLOTS, GROUPS, LANES))
        return wide.reshape(rows_here, LANES)

    def do_chunk(chunk, local, put):
        slots = pl.ds(chunk * SLOTS, SLOTS)
        flags = near_ref[slots, HEADS:, :].astype(jnp.float32)
        flags = flags + other_ref[slots].astype(jnp.float32)
        flags = jnp.sum(jnp.where(row_ids == flag_row, flags, 0.0), axis=1)
        marks = []
        for i, device in enumerate((me, me ^ 1)):
            lane = lax.rem(device * blocks_here, LANES)
            bias = jnp.where(pltpu.roll(flags, LANES - lane, 1) > 0.5, 0.0, NEG_BIG)
            marks.append(bias)
            for b in range(blocks_here):
                wide = jnp.broadcast_to(bias[:, b : b + 1], (SLOTS, LANES))
                at = i * span + b * BLOCK
                bias_ref[:, at : at + BLOCK] = tall(wide)
        mark = tall(marks[0])

        def blocks_of(scores):
            return [scores[:, b * LANES : (b + 1) * LANES] for b in range(span // LANES)]

        def scores_of(head):
            q = head_queries(near_ref, slots, head)
            cols = slice(head * HD, (head + 1) * HD)
            far = lane_dot(q, far_dk_ref[:, cols]) + bias_ref[:, span:]
            if scored:
                return blocks_of(far)
            return blocks_of(far), blocks_of(lane_dot(q, dk_ref[head]) + bias_ref[:, :span])

        def softmax_of(head, scores):
            if scored:
                far = scores
                near = blocks_of(score_ref[head] + bias_ref[:, :span])
                peaks = functools.reduce(jnp.maximum, far, peak_ref[head] + mark)
            else:
                far, near = scores
                peaks = functools.reduce(jnp.maximum, far + near)
            top = jnp.broadcast_to(jnp.max(peaks, axis=-1, keepdims=True), (rows_here, LANES))
            base = jnp.maximum(top, NEG_SAFE)
            weights = [
                [jnp.exp2((block - base) * EXP2_SCALE) for block in blocks]
                for blocks in (near, far)
            ]
            total = functools.reduce(jnp.add, weights[0] + weights[1])
            total = jnp.broadcast_to(
                jnp.sum(total, axis=-1, keepdims=True), (rows_here, LANES)
            )
            near, far = [
                jnp.concatenate([w.astype(jnp.bfloat16) for w in ws], axis=1) for ws in weights
            ]
            return top, total, near, far

        stats = jnp.zeros((rows_here, LANES), jnp.float32)
        ready = [scores_of(head) for head in range(DOC_AHEAD)]
        for head in range(KVH):
            cols = slice(head * HD, (head + 1) * HD)
            scores = ready.pop(0)
            if head + DOC_AHEAD < KVH:
                ready.append(scores_of(head + DOC_AHEAD))
            top, total, near, far = softmax_of(head, scores)
            out = jnp.dot(near, dv_ref[head], preferred_element_type=jnp.float32)
            out = out + jnp.dot(far, far_dv_ref[:, cols], preferred_element_type=jnp.float32)
            if local:
                terms = [(top[:GROUPS], total[:GROUPS], out[:GROUPS])]
                for ref in (own_ref, theirs_ref):
                    terms.append(
                        tuple(ref[head, i * GROUPS : (i + 1) * GROUPS] for i in range(3))
                    )
                new_top = functools.reduce(jnp.maximum, [t for t, _, _ in terms])
                base = jnp.maximum(new_top, NEG_SAFE)
                scales = [jnp.exp2((t - base) * EXP2_SCALE) for t, _, _ in terms]
                new_total = sum(s * l for s, (_, l, _) in zip(scales, terms))
                new_out = sum(s * o for s, (_, _, o) in zip(scales, terms))
                top = jnp.concatenate([new_top, top[GROUPS:]], axis=0)
                total = jnp.concatenate([new_total, total[GROUPS:]], axis=0)
                out = jnp.concatenate([new_out, out[GROUPS:]], axis=0)
            units = (out / jnp.maximum(total, 1.0)).astype(jnp.bfloat16)
            stats = jnp.where(lane_ids == head, top * EXP2_SCALE, stats)
            stats = jnp.where(lane_ids == KVH + head, total, stats)
            put(head * GROUPS, units.reshape(SLOTS, GROUPS, HD))
        put(HEADS, split_stats(stats, 1).reshape(SLOTS, GROUPS, LANES))

    size = out_refs[0].shape[0]
    if size < SLOTS:

        def put(row, value):
            for i, ref in enumerate(out_refs):
                ref[:, row : row + GROUPS, :] = value[i * size : (i + 1) * size]

        do_chunk(0, True, put)
        return
    steps = size // SLOTS
    for i, ref in enumerate(out_refs):

        def put_at(step):
            def put(row, value):
                ref[pl.ds(step * SLOTS, SLOTS), row : row + GROUPS, :] = value

            return put

        if i == 0:
            do_chunk(0, True, put_at(0))
        lax.fori_loop(
            1 if i == 0 else 0,
            steps,
            lambda step, _: do_chunk(i * steps + step, False, put_at(step)),
            None,
        )


def mix_weights(refs):
    rows = slice(HEADS, HEADS + GROUPS)
    stats = [join_stats(ref[:, rows, :], 2) for ref in refs]
    top = functools.reduce(jnp.maximum, [t for t, _ in stats])
    weights = [jnp.exp2(t - top) * total for t, total in stats]
    total = functools.reduce(jnp.add, weights)
    scale = 1.0 / jnp.maximum(total, 1.0)
    return top, total, [w * scale for w in weights[1:]]


def mixed_units(head, refs, weights):
    rows = slice(head * GROUPS, (head + 1) * GROUPS)
    first, *others = [ref[:, rows, :].astype(jnp.float32) for ref in refs]
    steps = [(u - first) * w[:, :, head : head + 1] for u, w in zip(others, weights)]
    return functools.reduce(jnp.add, steps, first)


def merge_kernel(count, *refs):
    sources, targets = refs[:count], refs[count:]
    top, total, weights = mix_weights(sources)
    size = targets[0].shape[0]
    for head in range(KVH):
        rows = slice(head * GROUPS, (head + 1) * GROUPS)
        units = mixed_units(head, sources, weights).astype(jnp.bfloat16)
        for i, target in enumerate(targets):
            target[:, rows, :] = units[i * size : (i + 1) * size]
    packed = split_stats(top + pltpu.roll(total, KVH, 2), 2)
    for i, target in enumerate(targets):
        target[:, HEADS : HEADS + GROUPS, :] = packed[i * size : (i + 1) * size]


def finish_kernel(count, *refs):
    sources, out_ref = refs[:count], refs[count]
    _, _, weights = mix_weights(sources)
    for head in range(KVH):
        units = mixed_units(head, sources, weights)[0]
        for g in range(GROUPS):
            h = head * GROUPS + g
            out_ref[:, h * HD : (h + 1) * HD] = units[g : g + 1, :].astype(jnp.bfloat16)


def whole(space=VMEM):
    return pl.BlockSpec(memory_space=space)


def near_core(x):
    return pltpu.with_memory_space_constraint(x, VMEM)


def on_core(kernel, out_shape, operands, cost=None, **kwargs):
    return pl.pallas_call(
        kernel,
        out_shape=out_shape,
        in_specs=kwargs.pop("in_specs", [whole()] * len(operands)),
        out_specs=jax.tree.map(lambda _: whole(), out_shape),
        compiler_params=pltpu.CompilerParams(vmem_limit_bytes=16 << 20),
        cost_estimate=cost,
        **kwargs,
    )(*operands)


def in_hbm(x):
    return pltpu.with_memory_space_constraint(x, pltpu.HBM)


def swap(x, bits):
    devices = lax.axis_size("seq")
    return lax.ppermute(x, "seq", [(i, i ^ bits) for i in range(devices)])


def stages_of(devices):
    far_bits = []
    while 2 ** (len(far_bits) + 3) < devices:
        far_bits.insert(0, (2 ** (len(far_bits) + 3) | 1,))
    return far_bits + [(3, 5, 7)[: devices // 2 - 1]]


def per_device(
    queries,
    new_keys,
    new_values,
    doc_keys,
    doc_values,
    suffix_keys,
    suffix_values,
    keep_lists,
    suffix_lengths,
):
    devices = lax.axis_size("seq")
    blocks = devices * doc_keys.shape[0] // BLOCK
    flag_rows = 8 * pl.cdiv(blocks, 8 * LANES)
    stages = stages_of(devices)
    packed = on_core(
        pack_kernel,
        VMEM((HEADS + flag_rows, HD), jnp.bfloat16),
        (in_hbm(keep_lists), in_hbm(queries)),
        cost=pl.CostEstimate(flops=10**10, bytes_accessed=10**5, transcendentals=0),
    )
    near = packed[None]
    own = near
    heads_of = lambda x: VMEM((KVH, x.shape[0], HD), x.dtype)
    size = 2 * suffix_keys.size
    pair = swap(own, 1)
    far_dk = swap(doc_keys, 1)
    far_dv = swap(doc_values, 1)
    partial = VMEM((KVH, 3 * GROUPS, LANES), jnp.float32)
    local, pair_local, dk, dv = on_core(
        suffix_kernel,
        [partial, partial, heads_of(doc_keys), heads_of(doc_values)],
        (
            near_core(suffix_lengths[None]),
            own,
            near_core(pair),
            suffix_keys,
            suffix_values,
            new_keys,
            new_values,
            doc_keys,
            doc_values,
        ),
        cost=pl.CostEstimate(flops=10**9, bytes_accessed=3 * size, transcendentals=10**6),
    )
    for step, stage in enumerate(stages):
        arrived = []
        for bits in stage:
            arrived.append(swap(near, bits))
        near = jnp.concatenate([near] + arrived, axis=0)
    other = swap(near[:, HEADS:, :], 1)
    near = near_core(near)
    theirs = swap(pair_local, 1)
    tokens = lambda count: VMEM((count, HEADS + GROUPS, HD), jnp.bfloat16)
    cost = pl.CostEstimate(flops=10**9, bytes_accessed=2 * size, transcendentals=10**6)
    span = doc_keys.shape[0]
    rows = devices // 2 * GROUPS
    scored = devices // 2 == SLOTS
    scores = ()
    if scored:
        scores = on_core(
            score_kernel,
            (
                VMEM((KVH, rows, span), jnp.float32),
                VMEM((KVH, rows, LANES), jnp.float32),
            ),
            (near, dk),
            cost=cost,
        )
    pieces = len(stages[-1]) + 1
    parts = on_core(
        functools.partial(attend_kernel, flag_rows, scored, pieces),
        [tokens(devices // 2 // pieces)] * pieces,
        (
            near,
            near_core(other),
            *scores,
            dk,
            dv,
            near_core(far_dk),
            near_core(far_dv),
            local,
            near_core(theirs),
        ),
        scratch_shapes=[VMEM((SLOTS * GROUPS, 2 * span), jnp.float32)],
        cost=cost,
    )
    step = len(stages) - 1
    while stages:
        stage = stages.pop()
        sources = [parts[0]]
        for bits, part in zip(stage, parts[1:]):
            sources.append(near_core(swap(part, bits)))
        step -= 1
        if stages:
            pieces = len(stages[-1]) + 1
            parts = on_core(
                functools.partial(merge_kernel, len(sources)),
                [tokens(sources[0].shape[0] // pieces)] * pieces,
                sources,
            )
    return on_core(
        functools.partial(finish_kernel, len(sources)),
        jax.ShapeDtypeStruct((1, HEADS * HD), jnp.bfloat16),
        sources,
    )


def solution(mesh):
    split = P(("parts", "seq"), None)
    return jax.shard_map(
        per_device,
        mesh=mesh,
        in_specs=(split,) * 8 + (P("parts"),),
        out_specs=split,
        check_vma=False,
    )
```

```python
import functools
import math

import jax
import jax.numpy as jnp
from jax import lax
from jax.experimental import pallas as pl
from jax.experimental.pallas import tpu as pltpu
from jax.sharding import PartitionSpec as P


HEADS = 64
KVH = 8
HD = 128
BLOCK = 128
GROUPS = HEADS // KVH
LANES = 128
SLOTS = 8

NEG_BIG = -1e30
NEG_SAFE = -5e29
AHEAD = 4
DOC_AHEAD = 3
EXP2_SCALE = HD**-0.5 * math.log2(math.e)

VMEM = pltpu.VMEM


def pack_kernel(list_ref, q_ref, out_ref):
    q = q_ref[...].astype(jnp.float32)
    rows = [q[:, h * HD : (h + 1) * HD] for h in range(HEADS)]
    out_ref[0:HEADS, :] = jnp.concatenate(rows, axis=0).astype(jnp.bfloat16)
    entries = list_ref.shape[1]
    ids = list_ref[...].astype(jnp.float32)
    diagonal = lax.broadcasted_iota(jnp.int32, (entries, entries), 0) == lax.broadcasted_iota(
        jnp.int32, (entries, entries), 1
    )
    column = jnp.sum(jnp.where(diagonal, ids, 0.0), axis=1, keepdims=True)
    lanes = lax.broadcasted_iota(jnp.int32, (entries, LANES), 1).astype(jnp.float32)
    found = [
        jnp.max(jnp.where(column == lanes + float(i * LANES), 1.0, 0.0), axis=0, keepdims=True)
        for i in range(out_ref.shape[0] - HEADS)
    ]
    out_ref[HEADS:, :] = jnp.concatenate(found, axis=0).astype(jnp.bfloat16)


def lane_dot(a, b):
    return lax.dot_general(a, b, (((1,), (1,)), ((), ())), preferred_element_type=jnp.float32)


def suffix_kernel(
    len_ref,
    own_ref,
    pair_ref,
    sk_ref,
    sv_ref,
    nk_ref,
    nv_ref,
    own_out_ref,
    pair_out_ref,
):
    me = lax.axis_index("seq")
    parity = lax.rem(me, 2)
    mine = lax.broadcasted_iota(jnp.int32, len_ref.shape, 1) == lax.div(me, 2)
    length = jnp.sum(
        jnp.where(mine, len_ref[...].astype(jnp.float32), 0.0), axis=1, keepdims=True
    )
    live_left = length.astype(jnp.int32) - parity * sv_ref.shape[0]

    def scores_of(head):
        rows = slice(head * GROUPS, (head + 1) * GROUPS)
        cols = slice(head * HD, (head + 1) * HD)
        q = jnp.concatenate(
            [ref[0, rows, :].astype(jnp.float32) for ref in (own_ref, pair_ref)], axis=0
        )
        scores = lane_dot(q.astype(jnp.bfloat16), sk_ref[:, cols])
        position = lax.broadcasted_iota(jnp.int32, scores.shape, 1)
        scores = jnp.where(position < live_left, scores, NEG_BIG)
        n_top = jnp.sum(q * nk_ref[:, cols].astype(jnp.float32), axis=-1, keepdims=True)
        hidden = (lax.broadcasted_iota(jnp.int32, n_top.shape, 0) >= GROUPS) & (parity == 1)
        return scores, jnp.where(hidden, NEG_BIG, n_top)

    ready = [scores_of(head) for head in range(AHEAD)]
    for head in range(KVH):
        cols = slice(head * HD, (head + 1) * HD)
        scores, n_top = ready.pop(0)
        if head + AHEAD < KVH:
            ready.append(scores_of(head + AHEAD))
        top = jnp.maximum(jnp.max(scores, axis=-1, keepdims=True), n_top)
        base = jnp.maximum(top, NEG_SAFE)
        weights = jnp.exp2((scores - base) * EXP2_SCALE)
        n_scale = jnp.exp2((n_top - base) * EXP2_SCALE)
        total = jnp.sum(weights, axis=-1, keepdims=True) + n_scale
        out = jnp.dot(
            weights.astype(jnp.bfloat16), sv_ref[:, cols], preferred_element_type=jnp.float32
        )
        out = out + n_scale * nv_ref[:, cols].astype(jnp.float32)
        for i, target in enumerate((own_out_ref, pair_out_ref)):
            mine = slice(i * GROUPS, (i + 1) * GROUPS)
            target[head, 0:GROUPS] = jnp.broadcast_to(top[mine], (GROUPS, LANES))
            target[head, GROUPS : 2 * GROUPS] = jnp.broadcast_to(total[mine], (GROUPS, LANES))
            target[head, 2 * GROUPS :] = out[mine]


def order_kernel(_, source, target):
    for head in range(KVH):
        target[head] = source[:, head * HD : (head + 1) * HD]


def split_stats(stats, axis):
    high = stats.astype(jnp.bfloat16).astype(jnp.float32)
    rest = stats - high
    middle = rest.astype(jnp.bfloat16).astype(jnp.float32)
    low = rest - middle
    packed = high + pltpu.roll(middle, 2 * KVH, axis) + pltpu.roll(low, 4 * KVH, axis)
    return packed.astype(jnp.bfloat16)


def join_stats(packed, axis):
    packed = packed.astype(jnp.float32)
    shifted = lambda by: pltpu.roll(packed, LANES - by * KVH, axis)
    live = lax.broadcasted_iota(jnp.int32, packed.shape, axis) < KVH
    top = jnp.where(live, packed + shifted(2) + shifted(4), 0.0)
    total = jnp.where(live, shifted(1) + shifted(3) + shifted(5), 0.0)
    return top, total


def head_queries(ref, slots, head):
    q = ref[slots, head * GROUPS : (head + 1) * GROUPS, :].astype(jnp.float32)
    return q.reshape(SLOTS * GROUPS, HD).astype(jnp.bfloat16)


def score_kernel(token_ref, dk_ref, score_ref, peak_ref):
    rows_here = SLOTS * GROUPS
    lane_ids = lax.broadcasted_iota(jnp.int32, (rows_here, LANES), 1)
    for head in range(KVH):
        scores = lane_dot(head_queries(token_ref, pl.ds(0, SLOTS), head), dk_ref[head])
        score_ref[head] = scores
        peaks = jnp.full((rows_here, LANES), NEG_BIG, jnp.float32)
        for b in range(scores.shape[1] // BLOCK):
            block = scores[:, b * BLOCK : (b + 1) * BLOCK]
            peaks = jnp.where(lane_ids == b, jnp.max(block, axis=-1, keepdims=True), peaks)
        peak_ref[head] = peaks


def attend_kernel(flag_rows, scored, pieces, *refs):
    near_ref, other_ref, *refs = refs
    if scored:
        score_ref, peak_ref, *refs = refs
    dk_ref, dv_ref, far_dk_ref, far_dv_ref, own_ref, theirs_ref, *refs = refs
    out_refs, (bias_ref,) = refs[:pieces], refs[pieces:]
    span = far_dk_ref.shape[1]
    blocks_here = span // BLOCK
    rows_here = SLOTS * GROUPS
    me = lax.axis_index("seq")
    flag_row = lax.div(me * blocks_here, LANES)
    row_ids = lax.broadcasted_iota(jnp.int32, (1, flag_rows, LANES), 1)
    lane_ids = lax.broadcasted_iota(jnp.int32, (rows_here, LANES), 1)

    def tall(x):
        wide = jnp.broadcast_to(x[:, None, :], (SLOTS, GROUPS, LANES))
        return wide.reshape(rows_here, LANES)

    def do_chunk(chunk, local, put):
        slots = pl.ds(chunk * SLOTS, SLOTS)
        flags = near_ref[slots, HEADS:, :].astype(jnp.float32)
        flags = flags + other_ref[slots].astype(jnp.float32)
        flags = jnp.sum(jnp.where(row_ids == flag_row, flags, 0.0), axis=1)
        marks = []
        for i, device in enumerate((me, me ^ 1)):
            lane = lax.rem(device * blocks_here, LANES)
            bias = jnp.where(pltpu.roll(flags, LANES - lane, 1) > 0.5, 0.0, NEG_BIG)
            marks.append(bias)
            for b in range(blocks_here):
                wide = jnp.broadcast_to(bias[:, b : b + 1], (SLOTS, LANES))
                at = i * span + b * BLOCK
                bias_ref[:, at : at + BLOCK] = tall(wide)
        mark = tall(marks[0])

        def blocks_of(scores):
            return [scores[:, b * LANES : (b + 1) * LANES] for b in range(span // LANES)]

        def scores_of(head):
            q = head_queries(near_ref, slots, head)
            far = lane_dot(q, far_dk_ref[head]) + bias_ref[:, span:]
            if scored:
                return blocks_of(far)
            return blocks_of(far), blocks_of(lane_dot(q, dk_ref[head]) + bias_ref[:, :span])

        def softmax_of(head, scores):
            if scored:
                far = scores
                near = blocks_of(score_ref[head] + bias_ref[:, :span])
                peaks = functools.reduce(jnp.maximum, far, peak_ref[head] + mark)
            else:
                far, near = scores
                peaks = functools.reduce(jnp.maximum, far + near)
            top = jnp.broadcast_to(jnp.max(peaks, axis=-1, keepdims=True), (rows_here, LANES))
            base = jnp.maximum(top, NEG_SAFE)
            weights = [
                [jnp.exp2((block - base) * EXP2_SCALE) for block in blocks]
                for blocks in (near, far)
            ]
            total = functools.reduce(jnp.add, weights[0] + weights[1])
            total = jnp.broadcast_to(
                jnp.sum(total, axis=-1, keepdims=True), (rows_here, LANES)
            )
            near, far = [
                jnp.concatenate([w.astype(jnp.bfloat16) for w in ws], axis=1) for ws in weights
            ]
            return top, total, near, far

        stats = jnp.zeros((rows_here, LANES), jnp.float32)
        ready = [scores_of(head) for head in range(DOC_AHEAD)]
        for head in range(KVH):
            cols = slice(head * HD, (head + 1) * HD)
            scores = ready.pop(0)
            if head + DOC_AHEAD < KVH:
                ready.append(scores_of(head + DOC_AHEAD))
            top, total, near, far = softmax_of(head, scores)
            out = jnp.dot(near, dv_ref[head], preferred_element_type=jnp.float32)
            out = out + jnp.dot(far, far_dv_ref[:, cols], preferred_element_type=jnp.float32)
            if local:
                terms = [(top[:GROUPS], total[:GROUPS], out[:GROUPS])]
                for ref in (own_ref, theirs_ref):
                    terms.append(
                        tuple(ref[head, i * GROUPS : (i + 1) * GROUPS] for i in range(3))
                    )
                new_top = functools.reduce(jnp.maximum, [t for t, _, _ in terms])
                base = jnp.maximum(new_top, NEG_SAFE)
                scales = [jnp.exp2((t - base) * EXP2_SCALE) for t, _, _ in terms]
                new_total = sum(s * l for s, (_, l, _) in zip(scales, terms))
                new_out = sum(s * o for s, (_, _, o) in zip(scales, terms))
                top = jnp.concatenate([new_top, top[GROUPS:]], axis=0)
                total = jnp.concatenate([new_total, total[GROUPS:]], axis=0)
                out = jnp.concatenate([new_out, out[GROUPS:]], axis=0)
            units = (out / jnp.maximum(total, 1.0)).astype(jnp.bfloat16)
            stats = jnp.where(lane_ids == head, top * EXP2_SCALE, stats)
            stats = jnp.where(lane_ids == KVH + head, total, stats)
            put(head * GROUPS, units.reshape(SLOTS, GROUPS, HD))
        put(HEADS, split_stats(stats, 1).reshape(SLOTS, GROUPS, LANES))

    size = out_refs[0].shape[0]
    if size < SLOTS:

        def put(row, value):
            for i, ref in enumerate(out_refs):
                ref[:, row : row + GROUPS, :] = value[i * size : (i + 1) * size]

        do_chunk(0, True, put)
        return
    steps = size // SLOTS
    for i, ref in enumerate(out_refs):

        def put_at(step):
            def put(row, value):
                ref[pl.ds(step * SLOTS, SLOTS), row : row + GROUPS, :] = value

            return put

        if i == 0:
            do_chunk(0, True, put_at(0))
        lax.fori_loop(
            1 if i == 0 else 0,
            steps,
            lambda step, _: do_chunk(i * steps + step, False, put_at(step)),
            None,
        )


def mix_weights(refs):
    rows = slice(HEADS, HEADS + GROUPS)
    stats = [join_stats(ref[:, rows, :], 2) for ref in refs]
    top = functools.reduce(jnp.maximum, [t for t, _ in stats])
    weights = [jnp.exp2(t - top) * total for t, total in stats]
    total = functools.reduce(jnp.add, weights)
    scale = 1.0 / jnp.maximum(total, 1.0)
    return top, total, [w * scale for w in weights[1:]]


def mixed_units(head, refs, weights):
    rows = slice(head * GROUPS, (head + 1) * GROUPS)
    first, *others = [ref[:, rows, :].astype(jnp.float32) for ref in refs]
    steps = [(u - first) * w[:, :, head : head + 1] for u, w in zip(others, weights)]
    return functools.reduce(jnp.add, steps, first)


def merge_kernel(count, *refs):
    sources, targets = refs[:count], refs[count:]
    top, total, weights = mix_weights(sources)
    size = targets[0].shape[0]
    for head in range(KVH):
        rows = slice(head * GROUPS, (head + 1) * GROUPS)
        units = mixed_units(head, sources, weights).astype(jnp.bfloat16)
        for i, target in enumerate(targets):
            target[:, rows, :] = units[i * size : (i + 1) * size]
    packed = split_stats(top + pltpu.roll(total, KVH, 2), 2)
    for i, target in enumerate(targets):
        target[:, HEADS : HEADS + GROUPS, :] = packed[i * size : (i + 1) * size]


def finish_kernel(count, *refs):
    sources, out_ref = refs[:count], refs[count]
    _, _, weights = mix_weights(sources)
    for head in range(KVH):
        units = mixed_units(head, sources, weights)[0]
        for g in range(GROUPS):
            h = head * GROUPS + g
            out_ref[:, h * HD : (h + 1) * HD] = units[g : g + 1, :].astype(jnp.bfloat16)


def whole(space=VMEM):
    return pl.BlockSpec(memory_space=space)


def near_core(x):
    return pltpu.with_memory_space_constraint(x, VMEM)


def on_core(kernel, out_shape, operands, cost=None, **kwargs):
    return pl.pallas_call(
        kernel,
        out_shape=out_shape,
        in_specs=kwargs.pop("in_specs", [whole()] * len(operands)),
        out_specs=jax.tree.map(lambda _: whole(), out_shape),
        compiler_params=pltpu.CompilerParams(vmem_limit_bytes=16 << 20),
        cost_estimate=cost,
        **kwargs,
    )(*operands)


def in_hbm(x):
    return pltpu.with_memory_space_constraint(x, pltpu.HBM)


def swap(x, bits):
    devices = lax.axis_size("seq")
    return lax.ppermute(x, "seq", [(i, i ^ bits) for i in range(devices)])


def stages_of(devices):
    far_bits = []
    while 2 ** (len(far_bits) + 3) < devices:
        far_bits.insert(0, (2 ** (len(far_bits) + 3) | 1,))
    return far_bits + [(3, 5, 7)[: devices // 2 - 1]]


def per_device(
    queries,
    new_keys,
    new_values,
    doc_keys,
    doc_values,
    suffix_keys,
    suffix_values,
    keep_lists,
    suffix_lengths,
):
    devices = lax.axis_size("seq")
    blocks = devices * doc_keys.shape[0] // BLOCK
    flag_rows = 8 * pl.cdiv(blocks, 8 * LANES)
    stages = stages_of(devices)
    packed = on_core(
        pack_kernel,
        VMEM((HEADS + flag_rows, HD), jnp.bfloat16),
        (in_hbm(keep_lists), in_hbm(queries)),
        cost=pl.CostEstimate(flops=10**10, bytes_accessed=10**5, transcendentals=0),
    )
    near = packed[None]
    own = near
    heads_of = lambda x: VMEM((KVH, x.shape[0], HD), x.dtype)
    size = 2 * suffix_keys.size
    pair = swap(own, 1)
    far_dk = swap(doc_keys, 1)
    far_dv = swap(doc_values, 1)

    def ordered(after, cache):
        return on_core(
            order_kernel,
            heads_of(cache),
            (after, cache),
            cost=pl.CostEstimate(flops=0, bytes_accessed=4 * size, transcendentals=0),
        )

    dk = ordered(own, doc_keys)
    dv = ordered(own, doc_values)
    partial = VMEM((KVH, 3 * GROUPS, LANES), jnp.float32)
    local, pair_local = on_core(
        suffix_kernel,
        [partial, partial],
        (
            near_core(suffix_lengths[None]),
            own,
            near_core(pair),
            suffix_keys,
            suffix_values,
            new_keys,
            new_values,
        ),
        cost=pl.CostEstimate(flops=10**9, bytes_accessed=3 * size, transcendentals=10**6),
    )
    far_dk = ordered(local, near_core(far_dk))
    for step, stage in enumerate(stages):
        arrived = []
        for bits in stage:
            arrived.append(swap(near, bits))
        near = jnp.concatenate([near] + arrived, axis=0)
    other = swap(near[:, HEADS:, :], 1)
    near = near_core(near)
    theirs = swap(pair_local, 1)
    tokens = lambda count: VMEM((count, HEADS + GROUPS, HD), jnp.bfloat16)
    cost = pl.CostEstimate(flops=10**9, bytes_accessed=2 * size, transcendentals=10**6)
    span = doc_keys.shape[0]
    rows = devices // 2 * GROUPS
    scored = devices // 2 == SLOTS
    scores = ()
    if scored:
        scores = on_core(
            score_kernel,
            (
                VMEM((KVH, rows, span), jnp.float32),
                VMEM((KVH, rows, LANES), jnp.float32),
            ),
            (near, dk),
            cost=cost,
        )
    pieces = len(stages[-1]) + 1
    parts = on_core(
        functools.partial(attend_kernel, flag_rows, scored, pieces),
        [tokens(devices // 2 // pieces)] * pieces,
        (
            near,
            near_core(other),
            *scores,
            dk,
            dv,
            far_dk,
            near_core(far_dv),
            local,
            near_core(theirs),
        ),
        scratch_shapes=[VMEM((SLOTS * GROUPS, 2 * span), jnp.float32)],
        cost=cost,
    )
    step = len(stages) - 1
    while stages:
        stage = stages.pop()
        sources = [parts[0]]
        for bits, part in zip(stage, parts[1:]):
            sources.append(near_core(swap(part, bits)))
        step -= 1
        if stages:
            pieces = len(stages[-1]) + 1
            parts = on_core(
                functools.partial(merge_kernel, len(sources)),
                [tokens(sources[0].shape[0] // pieces)] * pieces,
                sources,
            )
    return on_core(
        functools.partial(finish_kernel, len(sources)),
        jax.ShapeDtypeStruct((1, HEADS * HD), jnp.bfloat16),
        sources,
    )


def solution(mesh):
    split = P(("parts", "seq"), None)
    return jax.shard_map(
        per_device,
        mesh=mesh,
        in_specs=(split,) * 8 + (P("parts"),),
        out_specs=split,
        check_vma=False,
    )
```

```python
import functools
import math

import jax
import jax.numpy as jnp
from jax import lax
from jax.experimental import pallas as pl
from jax.experimental.pallas import tpu as pltpu
from jax.sharding import PartitionSpec as P


HEADS = 64
KVH = 8
HD = 128
BLOCK = 128
GROUPS = HEADS // KVH
LANES = 128
SLOTS = 8

NEG_BIG = -1e30
NEG_SAFE = -5e29
AHEAD = 4
DOC_AHEAD = 3
EXP2_SCALE = HD**-0.5 * math.log2(math.e)

VMEM = pltpu.VMEM


def pack_kernel(list_ref, q_ref, out_ref):
    q = q_ref[...].astype(jnp.float32)
    rows = [q[:, h * HD : (h + 1) * HD] for h in range(HEADS)]
    out_ref[0:HEADS, :] = jnp.concatenate(rows, axis=0).astype(jnp.bfloat16)
    entries = list_ref.shape[1]
    ids = list_ref[...].astype(jnp.float32)
    diagonal = lax.broadcasted_iota(jnp.int32, (entries, entries), 0) == lax.broadcasted_iota(
        jnp.int32, (entries, entries), 1
    )
    column = jnp.sum(jnp.where(diagonal, ids, 0.0), axis=1, keepdims=True)
    lanes = lax.broadcasted_iota(jnp.int32, (entries, LANES), 1).astype(jnp.float32)
    found = [
        jnp.max(jnp.where(column == lanes + float(i * LANES), 1.0, 0.0), axis=0, keepdims=True)
        for i in range(out_ref.shape[0] - HEADS)
    ]
    out_ref[HEADS:, :] = jnp.concatenate(found, axis=0).astype(jnp.bfloat16)


def lane_dot(a, b):
    return lax.dot_general(a, b, (((1,), (1,)), ((), ())), preferred_element_type=jnp.float32)


def suffix_kernel(
    len_ref,
    own_ref,
    pair_ref,
    sk_ref,
    sv_ref,
    nk_ref,
    nv_ref,
    own_out_ref,
    pair_out_ref,
):
    me = lax.axis_index("seq")
    parity = lax.rem(me, 2)
    mine = lax.broadcasted_iota(jnp.int32, len_ref.shape, 1) == lax.div(me, 2)
    length = jnp.sum(
        jnp.where(mine, len_ref[...].astype(jnp.float32), 0.0), axis=1, keepdims=True
    )
    live_left = length.astype(jnp.int32) - parity * sv_ref.shape[0]

    def scores_of(head):
        rows = slice(head * GROUPS, (head + 1) * GROUPS)
        cols = slice(head * HD, (head + 1) * HD)
        q = jnp.concatenate(
            [ref[0, rows, :].astype(jnp.float32) for ref in (own_ref, pair_ref)], axis=0
        )
        scores = lane_dot(q.astype(jnp.bfloat16), sk_ref[:, cols])
        position = lax.broadcasted_iota(jnp.int32, scores.shape, 1)
        scores = jnp.where(position < live_left, scores, NEG_BIG)
        n_top = jnp.sum(q * nk_ref[:, cols].astype(jnp.float32), axis=-1, keepdims=True)
        hidden = (lax.broadcasted_iota(jnp.int32, n_top.shape, 0) >= GROUPS) & (parity == 1)
        return scores, jnp.where(hidden, NEG_BIG, n_top)

    ready = [scores_of(head) for head in range(AHEAD)]
    for head in range(KVH):
        cols = slice(head * HD, (head + 1) * HD)
        scores, n_top = ready.pop(0)
        if head + AHEAD < KVH:
            ready.append(scores_of(head + AHEAD))
        top = jnp.maximum(jnp.max(scores, axis=-1, keepdims=True), n_top)
        base = jnp.maximum(top, NEG_SAFE)
        weights = jnp.exp2((scores - base) * EXP2_SCALE)
        n_scale = jnp.exp2((n_top - base) * EXP2_SCALE)
        total = jnp.sum(weights, axis=-1, keepdims=True) + n_scale
        out = jnp.dot(
            weights.astype(jnp.bfloat16), sv_ref[:, cols], preferred_element_type=jnp.float32
        )
        out = out + n_scale * nv_ref[:, cols].astype(jnp.float32)
        for i, target in enumerate((own_out_ref, pair_out_ref)):
            mine = slice(i * GROUPS, (i + 1) * GROUPS)
            target[head, 0:GROUPS] = jnp.broadcast_to(top[mine], (GROUPS, LANES))
            target[head, GROUPS : 2 * GROUPS] = jnp.broadcast_to(total[mine], (GROUPS, LANES))
            target[head, 2 * GROUPS :] = out[mine]


def order_kernel(_, source, target):
    for head in range(KVH):
        target[head] = source[:, head * HD : (head + 1) * HD]


def split_stats(stats, axis):
    high = stats.astype(jnp.bfloat16).astype(jnp.float32)
    rest = stats - high
    middle = rest.astype(jnp.bfloat16).astype(jnp.float32)
    low = rest - middle
    packed = high + pltpu.roll(middle, 2 * KVH, axis) + pltpu.roll(low, 4 * KVH, axis)
    return packed.astype(jnp.bfloat16)


def join_stats(packed, axis):
    packed = packed.astype(jnp.float32)
    shifted = lambda by: pltpu.roll(packed, LANES - by * KVH, axis)
    live = lax.broadcasted_iota(jnp.int32, packed.shape, axis) < KVH
    top = jnp.where(live, packed + shifted(2) + shifted(4), 0.0)
    total = jnp.where(live, shifted(1) + shifted(3) + shifted(5), 0.0)
    return top, total


def head_queries(ref, slots, head):
    q = ref[slots, head * GROUPS : (head + 1) * GROUPS, :].astype(jnp.float32)
    return q.reshape(SLOTS * GROUPS, HD).astype(jnp.bfloat16)


def score_kernel(token_ref, dk_ref, score_ref, peak_ref):
    rows_here = SLOTS * GROUPS
    lane_ids = lax.broadcasted_iota(jnp.int32, (rows_here, LANES), 1)
    for head in range(KVH):
        scores = lane_dot(head_queries(token_ref, pl.ds(0, SLOTS), head), dk_ref[head])
        score_ref[head] = scores
        peaks = jnp.full((rows_here, LANES), NEG_BIG, jnp.float32)
        for b in range(scores.shape[1] // BLOCK):
            block = scores[:, b * BLOCK : (b + 1) * BLOCK]
            peaks = jnp.where(lane_ids == b, jnp.max(block, axis=-1, keepdims=True), peaks)
        peak_ref[head] = peaks


def attend_kernel(flag_rows, scored, pieces, *refs):
    near_ref, other_ref, *refs = refs
    if scored:
        score_ref, peak_ref, *refs = refs
    dk_ref, dv_ref, far_dk_ref, far_dv_ref, own_ref, theirs_ref, *refs = refs
    out_refs, (bias_ref,) = refs[:pieces], refs[pieces:]
    span = far_dk_ref.shape[0]
    blocks_here = span // BLOCK
    rows_here = SLOTS * GROUPS
    me = lax.axis_index("seq")
    flag_row = lax.div(me * blocks_here, LANES)
    row_ids = lax.broadcasted_iota(jnp.int32, (1, flag_rows, LANES), 1)
    lane_ids = lax.broadcasted_iota(jnp.int32, (rows_here, LANES), 1)

    def tall(x):
        wide = jnp.broadcast_to(x[:, None, :], (SLOTS, GROUPS, LANES))
        return wide.reshape(rows_here, LANES)

    def do_chunk(chunk, local, put):
        slots = pl.ds(chunk * SLOTS, SLOTS)
        flags = near_ref[slots, HEADS:, :].astype(jnp.float32)
        flags = flags + other_ref[slots].astype(jnp.float32)
        flags = jnp.sum(jnp.where(row_ids == flag_row, flags, 0.0), axis=1)
        marks = []
        for i, device in enumerate((me, me ^ 1)):
            lane = lax.rem(device * blocks_here, LANES)
            bias = jnp.where(pltpu.roll(flags, lax.rem(LANES - lane, LANES), 1) > 0.5, 0.0, NEG_BIG)
            marks.append(bias)
            for b in range(blocks_here):
                wide = jnp.broadcast_to(bias[:, b : b + 1], (SLOTS, LANES))
                at = i * span + b * BLOCK
                bias_ref[:, at : at + BLOCK] = tall(wide)
        mark = tall(marks[0])

        def blocks_of(scores):
            return [scores[:, b * LANES : (b + 1) * LANES] for b in range(span // LANES)]

        def scores_of(head):
            q = head_queries(near_ref, slots, head)
            cols = slice(head * HD, (head + 1) * HD)
            far = lane_dot(q, far_dk_ref[:, cols]) + bias_ref[:, span:]
            if scored:
                return blocks_of(far)
            return blocks_of(far), blocks_of(lane_dot(q, dk_ref[head]) + bias_ref[:, :span])

        def softmax_of(head, scores):
            if scored:
                far = scores
                near = blocks_of(score_ref[head] + bias_ref[:, :span])
                peaks = functools.reduce(jnp.maximum, far, peak_ref[head] + mark)
            else:
                far, near = scores
                peaks = functools.reduce(jnp.maximum, far + near)
            top = jnp.broadcast_to(jnp.max(peaks, axis=-1, keepdims=True), (rows_here, LANES))
            base = jnp.maximum(top, NEG_SAFE)
            weights = [
                [jnp.exp2((block - base) * EXP2_SCALE) for block in blocks]
                for blocks in (near, far)
            ]
            total = functools.reduce(jnp.add, weights[0] + weights[1])
            total = jnp.broadcast_to(
                jnp.sum(total, axis=-1, keepdims=True), (rows_here, LANES)
            )
            near, far = [
                jnp.concatenate([w.astype(jnp.bfloat16) for w in ws], axis=1) for ws in weights
            ]
            return top, total, near, far

        stats = jnp.zeros((rows_here, LANES), jnp.float32)
        ready = [scores_of(head) for head in range(DOC_AHEAD)]
        for head in range(KVH):
            scores = ready.pop(0)
            if head + DOC_AHEAD < KVH:
                ready.append(scores_of(head + DOC_AHEAD))
            top, total, near, far = softmax_of(head, scores)
            out = jnp.dot(near, dv_ref[head], preferred_element_type=jnp.float32)
            out = out + jnp.dot(far, far_dv_ref[head], preferred_element_type=jnp.float32)
            if local:
                terms = [(top[:GROUPS], total[:GROUPS], out[:GROUPS])]
                for ref in (own_ref, theirs_ref):
                    terms.append(
                        tuple(ref[head, i * GROUPS : (i + 1) * GROUPS] for i in range(3))
                    )
                new_top = functools.reduce(jnp.maximum, [t for t, _, _ in terms])
                base = jnp.maximum(new_top, NEG_SAFE)
                scales = [jnp.exp2((t - base) * EXP2_SCALE) for t, _, _ in terms]
                new_total = sum(s * l for s, (_, l, _) in zip(scales, terms))
                new_out = sum(s * o for s, (_, _, o) in zip(scales, terms))
                top = jnp.concatenate([new_top, top[GROUPS:]], axis=0)
                total = jnp.concatenate([new_total, total[GROUPS:]], axis=0)
                out = jnp.concatenate([new_out, out[GROUPS:]], axis=0)
            units = (out / jnp.maximum(total, 1.0)).astype(jnp.bfloat16)
            stats = jnp.where(lane_ids == head, top * EXP2_SCALE, stats)
            stats = jnp.where(lane_ids == KVH + head, total, stats)
            put(head * GROUPS, units.reshape(SLOTS, GROUPS, HD))
        put(HEADS, split_stats(stats, 1).reshape(SLOTS, GROUPS, LANES))

    size = out_refs[0].shape[0]
    if size < SLOTS:

        def put(row, value):
            for i, ref in enumerate(out_refs):
                ref[:, row : row + GROUPS, :] = value[i * size : (i + 1) * size]

        do_chunk(0, True, put)
        return
    steps = size // SLOTS
    for i, ref in enumerate(out_refs):

        def put_at(step):
            def put(row, value):
                ref[pl.ds(step * SLOTS, SLOTS), row : row + GROUPS, :] = value

            return put

        if i == 0:
            do_chunk(0, True, put_at(0))
        lax.fori_loop(
            1 if i == 0 else 0,
            steps,
            lambda step, _: do_chunk(i * steps + step, False, put_at(step)),
            None,
        )


def mix_weights(refs):
    rows = slice(HEADS, HEADS + GROUPS)
    stats = [join_stats(ref[:, rows, :], 2) for ref in refs]
    top = functools.reduce(jnp.maximum, [t for t, _ in stats])
    weights = [jnp.exp2(t - top) * total for t, total in stats]
    total = functools.reduce(jnp.add, weights)
    scale = 1.0 / jnp.maximum(total, 1.0)
    return top, total, [w * scale for w in weights[1:]]


def mixed_units(head, refs, weights):
    rows = slice(head * GROUPS, (head + 1) * GROUPS)
    first, *others = [ref[:, rows, :].astype(jnp.float32) for ref in refs]
    steps = [(u - first) * w[:, :, head : head + 1] for u, w in zip(others, weights)]
    return functools.reduce(jnp.add, steps, first)


def merge_kernel(count, *refs):
    sources, targets = refs[:count], refs[count:]
    top, total, weights = mix_weights(sources)
    size = targets[0].shape[0]
    for head in range(KVH):
        rows = slice(head * GROUPS, (head + 1) * GROUPS)
        units = mixed_units(head, sources, weights).astype(jnp.bfloat16)
        for i, target in enumerate(targets):
            target[:, rows, :] = units[i * size : (i + 1) * size]
    packed = split_stats(top + pltpu.roll(total, KVH, 2), 2)
    for i, target in enumerate(targets):
        target[:, HEADS : HEADS + GROUPS, :] = packed[i * size : (i + 1) * size]


def finish_kernel(count, *refs):
    sources, out_ref = refs[:count], refs[count]
    _, _, weights = mix_weights(sources)
    for head in range(KVH):
        units = mixed_units(head, sources, weights)[0]
        for g in range(GROUPS):
            h = head * GROUPS + g
            out_ref[:, h * HD : (h + 1) * HD] = units[g : g + 1, :].astype(jnp.bfloat16)


def whole(space=VMEM):
    return pl.BlockSpec(memory_space=space)


def near_core(x):
    return pltpu.with_memory_space_constraint(x, VMEM)


def on_core(kernel, out_shape, operands, cost=None, **kwargs):
    return pl.pallas_call(
        kernel,
        out_shape=out_shape,
        in_specs=kwargs.pop("in_specs", [whole()] * len(operands)),
        out_specs=jax.tree.map(lambda _: whole(), out_shape),
        compiler_params=pltpu.CompilerParams(vmem_limit_bytes=16 << 20),
        cost_estimate=cost,
        **kwargs,
    )(*operands)


def in_hbm(x):
    return pltpu.with_memory_space_constraint(x, pltpu.HBM)


def swap(x, bits):
    devices = lax.axis_size("seq")
    return lax.ppermute(x, "seq", [(i, i ^ bits) for i in range(devices)])


def stages_of(devices):
    far_bits = []
    while 2 ** (len(far_bits) + 3) < devices:
        far_bits.insert(0, (2 ** (len(far_bits) + 3) | 1,))
    return far_bits + [(3, 5, 7)[: devices // 2 - 1]]


def per_device(
    queries,
    new_keys,
    new_values,
    doc_keys,
    doc_values,
    suffix_keys,
    suffix_values,
    keep_lists,
    suffix_lengths,
):
    devices = lax.axis_size("seq")
    blocks = devices * doc_keys.shape[0] // BLOCK
    flag_rows = 8 * pl.cdiv(blocks, 8 * LANES)
    stages = stages_of(devices)
    packed = on_core(
        pack_kernel,
        VMEM((HEADS + flag_rows, HD), jnp.bfloat16),
        (in_hbm(keep_lists), in_hbm(queries)),
        cost=pl.CostEstimate(flops=10**10, bytes_accessed=10**5, transcendentals=0),
    )
    near = packed[None]
    own = near
    heads_of = lambda x: VMEM((KVH, x.shape[0], HD), x.dtype)
    size = 2 * suffix_keys.size
    pair = swap(own, 1)
    far_dv = swap(doc_values, 1)
    far_dk = swap(doc_keys, 1)

    def ordered(after, cache):
        return on_core(
            order_kernel,
            heads_of(cache),
            (after, cache),
            cost=pl.CostEstimate(flops=0, bytes_accessed=4 * size, transcendentals=0),
        )

    dk = ordered(own, doc_keys)
    dv = ordered(own, doc_values)
    partial = VMEM((KVH, 3 * GROUPS, LANES), jnp.float32)
    local, pair_local = on_core(
        suffix_kernel,
        [partial, partial],
        (
            near_core(suffix_lengths[None]),
            own,
            near_core(pair),
            suffix_keys,
            suffix_values,
            new_keys,
            new_values,
        ),
        cost=pl.CostEstimate(flops=10**9, bytes_accessed=3 * size, transcendentals=10**6),
    )
    far_dv = ordered(local, near_core(far_dv))
    for step, stage in enumerate(stages):
        arrived = []
        for bits in stage:
            arrived.append(swap(near, bits))
        near = jnp.concatenate([near] + arrived, axis=0)
    other = swap(near[:, HEADS:, :], 1)
    near = near_core(near)
    theirs = swap(pair_local, 1)
    tokens = lambda count: VMEM((count, HEADS + GROUPS, HD), jnp.bfloat16)
    cost = pl.CostEstimate(flops=10**9, bytes_accessed=2 * size, transcendentals=10**6)
    span = doc_keys.shape[0]
    rows = devices // 2 * GROUPS
    scored = devices // 2 == SLOTS
    scores = ()
    if scored:
        scores = on_core(
            score_kernel,
            (
                VMEM((KVH, rows, span), jnp.float32),
                VMEM((KVH, rows, LANES), jnp.float32),
            ),
            (near, dk),
            cost=cost,
        )
    pieces = len(stages[-1]) + 1
    parts = on_core(
        functools.partial(attend_kernel, flag_rows, scored, pieces),
        [tokens(devices // 2 // pieces)] * pieces,
        (
            near,
            near_core(other),
            *scores,
            dk,
            dv,
            near_core(far_dk),
            far_dv,
            local,
            near_core(theirs),
        ),
        scratch_shapes=[VMEM((SLOTS * GROUPS, 2 * span), jnp.float32)],
        cost=cost,
    )
    step = len(stages) - 1
    while stages:
        stage = stages.pop()
        sources = [parts[0]]
        for bits, part in zip(stage, parts[1:]):
            sources.append(near_core(swap(part, bits)))
        step -= 1
        if stages:
            pieces = len(stages[-1]) + 1
            parts = on_core(
                functools.partial(merge_kernel, len(sources)),
                [tokens(sources[0].shape[0] // pieces)] * pieces,
                sources,
            )
    return on_core(
        functools.partial(finish_kernel, len(sources)),
        jax.ShapeDtypeStruct((1, HEADS * HD), jnp.bfloat16),
        sources,
    )


def solution(mesh):
    split = P(("parts", "seq"), None)
    return jax.shard_map(
        per_device,
        mesh=mesh,
        in_specs=(split,) * 8 + (P("parts"),),
        out_specs=split,
        check_vma=False,
    )
```

```python
import functools
import math

import jax
import jax.numpy as jnp
from jax import lax
from jax.experimental import pallas as pl
from jax.experimental.pallas import tpu as pltpu
from jax.sharding import PartitionSpec as P


HEADS = 64
KVH = 8
HD = 128
BLOCK = 128
GROUPS = HEADS // KVH
LANES = 128
SLOTS = 8

NEG_BIG = -1e30
NEG_SAFE = -5e29
AHEAD = 4
DOC_AHEAD = 3
EXP2_SCALE = HD**-0.5 * math.log2(math.e)

VMEM = pltpu.VMEM


def pack_kernel(list_ref, q_ref, out_ref):
    q = q_ref[...].astype(jnp.float32)
    rows = [q[:, h * HD : (h + 1) * HD] for h in range(HEADS)]
    out_ref[0:HEADS, :] = jnp.concatenate(rows, axis=0).astype(jnp.bfloat16)
    entries = list_ref.shape[1]
    ids = list_ref[...].astype(jnp.float32)
    diagonal = lax.broadcasted_iota(jnp.int32, (entries, entries), 0) == lax.broadcasted_iota(
        jnp.int32, (entries, entries), 1
    )
    column = jnp.sum(jnp.where(diagonal, ids, 0.0), axis=1, keepdims=True)
    lanes = lax.broadcasted_iota(jnp.int32, (entries, LANES), 1).astype(jnp.float32)
    found = [
        jnp.max(jnp.where(column == lanes + float(i * LANES), 1.0, 0.0), axis=0, keepdims=True)
        for i in range(out_ref.shape[0] - HEADS)
    ]
    out_ref[HEADS:, :] = jnp.concatenate(found, axis=0).astype(jnp.bfloat16)


def lane_dot(a, b):
    return lax.dot_general(a, b, (((1,), (1,)), ((), ())), preferred_element_type=jnp.float32)


def suffix_kernel(
    len_ref,
    own_ref,
    pair_ref,
    sk_ref,
    sv_ref,
    nk_ref,
    nv_ref,
    own_out_ref,
    pair_out_ref,
):
    me = lax.axis_index("seq")
    parity = lax.rem(me, 2)
    mine = lax.broadcasted_iota(jnp.int32, len_ref.shape, 1) == lax.div(me, 2)
    length = jnp.sum(
        jnp.where(mine, len_ref[...].astype(jnp.float32), 0.0), axis=1, keepdims=True
    )
    live_left = length.astype(jnp.int32) - parity * sv_ref.shape[0]

    def scores_of(head):
        rows = slice(head * GROUPS, (head + 1) * GROUPS)
        cols = slice(head * HD, (head + 1) * HD)
        q = jnp.concatenate(
            [ref[0, rows, :].astype(jnp.float32) for ref in (own_ref, pair_ref)], axis=0
        )
        scores = lane_dot(q.astype(jnp.bfloat16), sk_ref[:, cols])
        position = lax.broadcasted_iota(jnp.int32, scores.shape, 1)
        scores = jnp.where(position < live_left, scores, NEG_BIG)
        n_top = jnp.sum(q * nk_ref[:, cols].astype(jnp.float32), axis=-1, keepdims=True)
        hidden = (lax.broadcasted_iota(jnp.int32, n_top.shape, 0) >= GROUPS) & (parity == 1)
        return scores, jnp.where(hidden, NEG_BIG, n_top)

    ready = [scores_of(head) for head in range(AHEAD)]
    for head in range(KVH):
        cols = slice(head * HD, (head + 1) * HD)
        scores, n_top = ready.pop(0)
        if head + AHEAD < KVH:
            ready.append(scores_of(head + AHEAD))
        top = jnp.maximum(jnp.max(scores, axis=-1, keepdims=True), n_top)
        base = jnp.maximum(top, NEG_SAFE)
        weights = jnp.exp2((scores - base) * EXP2_SCALE)
        n_scale = jnp.exp2((n_top - base) * EXP2_SCALE)
        total = jnp.sum(weights, axis=-1, keepdims=True) + n_scale
        out = jnp.dot(
            weights.astype(jnp.bfloat16), sv_ref[:, cols], preferred_element_type=jnp.float32
        )
        out = out + n_scale * nv_ref[:, cols].astype(jnp.float32)
        for i, target in enumerate((own_out_ref, pair_out_ref)):
            mine = slice(i * GROUPS, (i + 1) * GROUPS)
            target[head, 0:GROUPS] = jnp.broadcast_to(top[mine], (GROUPS, LANES))
            target[head, GROUPS : 2 * GROUPS] = jnp.broadcast_to(total[mine], (GROUPS, LANES))
            target[head, 2 * GROUPS :] = out[mine]


def order_kernel(_, *refs):
    half = len(refs) // 2
    for source, target in zip(refs[:half], refs[half:]):
        for head in range(KVH):
            target[head] = source[:, head * HD : (head + 1) * HD]


def split_stats(stats, axis):
    high = stats.astype(jnp.bfloat16).astype(jnp.float32)
    rest = stats - high
    middle = rest.astype(jnp.bfloat16).astype(jnp.float32)
    low = rest - middle
    packed = high + pltpu.roll(middle, 2 * KVH, axis) + pltpu.roll(low, 4 * KVH, axis)
    return packed.astype(jnp.bfloat16)


def join_stats(packed, axis):
    packed = packed.astype(jnp.float32)
    shifted = lambda by: pltpu.roll(packed, LANES - by * KVH, axis)
    live = lax.broadcasted_iota(jnp.int32, packed.shape, axis) < KVH
    top = jnp.where(live, packed + shifted(2) + shifted(4), 0.0)
    total = jnp.where(live, shifted(1) + shifted(3) + shifted(5), 0.0)
    return top, total


def head_queries(ref, slots, head):
    q = ref[slots, head * GROUPS : (head + 1) * GROUPS, :].astype(jnp.float32)
    return q.reshape(SLOTS * GROUPS, HD).astype(jnp.bfloat16)


def score_kernel(token_ref, dk_ref, score_ref, peak_ref):
    rows_here = SLOTS * GROUPS
    lane_ids = lax.broadcasted_iota(jnp.int32, (rows_here, LANES), 1)
    for head in range(KVH):
        scores = lane_dot(head_queries(token_ref, pl.ds(0, SLOTS), head), dk_ref[head])
        score_ref[head] = scores
        peaks = jnp.full((rows_here, LANES), NEG_BIG, jnp.float32)
        for b in range(scores.shape[1] // BLOCK):
            block = scores[:, b * BLOCK : (b + 1) * BLOCK]
            peaks = jnp.where(lane_ids == b, jnp.max(block, axis=-1, keepdims=True), peaks)
        peak_ref[head] = peaks


def attend_kernel(flag_rows, scored, pieces, *refs):
    near_ref, other_ref, *refs = refs
    if scored:
        score_ref, peak_ref, *refs = refs
    dk_ref, dv_ref, far_dk_ref, far_dv_ref, own_ref, theirs_ref, *refs = refs
    out_refs, (bias_ref,) = refs[:pieces], refs[pieces:]
    span = far_dk_ref.shape[0]
    blocks_here = span // BLOCK
    rows_here = SLOTS * GROUPS
    me = lax.axis_index("seq")
    flag_row = lax.div(me * blocks_here, LANES)
    row_ids = lax.broadcasted_iota(jnp.int32, (1, flag_rows, LANES), 1)
    lane_ids = lax.broadcasted_iota(jnp.int32, (rows_here, LANES), 1)

    def tall(x):
        wide = jnp.broadcast_to(x[:, None, :], (SLOTS, GROUPS, LANES))
        return wide.reshape(rows_here, LANES)

    def do_chunk(chunk, local, put):
        slots = pl.ds(chunk * SLOTS, SLOTS)
        flags = near_ref[slots, HEADS:, :].astype(jnp.float32)
        flags = flags + other_ref[slots].astype(jnp.float32)
        flags = jnp.sum(jnp.where(row_ids == flag_row, flags, 0.0), axis=1)
        marks = []
        for i, device in enumerate((me, me ^ 1)):
            lane = lax.rem(device * blocks_here, LANES)
            bias = jnp.where(pltpu.roll(flags, lax.rem(LANES - lane, LANES), 1) > 0.5, 0.0, NEG_BIG)
            marks.append(bias)
            for b in range(blocks_here):
                wide = jnp.broadcast_to(bias[:, b : b + 1], (SLOTS, LANES))
                at = i * span + b * BLOCK
                bias_ref[:, at : at + BLOCK] = tall(wide)
        mark = tall(marks[0])

        def blocks_of(scores):
            return [scores[:, b * LANES : (b + 1) * LANES] for b in range(span // LANES)]

        def scores_of(head):
            q = head_queries(near_ref, slots, head)
            cols = slice(head * HD, (head + 1) * HD)
            far = lane_dot(q, far_dk_ref[:, cols]) + bias_ref[:, span:]
            if scored:
                return blocks_of(far)
            return blocks_of(far), blocks_of(lane_dot(q, dk_ref[head]) + bias_ref[:, :span])

        def softmax_of(head, scores):
            if scored:
                far = scores
                near = blocks_of(score_ref[head] + bias_ref[:, :span])
                peaks = functools.reduce(jnp.maximum, far, peak_ref[head] + mark)
            else:
                far, near = scores
                peaks = functools.reduce(jnp.maximum, far + near)
            top = jnp.broadcast_to(jnp.max(peaks, axis=-1, keepdims=True), (rows_here, LANES))
            base = jnp.maximum(top, NEG_SAFE)
            weights = [
                [jnp.exp2((block - base) * EXP2_SCALE) for block in blocks]
                for blocks in (near, far)
            ]
            total = functools.reduce(jnp.add, weights[0] + weights[1])
            total = jnp.broadcast_to(
                jnp.sum(total, axis=-1, keepdims=True), (rows_here, LANES)
            )
            near, far = [
                jnp.concatenate([w.astype(jnp.bfloat16) for w in ws], axis=1) for ws in weights
            ]
            return top, total, near, far

        stats = jnp.zeros((rows_here, LANES), jnp.float32)
        ready = [scores_of(head) for head in range(DOC_AHEAD)]
        for head in range(KVH):
            scores = ready.pop(0)
            if head + DOC_AHEAD < KVH:
                ready.append(scores_of(head + DOC_AHEAD))
            top, total, near, far = softmax_of(head, scores)
            out = jnp.dot(near, dv_ref[head], preferred_element_type=jnp.float32)
            out = out + jnp.dot(far, far_dv_ref[head], preferred_element_type=jnp.float32)
            if local:
                terms = [(top[:GROUPS], total[:GROUPS], out[:GROUPS])]
                for ref in (own_ref, theirs_ref):
                    terms.append(
                        tuple(ref[head, i * GROUPS : (i + 1) * GROUPS] for i in range(3))
                    )
                new_top = functools.reduce(jnp.maximum, [t for t, _, _ in terms])
                base = jnp.maximum(new_top, NEG_SAFE)
                scales = [jnp.exp2((t - base) * EXP2_SCALE) for t, _, _ in terms]
                new_total = sum(s * l for s, (_, l, _) in zip(scales, terms))
                new_out = sum(s * o for s, (_, _, o) in zip(scales, terms))
                top = jnp.concatenate([new_top, top[GROUPS:]], axis=0)
                total = jnp.concatenate([new_total, total[GROUPS:]], axis=0)
                out = jnp.concatenate([new_out, out[GROUPS:]], axis=0)
            units = (out / jnp.maximum(total, 1.0)).astype(jnp.bfloat16)
            stats = jnp.where(lane_ids == head, top * EXP2_SCALE, stats)
            stats = jnp.where(lane_ids == KVH + head, total, stats)
            put(head * GROUPS, units.reshape(SLOTS, GROUPS, HD))
        put(HEADS, split_stats(stats, 1).reshape(SLOTS, GROUPS, LANES))

    size = out_refs[0].shape[0]
    if size < SLOTS:

        def put(row, value):
            for i, ref in enumerate(out_refs):
                ref[:, row : row + GROUPS, :] = value[i * size : (i + 1) * size]

        do_chunk(0, True, put)
        return
    steps = size // SLOTS
    for i, ref in enumerate(out_refs):

        def put_at(step):
            def put(row, value):
                ref[pl.ds(step * SLOTS, SLOTS), row : row + GROUPS, :] = value

            return put

        if i == 0:
            do_chunk(0, True, put_at(0))
        lax.fori_loop(
            1 if i == 0 else 0,
            steps,
            lambda step, _: do_chunk(i * steps + step, False, put_at(step)),
            None,
        )


def mix_weights(refs):
    rows = slice(HEADS, HEADS + GROUPS)
    stats = [join_stats(ref[:, rows, :], 2) for ref in refs]
    top = functools.reduce(jnp.maximum, [t for t, _ in stats])
    weights = [jnp.exp2(t - top) * total for t, total in stats]
    total = functools.reduce(jnp.add, weights)
    scale = 1.0 / jnp.maximum(total, 1.0)
    return top, total, [w * scale for w in weights[1:]]


def mixed_units(head, refs, weights):
    rows = slice(head * GROUPS, (head + 1) * GROUPS)
    first, *others = [ref[:, rows, :].astype(jnp.float32) for ref in refs]
    steps = [(u - first) * w[:, :, head : head + 1] for u, w in zip(others, weights)]
    return functools.reduce(jnp.add, steps, first)


def merge_kernel(count, *refs):
    sources, targets = refs[:count], refs[count:]
    top, total, weights = mix_weights(sources)
    size = targets[0].shape[0]
    for head in range(KVH):
        rows = slice(head * GROUPS, (head + 1) * GROUPS)
        units = mixed_units(head, sources, weights).astype(jnp.bfloat16)
        for i, target in enumerate(targets):
            target[:, rows, :] = units[i * size : (i + 1) * size]
    packed = split_stats(top + pltpu.roll(total, KVH, 2), 2)
    for i, target in enumerate(targets):
        target[:, HEADS : HEADS + GROUPS, :] = packed[i * size : (i + 1) * size]


def finish_kernel(count, *refs):
    sources, out_ref = refs[:count], refs[count]
    _, _, weights = mix_weights(sources)
    for head in range(KVH):
        units = mixed_units(head, sources, weights)[0]
        for g in range(GROUPS):
            h = head * GROUPS + g
            out_ref[:, h * HD : (h + 1) * HD] = units[g : g + 1, :].astype(jnp.bfloat16)


def whole(space=VMEM):
    return pl.BlockSpec(memory_space=space)


def near_core(x):
    return pltpu.with_memory_space_constraint(x, VMEM)


def on_core(kernel, out_shape, operands, cost=None, **kwargs):
    return pl.pallas_call(
        kernel,
        out_shape=out_shape,
        in_specs=kwargs.pop("in_specs", [whole()] * len(operands)),
        out_specs=jax.tree.map(lambda _: whole(), out_shape),
        compiler_params=pltpu.CompilerParams(vmem_limit_bytes=16 << 20),
        cost_estimate=cost,
        **kwargs,
    )(*operands)


def in_hbm(x):
    return pltpu.with_memory_space_constraint(x, pltpu.HBM)


def swap(x, bits):
    devices = lax.axis_size("seq")
    return lax.ppermute(x, "seq", [(i, i ^ bits) for i in range(devices)])


def stages_of(devices):
    far_bits = []
    while 2 ** (len(far_bits) + 3) < devices:
        far_bits.insert(0, (2 ** (len(far_bits) + 3) | 1,))
    return far_bits + [(3, 5, 7)[: devices // 2 - 1]]


def per_device(
    queries,
    new_keys,
    new_values,
    doc_keys,
    doc_values,
    suffix_keys,
    suffix_values,
    keep_lists,
    suffix_lengths,
):
    devices = lax.axis_size("seq")
    blocks = devices * doc_keys.shape[0] // BLOCK
    flag_rows = 8 * pl.cdiv(blocks, 8 * LANES)
    stages = stages_of(devices)
    packed = on_core(
        pack_kernel,
        VMEM((HEADS + flag_rows, HD), jnp.bfloat16),
        (in_hbm(keep_lists), in_hbm(queries)),
        cost=pl.CostEstimate(flops=10**10, bytes_accessed=10**5, transcendentals=0),
    )
    near = packed[None]
    own = near
    heads_of = lambda x: VMEM((KVH, x.shape[0], HD), x.dtype)
    size = 2 * suffix_keys.size
    pair = swap(own, 1)
    far_dv = swap(doc_values, 1)
    far_dk = swap(doc_keys, 1)

    def ordered(after, caches):
        return on_core(
            order_kernel,
            [heads_of(cache) for cache in caches],
            (after, *caches),
            cost=pl.CostEstimate(flops=0, bytes_accessed=4 * size, transcendentals=0),
        )

    dk, dv = ordered(own, (doc_keys, doc_values))
    partial = VMEM((KVH, 3 * GROUPS, LANES), jnp.float32)
    local, pair_local = on_core(
        suffix_kernel,
        [partial, partial],
        (
            near_core(suffix_lengths[None]),
            own,
            near_core(pair),
            suffix_keys,
            suffix_values,
            new_keys,
            new_values,
        ),
        cost=pl.CostEstimate(flops=10**9, bytes_accessed=3 * size, transcendentals=10**6),
    )
    (far_dv,) = ordered(local, (near_core(far_dv),))
    for step, stage in enumerate(stages):
        arrived = []
        for bits in stage:
            arrived.append(swap(near, bits))
        near = jnp.concatenate([near] + arrived, axis=0)
    other = swap(near[:, HEADS:, :], 1)
    near = near_core(near)
    theirs = swap(pair_local, 1)
    tokens = lambda count: VMEM((count, HEADS + GROUPS, HD), jnp.bfloat16)
    cost = pl.CostEstimate(flops=10**9, bytes_accessed=2 * size, transcendentals=10**6)
    span = doc_keys.shape[0]
    rows = devices // 2 * GROUPS
    scored = devices // 2 == SLOTS
    scores = ()
    if scored:
        scores = on_core(
            score_kernel,
            (
                VMEM((KVH, rows, span), jnp.float32),
                VMEM((KVH, rows, LANES), jnp.float32),
            ),
            (near, dk),
            cost=cost,
        )
    pieces = len(stages[-1]) + 1
    parts = on_core(
        functools.partial(attend_kernel, flag_rows, scored, pieces),
        [tokens(devices // 2 // pieces)] * pieces,
        (
            near,
            near_core(other),
            *scores,
            dk,
            dv,
            near_core(far_dk),
            far_dv,
            local,
            near_core(theirs),
        ),
        scratch_shapes=[VMEM((SLOTS * GROUPS, 2 * span), jnp.float32)],
        cost=cost,
    )
    step = len(stages) - 1
    while stages:
        stage = stages.pop()
        sources = [parts[0]]
        for bits, part in zip(stage, parts[1:]):
            sources.append(near_core(swap(part, bits)))
        step -= 1
        if stages:
            pieces = len(stages[-1]) + 1
            parts = on_core(
                functools.partial(merge_kernel, len(sources)),
                [tokens(sources[0].shape[0] // pieces)] * pieces,
                sources,
            )
    return on_core(
        functools.partial(finish_kernel, len(sources)),
        jax.ShapeDtypeStruct((1, HEADS * HD), jnp.bfloat16),
        sources,
    )


def solution(mesh):
    split = P(("parts", "seq"), None)
    return jax.shard_map(
        per_device,
        mesh=mesh,
        in_specs=(split,) * 8 + (P("parts"),),
        out_specs=split,
        check_vma=False,
    )
```
